32 devices in a mesh: img: 16 (over z, y, core), seq: 2 (over x).
Axes of the slice: x: 2, y: 2, z: 4, core: 2. Of those that a mesh axis runs over, the one named last changes fastest.
Arguments:
- patches: bfloat16 [96, 2, 160, 768], P('img', 'seq'), may hold values from -6 to 6
- grid_shape: int32 [96, 2], P('img'), may hold values from 8 to 24, as said below
- split_rows: int32 [96], P('img'), may hold values from 1 to 11, as said below
- owner_shard: int32 [96], P('img'), may hold values from 0 to 1
- drop_masks: int32 [96, 2], P('img'), may hold values 0 or 1
- ln1_gain: float32 [768], replicated, may hold values from 0.25 to 1.75
- ln1_bias: float32 [768], replicated, may hold values from -3 to 3
- qkv_weight: bfloat16 [768, 2304], replicated, may hold values from -0.21875 to 0.21875
- qv_bias: float32 [1536], replicated, may hold values from -3 to 3
- proj_weight: bfloat16 [768, 768], replicated, may hold values from -0.875 to 0.875
- proj_bias: float32 [768], replicated, may hold values from -3 to 3
- ln2_gain: float32 [768], replicated, may hold values from 0.25 to 1.75
- ln2_bias: float32 [768], replicated, may hold values from -3 to 3
- fc1_weight: bfloat16 [768, 3072], replicated, may hold values from -0.21875 to 0.21875
- fc1_bias: float32 [3072], replicated, may hold values from -3 to 3
- fc2_weight: bfloat16 [3072, 768], replicated, may hold values from -0.21875 to 0.21875
- fc2_bias: float32 [768], replicated, may hold values from -3 to 3
- cotangent: bfloat16 [96, 2, 160, 768], P('img', 'seq'), may hold values from -6 to 6
Outputs:
- layer_out: bfloat16 [96, 2, 160, 768], P('img', 'seq')
- patches_grad: float32 [96, 2, 160, 768], P('img', 'seq')
- ln1_gain_grad: float32 [768], P(('img', 'seq'))
- ln1_bias_grad: float32 [768], P(('img', 'seq'))
- qkv_weight_grad: float32 [768, 2304], P(('img', 'seq'))
- qv_bias_grad: float32 [1536], P(('img', 'seq'))
- proj_weight_grad: float32 [768, 768], P(('img', 'seq'))
- proj_bias_grad: float32 [768], P(('img', 'seq'))
- ln2_gain_grad: float32 [768], P(('img', 'seq'))
- ln2_bias_grad: float32 [768], P(('img', 'seq'))
- fc1_weight_grad: float32 [768, 3072], P(('img', 'seq'))
- fc1_bias_grad: float32 [3072], P(('img', 'seq'))
- fc2_weight_grad: float32 [3072, 768], P(('img', 'seq'))
- fc2_bias_grad: float32 [768], P(('img', 'seq'))
The draws below stay inside these ranges and needn't reach their ends.
Inputs may be any that keep to these rules, and one draw needn't show every extreme that they name: `grid_shape`: column 0 is the height, from 8 to 20; column 1 is the width, min(24, 280 // height), so an image has at most 280 patches. `split_rows`: both parts of every image hold at least one and at most 158 patches.
All inputs are finite; a program needn't handle non-finite values. No bound on the sum of `drop_masks` on one device may be relied on, other than what follows from the above.
Results may differ from the reference program's by a relative error of at most 0.014.
Values may be sent and summed in bfloat16 or wider, within the bound.
A program may use at most 192 MiB of HBM per device.

```python
import jax
import jax.numpy as jnp
from jax import lax

D = 768
HEADS = 12
HEAD_DIM = 64
FF = 3072
HALF = 158
SLOT = 160
H_LO = 8
H_HI = 20
W_HI = 24
AREA = 280
IMG_DEV = 6
IMAGES = 96
N_SEQ = 2


def grid_parts(key):
    height = jax.random.randint(jax.random.fold_in(key, 101), (IMAGES,), H_LO, H_HI + 1)
    across = jnp.minimum(W_HI, AREA // height)
    area_cells = height * across
    lowest = (area_cells - HALF + across - 1) // across
    highest = HALF // across
    jitter = jax.random.randint(jax.random.fold_in(key, 202), (IMAGES,), -1, 2)
    split_at = jnp.clip(height // 2 + jitter, lowest, highest)
    return (height, across, split_at)


def draw_grid_shape(key, part):
    height, across, split_at = grid_parts(key)
    return jnp.stack([height, across], axis=1).astype(jnp.int32)


def draw_split_rows(key, part):
    height, across, split_at = grid_parts(key)
    return split_at.astype(jnp.int32)


def touch_ends(values, rng, low, top_value):
    dims = values.shape
    spot = [jax.random.randint(jax.random.fold_in(rng, axis), (), 0, dims[axis]) for axis in range(len(dims))]
    values = values.at[tuple(spot)].set(low)
    longest = dims.index(max(dims))
    spot[longest] = (spot[longest] + 1) % dims[longest]
    return values.at[tuple(spot)].set(top_value)


def shard_levels(own_key, extent, cuts, least, high):
    factor_of, own = 1.0, jax.random.fold_in(own_key, 6)
    for dim, shards_of in cuts:
        steps = jnp.exp(jax.random.uniform(jax.random.fold_in(own, dim), (shards_of,), jnp.float32, least / len(cuts), high / len(cuts)))
        factor_of = factor_of * jnp.repeat(steps, extent[dim] // shards_of).reshape([-1 if axis == dim else 1 for axis in range(len(extent))])
    return factor_of


def bell_draw(rng, dims, deviation, reach, cuts=(), kind=jnp.bfloat16):
    drawn = deviation * jax.random.normal(rng, dims, jnp.float32)
    if cuts:
        drawn = drawn * shard_levels(rng, dims, cuts, -0.22, 0.18)
    return jnp.clip(drawn, -reach, reach).astype(kind)


def setup_inputs(seed: int = 0) -> dict:
    arg_keys = jax.random.split(jax.random.key(seed), 19)
    patches = bell_draw(arg_keys[0], (IMAGES, N_SEQ, SLOT, D), 1.0, 6.0, ((0, 16), (1, 2)))
    grid_shape = draw_grid_shape(jax.random.fold_in(arg_keys[18], 71), 0)
    split_rows = draw_split_rows(jax.random.fold_in(arg_keys[18], 71), 0)
    owner_shard = touch_ends(jax.random.randint(arg_keys[3], (IMAGES,), 0, N_SEQ), jax.random.fold_in(arg_keys[3], 1), 0, N_SEQ - 1).astype(jnp.int32)
    drop_masks = touch_ends((jax.random.randint(arg_keys[4], (IMAGES, 2), 0, 10) < 9).astype(jnp.int32), jax.random.fold_in(arg_keys[4], 1), 0, 1)
    ln1_gain = jnp.clip(1.0 + 0.15 * jax.random.normal(arg_keys[5], (D,), jnp.float32), 0.25, 1.75)
    ln1_bias = bell_draw(arg_keys[6], (D,), 0.3, 3.0, (), jnp.float32)
    qkv_weight = bell_draw(arg_keys[7], (D, 3 * D), D ** -0.5, 0.21875)
    qv_bias = bell_draw(arg_keys[8], (2 * D,), 0.3, 3.0, (), jnp.float32)
    proj_weight = bell_draw(arg_keys[9], (D, D), (D // 16) ** -0.5, 0.875)
    proj_bias = bell_draw(arg_keys[10], (D,), 0.3, 3.0, (), jnp.float32)
    ln2_gain = jnp.clip(1.0 + 0.15 * jax.random.normal(arg_keys[11], (D,), jnp.float32), 0.25, 1.75)
    ln2_bias = bell_draw(arg_keys[12], (D,), 0.3, 3.0, (), jnp.float32)
    fc1_weight = bell_draw(arg_keys[13], (D, FF), D ** -0.5, 0.21875)
    fc1_bias = bell_draw(arg_keys[14], (FF,), 0.3, 3.0, (), jnp.float32)
    fc2_weight = bell_draw(arg_keys[15], (FF, D), (FF // 4) ** -0.5, 0.21875)
    fc2_bias = bell_draw(arg_keys[16], (D,), 0.3, 3.0, (), jnp.float32)
    cotangent = bell_draw(arg_keys[17], (IMAGES, N_SEQ, SLOT, D), 1.0, 6.0, ((0, 16), (1, 2)))
    return {"patches": patches, "grid_shape": grid_shape, "split_rows": split_rows, "owner_shard": owner_shard, "drop_masks": drop_masks, "ln1_gain": ln1_gain, "ln1_bias": ln1_bias, "qkv_weight": qkv_weight, "qv_bias": qv_bias, "proj_weight": proj_weight, "proj_bias": proj_bias, "ln2_gain": ln2_gain, "ln2_bias": ln2_bias, "fc1_weight": fc1_weight, "fc1_bias": fc1_bias, "fc2_weight": fc2_weight, "fc2_bias": fc2_bias, "cotangent": cotangent}


LN_EPS = 1e-06
KEEP_SCALE = 1.0 / 0.9
MASK_FILL = -1e+30
HIGH_PREC = lax.Precision.HIGHEST

@jax.custom_vjp
def low(v):
    return lax.optimization_barrier(v.astype(jnp.bfloat16)).astype(jnp.float32)

@jax.custom_vjp
def low_back(v):
    return v

def low_keep(v):
    return (low(v), None)

def low_pass(kept, grad):
    return (grad,)

def back_keep(v):
    return (v, None)

def back_low(kept, grad):
    return (low(grad),)
low.defvjp(low_keep, low_pass)
low_back.defvjp(back_keep, back_low)

def both_round(values):
    return low(low_back(values))

def layer_norm(values, gain_vec, bias_vec):
    row_mean = lax.optimization_barrier(jnp.mean(values, axis=-1, keepdims=True))
    centred = values - row_mean
    variance = lax.optimization_barrier(jnp.mean(centred * centred, axis=-1, keepdims=True))
    return centred * lax.rsqrt(variance + LN_EPS) * gain_vec + bias_vec

def exact_gelu(values):
    return jax.nn.gelu(values, approximate=False)

def token_valid(grid_shape, split_rows, owner_shard, slot_len):
    height = grid_shape[:, 0]
    across = grid_shape[:, 1]
    counts = jnp.stack([split_rows * across, (height - split_rows) * across], axis=1)
    row_ids = jnp.arange(slot_len, dtype=jnp.int32)[None, None, :]
    seq_ids = jnp.arange(counts.shape[1], dtype=jnp.int32)[None, :, None]
    special = row_ids < 2
    owned_slot = owner_shard[:, None, None] == seq_ids
    filled = row_ids - 2 < counts[:, :, None]
    return jnp.where(special, owned_slot, filled).astype(jnp.float32)

def group_layer(params, block, valid, keeps):
    ln1_gain, ln1_bias, qkv_weight, qv_bias, proj_weight, proj_bias, ln2_gain, ln2_bias, fc1_weight, fc1_bias, fc2_weight, fc2_bias = params
    group_size = block.shape[0]
    key_count = block.shape[1] * block.shape[2]
    tokens = block.reshape(group_size, key_count, D)
    head_shape = (group_size, key_count, HEADS, HEAD_DIM)
    normed_one = low(layer_norm(tokens, ln1_gain, ln1_bias))
    joined = jnp.einsum('gkd,de->gke', normed_one, qkv_weight, precision=HIGH_PREC)
    queries = both_round(joined[..., :D] + qv_bias[:D]).reshape(head_shape)
    keyed = both_round(joined[..., D:2 * D]).reshape(head_shape)
    valued = both_round(joined[..., 2 * D:] + qv_bias[D:]).reshape(head_shape)
    raw_scores = low_back(jnp.einsum('gqhd,gkhd->ghqk', queries, keyed, precision=HIGH_PREC) * HEAD_DIM ** (-0.5))
    flat_valid = valid.reshape(group_size, key_count)
    scores = jnp.where(flat_valid[:, None, None, :] > 0.5, raw_scores, MASK_FILL)
    top_score = lax.optimization_barrier(jnp.max(scores, axis=-1, keepdims=True))
    log_total = top_score + jnp.log(lax.optimization_barrier(jnp.sum(jnp.exp(scores - top_score), axis=-1, keepdims=True)))
    probs = low(jnp.exp(scores - log_total))
    attended = both_round(jnp.einsum('ghqk,gkhd->gqhd', probs, valued, precision=HIGH_PREC).reshape(group_size, key_count, D))
    branch = low_back(jnp.einsum('gkd,de->gke', attended, proj_weight, precision=HIGH_PREC) + proj_bias)
    middle = tokens + keeps[:, 0, None, None] * branch
    normed_two = low(layer_norm(middle, ln2_gain, ln2_bias))
    hidden_pre = low_back(jnp.einsum('gkd,de->gke', normed_two, fc1_weight, precision=HIGH_PREC) + fc1_bias)
    hidden = low(exact_gelu(hidden_pre))
    mlp_out = low_back(jnp.einsum('gke,ed->gkd', hidden, fc2_weight, precision=HIGH_PREC) + fc2_bias)
    final = middle + keeps[:, 1, None, None] * mlp_out
    return (final * flat_valid[:, :, None]).reshape(block.shape)

def reference(patches, grid_shape, split_rows, owner_shard, drop_masks, ln1_gain, ln1_bias, qkv_weight, qv_bias, proj_weight, proj_bias, ln2_gain, ln2_bias, fc1_weight, fc1_bias, fc2_weight, fc2_bias, cotangent):
    valid = token_valid(grid_shape, split_rows, owner_shard, SLOT)
    keeps = drop_masks.astype(jnp.float32) * KEEP_SCALE
    params = (ln1_gain, ln1_bias, qkv_weight.astype(jnp.float32), qv_bias, proj_weight.astype(jnp.float32), proj_bias, ln2_gain, ln2_bias, fc1_weight.astype(jnp.float32), fc1_bias, fc2_weight.astype(jnp.float32), fc2_bias)
    group_count = IMAGES // IMG_DEV
    valid_groups = valid.reshape((group_count, IMG_DEV) + valid.shape[1:])
    keep_groups = keeps.reshape(group_count, IMG_DEV, 2)

    def whole(inputs, weights):

        def one_group(pieces):
            return group_layer(weights, pieces[0], pieces[1], pieces[2])
        stepper = jax.checkpoint(one_group)
        blocks = inputs.reshape((group_count, IMG_DEV) + inputs.shape[1:])
        outputs = lax.map(stepper, (blocks, valid_groups, keep_groups))
        return outputs.reshape(inputs.shape)
    result, pullback = jax.vjp(whole, patches.astype(jnp.float32), params)
    input_grad, weight_grads = pullback(cotangent.astype(jnp.float32))
    return (result.astype(jnp.bfloat16), input_grad, weight_grads[0], weight_grads[1], weight_grads[2], weight_grads[3], weight_grads[4], weight_grads[5], weight_grads[6], weight_grads[7], weight_grads[8], weight_grads[9], weight_grads[10], weight_grads[11])
```

```python
import functools

import jax
import jax.numpy as jnp
from jax import lax
from jax.experimental import pallas as pl
from jax.experimental.pallas import tpu as pltpu
from jax.sharding import PartitionSpec as P

HEAD_DIM = 64
LN_EPS = 1e-06
KEEP_SCALE = 1.0 / 0.9
MASK_FILL = -1e30
BF16 = jnp.bfloat16
F32 = jnp.float32
MIB = 1024 * 1024


def dot_nn(a, b):
    return lax.dot_general(a, b, (((1,), (0,)), ((), ())), preferred_element_type=F32)


def dot_nt(a, b):
    return lax.dot_general(a, b, (((1,), (1,)), ((), ())), preferred_element_type=F32)


def dot_tn(a, b):
    return lax.dot_general(a, b, (((0,), (0,)), ((), ())), preferred_element_type=F32)


def norm_parts(values):
    row_mean = jnp.mean(values, axis=-1, keepdims=True)
    centred = values - row_mean
    variance = jnp.mean(centred * centred, axis=-1, keepdims=True)
    rstd = lax.rsqrt(variance + LN_EPS)
    return centred * rstd, rstd


def norm_back(d_normed, gain, unit, rstd):
    d_unit = d_normed * gain
    mean_one = jnp.mean(d_unit, axis=-1, keepdims=True)
    mean_two = jnp.mean(d_unit * unit, axis=-1, keepdims=True)
    return rstd * (d_unit - mean_one - unit * mean_two)


def gelu_both(values):
    size = jnp.abs(values)
    t = 1.0 / (1.0 + 0.23164189 * size)
    bell = jnp.exp(-0.5 * values * values)
    poly = t * (
        0.127414796
        + t * (-0.142248368 + t * (0.7107068705 + t * (-0.7265760135 + t * 0.5307027145)))
    )
    tail = poly * bell
    cdf = jnp.where(values >= 0.0, 1.0 - tail, tail)
    return values * cdf, cdf + values * (0.3989422804014327 * bell)


def row_valid(scal_ref, image, rows, half, axis):
    shape = (rows, 1) if axis == 0 else (1, rows)
    slot = lax.broadcasted_iota(jnp.int32, shape, axis)
    other = slot >= half
    place = jnp.where(other, slot - half, slot)
    count = jnp.where(other, scal_ref[image, 2], scal_ref[image, 0])
    special = jnp.where(other, scal_ref[image, 3], scal_ref[image, 1])
    return jnp.where(place < 2, special, (place - 2 < count).astype(jnp.int32)) > 0


def front_kernel(
    scal_ref, own_ref, oth_ref, g1_ref, b1_ref, wqkv_ref, qb_ref, vb_ref, wp_ref, pb_ref, g2_ref, b2_ref,
    n1_ref, qkv_ref, probs_ref, att_ref, mid_ref, n2_ref,
):
    image = pl.program_id(0)
    half, width = own_ref.shape[1], own_ref.shape[2]
    rows = 2 * half
    x = jnp.concatenate([own_ref[0].astype(F32), oth_ref[0].astype(F32)], axis=0)
    unit, _ = norm_parts(x)
    n1 = (unit * g1_ref[...] + b1_ref[...]).astype(BF16)
    n1_ref[0] = n1
    qkv_ref[0, :, :width] = ((dot_nn(n1, wqkv_ref[:, :width]) + qb_ref[...]).astype(BF16) * BF16(HEAD_DIM**-0.5))
    qkv_ref[0, :, width : 2 * width] = dot_nn(n1, wqkv_ref[:, width : 2 * width]).astype(BF16)
    qkv_ref[0, :, 2 * width :] = (dot_nn(n1, wqkv_ref[:, 2 * width :]) + vb_ref[...]).astype(BF16)
    fill = jnp.where(row_valid(scal_ref, image, rows, half, 1), 0.0, MASK_FILL)
    low_lane = lax.broadcasted_iota(jnp.int32, (rows, 128), 1) < HEAD_DIM
    for pair in range(width // 128):
        cut = slice(128 * pair, 128 * pair + 128)
        q2 = qkv_ref[0, :, cut]
        k2 = qkv_ref[0, :, width + 128 * pair : width + 128 * pair + 128]
        v2 = qkv_ref[0, :, 2 * width + 128 * pair : 2 * width + 128 * pair + 128]
        total = None
        for side in range(2):
            mine = low_lane if side == 0 else jnp.logical_not(low_lane)
            scores = dot_nt(jnp.where(mine, q2, 0), k2) + fill
            top = jnp.max(scores, axis=-1, keepdims=True)
            weight = jnp.exp(scores - top)
            probs = (weight * (1.0 / jnp.sum(weight, axis=-1, keepdims=True))).astype(BF16)
            probs_ref[0, 2 * pair + side] = probs
            part = dot_nn(probs, jnp.where(mine, v2, 0))
            total = part if total is None else total + part
        att_ref[0, :, cut] = total.astype(BF16)
    keep = scal_ref[image, 4].astype(F32) * KEEP_SCALE
    branch = dot_nn(att_ref[0], wp_ref[...]) + pb_ref[...]
    middle = jnp.concatenate([own_ref[0].astype(F32), oth_ref[0].astype(F32)], axis=0) + keep * branch
    mid_ref[0] = middle
    unit, _ = norm_parts(middle)
    n2_ref[0] = (unit * g2_ref[...] + b2_ref[...]).astype(BF16)


def full(shape):
    zeros = (0,) * len(shape)
    return pl.BlockSpec(shape, lambda *_: zeros, pipeline_mode=pl.Buffered(1))


def front(scal, own, oth, w):
    images, half, width = own.shape
    rows = 2 * half
    heads = width // HEAD_DIM
    per = lambda *tail: pl.BlockSpec((1,) + tail, lambda i, s: (i,) + (0,) * len(tail))
    flops = 2 * images * rows * width * (4 * width + 4 * rows)
    return pl.pallas_call(
        front_kernel,
        grid_spec=pltpu.PrefetchScalarGridSpec(
            num_scalar_prefetch=1,
            grid=(images,),
            in_specs=[
                per(half, width), per(half, width), full((1, width)), full((1, width)),
                full((width, 3 * width)), full((1, width)), full((1, width)),
                full((width, width)), full((1, width)), full((1, width)), full((1, width)),
            ],
            out_specs=[
                per(rows, width), per(rows, 3 * width), per(heads, rows, rows),
                per(rows, width), per(rows, width), per(rows, width),
            ],
        ),
        out_shape=[
            jax.ShapeDtypeStruct((images, rows, width), BF16),
            jax.ShapeDtypeStruct((images, rows, 3 * width), BF16),
            jax.ShapeDtypeStruct((images, heads, rows, rows), BF16),
            jax.ShapeDtypeStruct((images, rows, width), BF16),
            jax.ShapeDtypeStruct((images, rows, width), F32),
            jax.ShapeDtypeStruct((images, rows, width), BF16),
        ],
        compiler_params=pltpu.CompilerParams(vmem_limit_bytes=56 * MIB),
        cost_estimate=pl.CostEstimate(flops=flops, transcendentals=images * heads * rows * rows, bytes_accessed=30_000_000),
        name="front",
    )(scal, own, oth, w["ln1_gain"], w["ln1_bias"], w["qkv_weight"], w["q_bias"], w["v_bias"],
      w["proj_weight"], w["proj_bias"], w["ln2_gain"], w["ln2_bias"])


def mlp_kernel(
    scal_ref, n2_ref, mid_ref, w1_ref, c1_ref, w2_ref, c2_ref,
    hid_ref, slope_ref, own_ref, oth_ref, acc_ref,
):
    step = pl.program_id(0)
    images, half, width = own_ref.shape
    rows = 2 * half
    hidden, slope = gelu_both(dot_nn(n2_ref[...], w1_ref[...]) + c1_ref[...])
    hidden = hidden.astype(BF16)
    hid_ref[...] = hidden
    slope_ref[...] = slope.astype(BF16)
    part = dot_nn(hidden, w2_ref[...])

    @pl.when(step == 0)
    def _():
        acc_ref[...] = part

    @pl.when(step > 0)
    def _():
        acc_ref[...] += part

    @pl.when(step == pl.num_programs(0) - 1)
    def _():
        for image in range(images):
            keep = scal_ref[image, 5].astype(F32) * KEEP_SCALE
            cut = slice(rows * image, rows * image + rows)
            final = mid_ref[cut, :] + keep * (acc_ref[cut, :] + c2_ref[...])
            out = jnp.where(row_valid(scal_ref, image, rows, half, 0), final, 0.0).astype(BF16)
            own_ref[image] = out[:half]
            oth_ref[image] = out[half:]


def mlp(scal, n2, middle, w, images, tile):
    tokens, width = n2.shape
    hidden_width = w["fc1_weight"].shape[1]
    half = tokens // images // 2
    return pl.pallas_call(
        mlp_kernel,
        grid_spec=pltpu.PrefetchScalarGridSpec(
            num_scalar_prefetch=1,
            grid=(hidden_width // tile,),
            in_specs=[
                full((tokens, width)), full((tokens, width)),
                pl.BlockSpec((width, tile), lambda j, s: (0, j)), pl.BlockSpec((1, tile), lambda j, s: (0, j)),
                pl.BlockSpec((tile, width), lambda j, s: (j, 0)), full((1, width)),
            ],
            out_specs=[
                pl.BlockSpec((tokens, tile), lambda j, s: (0, j)), pl.BlockSpec((tokens, tile), lambda j, s: (0, j)),
                full((images, half, width)), full((images, half, width)),
            ],
            scratch_shapes=[pltpu.VMEM((tokens, width), F32)],
        ),
        out_shape=[
            jax.ShapeDtypeStruct((tokens, hidden_width), BF16),
            jax.ShapeDtypeStruct((tokens, hidden_width), BF16),
            jax.ShapeDtypeStruct((images, half, width), BF16),
            jax.ShapeDtypeStruct((images, half, width), BF16),
        ],
        compiler_params=pltpu.CompilerParams(vmem_limit_bytes=56 * MIB),
        cost_estimate=pl.CostEstimate(flops=4 * tokens * width * hidden_width, transcendentals=2 * tokens * hidden_width, bytes_accessed=30_000_000),
        name="mlp",
    )(scal, n2, middle, w["fc1_weight"], w["fc1_bias"], w["fc2_weight"], w["fc2_bias"])


def put_halves(grad_ref, value, send_ref, keep_ref, mine, lead):
    grad_ref[...] = value.astype(BF16)
    run = send_ref.shape[-2]
    runs = grad_ref.shape[0] // (2 * run)
    for k in range(runs):
        away = pl.multiple_of((2 * k + 1 - mine) * run, 16)
        here = pl.multiple_of((2 * k + mine) * run, 16)
        send_ref[lead + (k,)] = grad_ref[pl.ds(away, run), :]
        keep_ref[lead + (k,)] = grad_ref[pl.ds(here, run), :]


def mlp_back_kernel(
    scal_ref, mine_ref, own_ref, oth_ref, n2_ref, hid_ref, slope_ref, w1_ref, w2_ref,
    dn2_ref, s2_ref, k2_ref, s1_ref, k1_ref, c2_ref, c1_ref, dmlp_ref, grad_ref, acc_ref,
):
    step = pl.program_id(0)
    images, half, width = own_ref.shape
    rows = 2 * half
    mine = mine_ref[0]

    @pl.when(step == 0)
    def _():
        total = jnp.zeros((1, width), F32)
        for image in range(images):
            keep = scal_ref[image, 5].astype(F32) * KEEP_SCALE
            cot = jnp.concatenate([own_ref[image].astype(F32), oth_ref[image].astype(F32)], axis=0)
            live = row_valid(scal_ref, image, rows, half, 0)
            d_mlp = (jnp.where(live, cot, 0.0) * keep).astype(BF16)
            dmlp_ref[rows * image : rows * image + rows, :] = d_mlp
            total += jnp.sum(d_mlp.astype(F32), axis=0, keepdims=True)
        c2_ref[...] = total

    d_pre = slope_ref[...].astype(F32) * dot_nt(dmlp_ref[...], w2_ref[...])
    d_pre = d_pre.astype(BF16)
    c1_ref[...] = jnp.sum(d_pre.astype(F32), axis=0, keepdims=True)
    part = dot_nt(d_pre, w1_ref[...])
    put_halves(grad_ref, dot_tn(n2_ref[...], d_pre), s1_ref, k1_ref, mine, ())
    put_halves(grad_ref, dot_tn(hid_ref[...], dmlp_ref[...]), s2_ref, k2_ref, mine, (0,))

    @pl.when(step == 0)
    def _():
        acc_ref[...] = part

    @pl.when(step > 0)
    def _():
        acc_ref[...] += part

    @pl.when(step == pl.num_programs(0) - 1)
    def _():
        dn2_ref[...] = acc_ref[...]


def mlp_back(scal, mine, own, oth, n2, hidden, slope, w, run1, run2):
    tokens, width = n2.shape
    images, half, _ = own.shape
    hidden_width = hidden.shape[1]
    tile = width
    steps = hidden_width // tile
    runs1, runs2 = width // (2 * run1), tile // (2 * run2)
    col = pl.BlockSpec((tokens, tile), lambda j, s, m: (0, j))
    half1 = pl.BlockSpec((runs1, run1, tile), lambda j, s, m: (0, 0, j))
    half2 = pl.BlockSpec((1, runs2, run2, width), lambda j, s, m: (j, 0, 0, 0))
    return pl.pallas_call(
        mlp_back_kernel,
        grid_spec=pltpu.PrefetchScalarGridSpec(
            num_scalar_prefetch=2,
            grid=(steps,),
            in_specs=[
                full((images, half, width)), full((images, half, width)), full((tokens, width)), col, col,
                pl.BlockSpec((width, tile), lambda j, s, m: (0, j)), pl.BlockSpec((tile, width), lambda j, s, m: (j, 0)),
            ],
            out_specs=[
                full((tokens, width)), half2, half2, half1, half1,
                full((1, width)), pl.BlockSpec((1, tile), lambda j, s, m: (0, j)),
            ],
            scratch_shapes=[
                pltpu.VMEM((tokens, width), BF16), pltpu.VMEM((width, width), BF16), pltpu.VMEM((tokens, width), F32),
            ],
        ),
        out_shape=[
            jax.ShapeDtypeStruct((tokens, width), F32),
            jax.ShapeDtypeStruct((steps, runs2, run2, width), BF16),
            jax.ShapeDtypeStruct((steps, runs2, run2, width), BF16),
            jax.ShapeDtypeStruct((runs1, run1, hidden_width), BF16),
            jax.ShapeDtypeStruct((runs1, run1, hidden_width), BF16),
            jax.ShapeDtypeStruct((1, width), F32),
            jax.ShapeDtypeStruct((1, hidden_width), F32),
        ],
        compiler_params=pltpu.CompilerParams(vmem_limit_bytes=58 * MIB),
        cost_estimate=pl.CostEstimate(flops=8 * tokens * width * hidden_width, transcendentals=0, bytes_accessed=35_000_000),
        name="mlp_back",
    )(scal, mine, own, oth, n2, hidden, slope, w["fc1_weight"], w["fc2_weight"])


def attend_back_kernel(
    scal_ref, own_ref, oth_ref, dn2_ref, mid_ref, qkv_ref, probs_ref, wp_ref, g2_ref,
    dmid_ref, dbr_ref, djoin_ref, g2g_ref, g2b_ref, pbg_ref, qbg_ref, vbg_ref, datt_ref,
):
    image = pl.program_id(0)
    half, width = own_ref.shape[1], own_ref.shape[2]
    rows = 2 * half
    live = row_valid(scal_ref, image, rows, half, 0)
    d_final = jnp.where(live, jnp.concatenate([own_ref[0].astype(F32), oth_ref[0].astype(F32)], axis=0), 0.0)
    unit, rstd = norm_parts(mid_ref[0])
    dn2 = dn2_ref[0]
    gain_part = jnp.sum(dn2 * unit, axis=0, keepdims=True)
    bias_part = jnp.sum(dn2, axis=0, keepdims=True)
    d_middle = d_final + norm_back(dn2, g2_ref[...], unit, rstd)
    dmid_ref[0] = d_middle
    keep = scal_ref[image, 4].astype(F32) * KEEP_SCALE
    d_branch = (d_middle * keep).astype(BF16)
    dbr_ref[0] = d_branch
    proj_part = jnp.sum(d_branch.astype(F32), axis=0, keepdims=True)
    datt_ref[...] = dot_nt(d_branch, wp_ref[...]).astype(BF16)
    low_lane = lax.broadcasted_iota(jnp.int32, (rows, 128), 1) < HEAD_DIM
    for pair in range(width // 128):
        cut = slice(128 * pair, 128 * pair + 128)
        q2 = qkv_ref[0, :, cut]
        k2 = qkv_ref[0, :, width + 128 * pair : width + 128 * pair + 128]
        v2 = qkv_ref[0, :, 2 * width + 128 * pair : 2 * width + 128 * pair + 128]
        a2 = datt_ref[:, cut]
        dq = dk = dv = None
        for side in range(2):
            mine = low_lane if side == 0 else jnp.logical_not(low_lane)
            probs_low = probs_ref[0, 2 * pair + side]
            probs = probs_low.astype(F32)
            a_side = jnp.where(mine, a2, 0)
            d_probs = dot_nt(a_side, v2)
            inner = jnp.sum(probs * d_probs, axis=-1, keepdims=True)
            d_scores = (probs * (d_probs - inner)).astype(BF16)
            dq_part = dot_nn(d_scores, jnp.where(mine, k2, 0))
            dk_part = dot_tn(d_scores, jnp.where(mine, q2, 0))
            dv_part = dot_tn(probs_low, a_side)
            dq = dq_part if dq is None else dq + dq_part
            dk = dk_part if dk is None else dk + dk_part
            dv = dv_part if dv is None else dv + dv_part
        djoin_ref[0, :, cut] = (dq * HEAD_DIM**-0.5).astype(BF16)
        djoin_ref[0, :, width + 128 * pair : width + 128 * pair + 128] = dk.astype(BF16)
        djoin_ref[0, :, 2 * width + 128 * pair : 2 * width + 128 * pair + 128] = dv.astype(BF16)
    q_part = jnp.sum(djoin_ref[0, :, :width].astype(F32), axis=0, keepdims=True)
    v_part = jnp.sum(djoin_ref[0, :, 2 * width :].astype(F32), axis=0, keepdims=True)
    sums = ((g2g_ref, gain_part), (g2b_ref, bias_part), (pbg_ref, proj_part), (qbg_ref, q_part), (vbg_ref, v_part))

    @pl.when(image == 0)
    def _():
        for ref, part in sums:
            ref[...] = part

    @pl.when(image > 0)
    def _():
        for ref, part in sums:
            ref[...] += part


def attend_back(scal, own, oth, dn2, middle, qkv, probs, w):
    images, half, width = own.shape
    rows = 2 * half
    heads = width // HEAD_DIM
    per = lambda *tail: pl.BlockSpec((1,) + tail, lambda i, s: (i,) + (0,) * len(tail))
    vec = jax.ShapeDtypeStruct((1, width), F32)
    return pl.pallas_call(
        attend_back_kernel,
        grid_spec=pltpu.PrefetchScalarGridSpec(
            num_scalar_prefetch=1,
            grid=(images,),
            in_specs=[
                per(half, width), per(half, width), per(rows, width), per(rows, width), per(rows, 3 * width),
                per(heads, rows, rows), full((width, width)), full((1, width)),
            ],
            out_specs=[per(rows, width), per(rows, width), per(rows, 3 * width)] + [full((1, width))] * 5,
            scratch_shapes=[pltpu.VMEM((rows, width), BF16)],
        ),
        out_shape=[
            jax.ShapeDtypeStruct((images, rows, width), F32),
            jax.ShapeDtypeStruct((images, rows, width), BF16),
            jax.ShapeDtypeStruct((images, rows, 3 * width), BF16),
            vec, vec, vec, vec, vec,
        ],
        compiler_params=pltpu.CompilerParams(vmem_limit_bytes=56 * MIB),
        cost_estimate=pl.CostEstimate(flops=2 * images * rows * width * (width + 8 * rows), transcendentals=0, bytes_accessed=35_000_000),
        name="attend_back",
    )(scal, own, oth, dn2, middle, qkv, probs, w["proj_weight"], w["ln2_gain"])


def tail_kernel(
    mine_ref, n1_ref, djoin_ref, att_ref, dbr_ref, wqkv_ref, xo_ref, xt_ref, dmid_ref, g1_ref,
    send_ref, keep_ref, go_ref, gt_ref, g1g_ref, g1b_ref, grad_ref, acc_ref,
):
    step = pl.program_id(0)
    last = pl.num_programs(0) - 1
    images, half, width = xo_ref.shape
    rows = 2 * half
    mine = mine_ref[0]

    @pl.when(step < last)
    def _():
        put_halves(grad_ref, dot_tn(n1_ref[...], djoin_ref[...]), send_ref, keep_ref, mine, ())
        part = dot_nt(djoin_ref[...], wqkv_ref[...])

        @pl.when(step == 0)
        def _():
            acc_ref[...] = part

        @pl.when(step > 0)
        def _():
            acc_ref[...] += part

    @pl.when(step == last)
    def _():
        put_halves(grad_ref, dot_tn(att_ref[...], dbr_ref[...]), send_ref, keep_ref, mine, ())
        gain_sum = jnp.zeros((1, width), F32)
        bias_sum = jnp.zeros((1, width), F32)
        for image in range(images):
            x = jnp.concatenate([xo_ref[image].astype(F32), xt_ref[image].astype(F32)], axis=0)
            unit, rstd = norm_parts(x)
            dn1 = acc_ref[rows * image : rows * image + rows, :]
            gain_sum += jnp.sum(dn1 * unit, axis=0, keepdims=True)
            bias_sum += jnp.sum(dn1, axis=0, keepdims=True)
            out = dmid_ref[rows * image : rows * image + rows, :] + norm_back(dn1, g1_ref[...], unit, rstd)
            go_ref[image] = out[:half]
            gt_ref[image] = out[half:].astype(BF16)
        g1g_ref[...] = gain_sum
        g1b_ref[...] = bias_sum


def tail(mine, n1, d_join, attended, d_branch, own, oth, d_middle, w, run):
    tokens, width = n1.shape
    images, half, _ = own.shape
    runs = width // (2 * run)
    halves = pl.BlockSpec((runs, run, width), lambda j, m: (0, 0, j))
    clip = lambda j: jnp.minimum(j, 2)
    return pl.pallas_call(
        tail_kernel,
        grid_spec=pltpu.PrefetchScalarGridSpec(
            num_scalar_prefetch=1,
            grid=(4,),
            in_specs=[
                full((tokens, width)), pl.BlockSpec((tokens, width), lambda j, m: (0, clip(j))), full((tokens, width)),
                full((tokens, width)), pl.BlockSpec((width, width), lambda j, m: (0, clip(j))),
                full((images, half, width)), full((images, half, width)), full((tokens, width)), full((1, width)),
            ],
            out_specs=[
                halves, halves, full((images, half, width)), full((images, half, width)),
                full((1, width)), full((1, width)),
            ],
            scratch_shapes=[pltpu.VMEM((width, width), BF16), pltpu.VMEM((tokens, width), F32)],
        ),
        out_shape=[
            jax.ShapeDtypeStruct((runs, run, 4 * width), BF16),
            jax.ShapeDtypeStruct((runs, run, 4 * width), BF16),
            jax.ShapeDtypeStruct((images, half, width), F32),
            jax.ShapeDtypeStruct((images, half, width), BF16),
            jax.ShapeDtypeStruct((1, width), F32),
            jax.ShapeDtypeStruct((1, width), F32),
        ],
        compiler_params=pltpu.CompilerParams(vmem_limit_bytes=56 * MIB),
        cost_estimate=pl.CostEstimate(flops=14 * tokens * width * width, transcendentals=0, bytes_accessed=35_000_000),
        name="tail",
    )(mine, n1, d_join, attended, d_branch, w["qkv_weight"], own, oth, d_middle, w["ln1_gain"])


def swap(value, axis, bit, size):
    return lax.ppermute(value, axis, [(i, i ^ bit) for i in range(size)])


def shards(img_size, args):
    (patches, grid_shape, split_rows, owner_shard, drop_masks, ln1_gain, ln1_bias, qkv_weight, qv_bias, proj_weight,
     proj_bias, ln2_gain, ln2_bias, fc1_weight, fc1_bias, fc2_weight, fc2_bias, cotangent) = args
    all_images, _, half, width = patches.shape
    images = all_images // 2
    rows = 2 * half
    tokens = images * rows
    side = lax.axis_index("seq")
    line = lax.axis_index("img")
    owners = 2 * img_size
    row = lambda v: v.reshape(1, -1)
    w = dict(
        ln1_gain=row(ln1_gain), ln1_bias=row(ln1_bias), qkv_weight=qkv_weight, q_bias=row(qv_bias[:width]),
        v_bias=row(qv_bias[width:]), proj_weight=proj_weight, proj_bias=row(proj_bias), ln2_gain=row(ln2_gain),
        ln2_bias=row(ln2_bias), fc1_weight=fc1_weight, fc1_bias=row(fc1_bias), fc2_weight=fc2_weight, fc2_bias=row(fc2_bias),
    )

    def exchange(value):
        value = value.reshape(all_images, half, width)
        own = lax.dynamic_slice_in_dim(value, side * images, images, axis=0)
        away = lax.dynamic_slice_in_dim(value, (1 - side) * images, images, axis=0)
        return own, swap(away, "seq", 1, 2)

    def restore(own, oth):
        back = swap(oth, "seq", 1, 2).astype(own.dtype)
        first = jnp.where(side == 0, own, back)
        second = jnp.where(side == 0, back, own)
        return jnp.concatenate([first, second], axis=0).reshape(all_images, 1, half, width)

    x_own, x_oth = exchange(patches)
    c_own, c_oth = exchange(cotangent)
    across = grid_shape[:, 1]
    counts = jnp.stack([split_rows * across, (grid_shape[:, 0] - split_rows) * across], axis=0)
    count_own = jnp.where(side == 0, counts[0], counts[1])
    count_oth = jnp.where(side == 0, counts[1], counts[0])
    special = (owner_shard == side).astype(jnp.int32)
    table = jnp.stack([count_own, special, count_oth, 1 - special, drop_masks[:, 0], drop_masks[:, 1]], axis=1)
    scal = lax.dynamic_slice_in_dim(table, side * images, images, axis=0)

    n1, qkv, probs, attended, middle, n2 = front(scal, x_own, x_oth, w)
    flat = lambda v: v.reshape(tokens, v.shape[-1])
    hidden, slope, out_own, out_oth = mlp(scal, flat(n2), flat(middle), w, images, 512)
    layer_out = restore(out_own, out_oth)

    mine = lax.rem(line, 2).reshape(1)
    run1 = 2 * (width // owners)
    run2 = 2 * (fc2_weight.shape[0] // owners)
    dn2, s2, k2, s1, k1, fc2_bias_grad, fc1_bias_grad = mlp_back(
        scal, mine, c_own, c_oth, flat(n2), hidden, slope, w, run1, run2
    )
    d_middle, d_branch, d_join, ln2_gain_grad, ln2_bias_grad, proj_bias_grad, q_grad, v_grad = attend_back(
        scal, c_own, c_oth, dn2.reshape(images, rows, width), middle, qkv, probs, w
    )
    st, kt, grad_own, grad_oth, ln1_gain_grad, ln1_bias_grad = tail(
        mine, flat(n1), flat(d_join), flat(attended), flat(d_branch), x_own, x_oth, flat(d_middle), w, run1
    )
    patches_grad = restore(grad_own, grad_oth)

    levels = []
    bit = 2
    while bit < img_size:
        levels.append(bit)
        bit *= 2

    def scatter(send, keep, order):
        cols = send.shape[-1]
        span = (2,) * (len(levels) + 1)
        shape = span + (-1, cols)
        total = keep.reshape(shape).astype(F32) + swap(send, "img", 1, img_size).reshape(shape).astype(F32)
        left = list(range(len(levels), -1, -1))
        for level in order:
            if level == 0:
                here, name, mask, size = side, "seq", 1, 2
            else:
                here, name, mask, size = (line // levels[level - 1]) % 2, "img", levels[level - 1], img_size
            dim = left.index(level)
            total = total.astype(BF16)
            away = lax.dynamic_index_in_dim(total, 1 - here, dim, keepdims=False)
            stay = lax.dynamic_index_in_dim(total, here, dim, keepdims=False)
            total = stay.astype(F32) + swap(away, name, mask, size).astype(F32)
            left.pop(dim)
        return total

    top = len(levels)
    order_a = list(range(1, top + 1)) + [0]
    order_b = [2] + [1] + list(range(3, top + 1)) + [0]
    fc2_grad = scatter(s2, k2, order_a)
    fc1_grad = scatter(s1, k1, order_b)
    tail_grad = scatter(st, kt, order_a)
    qkv_grad, proj_grad = tail_grad[:, : 3 * width], tail_grad[:, 3 * width :]

    small = jnp.concatenate(
        [v.reshape(owners, -1) for v in (
            ln1_gain_grad, ln1_bias_grad, jnp.concatenate([q_grad, v_grad], axis=1), proj_bias_grad, ln2_gain_grad,
            ln2_bias_grad, fc1_bias_grad, fc2_bias_grad)],
        axis=1,
    )
    small = lax.psum_scatter(small, ("img", "seq"), scatter_dimension=0, tiled=True).reshape(-1)
    unit = width // owners
    pieces = []
    at = 0
    for count in (1, 1, 2, 1, 1, 1, fc1_weight.shape[1] // width, 1):
        pieces.append(small[at : at + count * unit])
        at += count * unit
    l1g, l1b, qvb, pjb, l2g, l2b, f1b, f2b = pieces
    return (
        layer_out, patches_grad, l1g, l1b, qkv_grad, qvb, proj_grad, pjb, l2g, l2b, fc1_grad, f1b, fc2_grad, f2b,
    )


def solution(mesh):
    rep = [P()] * 12
    vec = P(("img", "seq"))
    mat = P(("img", "seq"), None)
    rows = P("img", "seq", None, None)

    def run(*args):
        return shards(mesh.shape["img"], args)

    return jax.shard_map(
        run,
        mesh=mesh,
        in_specs=(rows, P("img", None), P("img"), P("img"), P("img", None), *rep, rows),
        out_specs=(rows, rows, vec, vec, mat, vec, mat, vec, vec, vec, mat, vec, mat, vec),
        check_vma=False,
    )
```

```python
import functools

import jax
import jax.numpy as jnp
from jax import lax
from jax.experimental import pallas as pl
from jax.experimental.pallas import tpu as pltpu
from jax.sharding import PartitionSpec as P

HEAD_DIM = 64
LN_EPS = 1e-06
KEEP_SCALE = 1.0 / 0.9
MASK_FILL = -1e30
BF16 = jnp.bfloat16
F32 = jnp.float32
MIB = 1024 * 1024


def dot_nn(a, b):
    return lax.dot_general(a, b, (((1,), (0,)), ((), ())), preferred_element_type=F32)


def dot_nt(a, b):
    return lax.dot_general(a, b, (((1,), (1,)), ((), ())), preferred_element_type=F32)


def dot_tn(a, b):
    return lax.dot_general(a, b, (((0,), (0,)), ((), ())), preferred_element_type=F32)


def norm_parts(values):
    row_mean = jnp.mean(values, axis=-1, keepdims=True)
    centred = values - row_mean
    variance = jnp.mean(centred * centred, axis=-1, keepdims=True)
    rstd = lax.rsqrt(variance + LN_EPS)
    return centred * rstd, rstd


def norm_back(d_normed, gain, unit, rstd):
    d_unit = d_normed * gain
    mean_one = jnp.mean(d_unit, axis=-1, keepdims=True)
    mean_two = jnp.mean(d_unit * unit, axis=-1, keepdims=True)
    return rstd * (d_unit - mean_one - unit * mean_two)


def gelu_both(values):
    size = jnp.abs(values)
    t = 1.0 / (1.0 + 0.23164189 * size)
    bell = jnp.exp(-0.5 * values * values)
    poly = t * (
        0.127414796
        + t * (-0.142248368 + t * (0.7107068705 + t * (-0.7265760135 + t * 0.5307027145)))
    )
    tail = poly * bell
    cdf = jnp.where(values >= 0.0, 1.0 - tail, tail)
    return values * cdf, cdf + values * (0.3989422804014327 * bell)


def row_valid(scal_ref, image, rows, half, axis):
    shape = (rows, 1) if axis == 0 else (1, rows)
    slot = lax.broadcasted_iota(jnp.int32, shape, axis)
    other = slot >= half
    place = jnp.where(other, slot - half, slot)
    count = jnp.where(other, scal_ref[image, 2], scal_ref[image, 0])
    special = jnp.where(other, scal_ref[image, 3], scal_ref[image, 1])
    return jnp.where(place < 2, special, (place - 2 < count).astype(jnp.int32)) > 0


def front_kernel(
    scal_ref, own_ref, oth_ref, g1_ref, b1_ref, wqkv_ref, qb_ref, vb_ref, wp_ref, pb_ref, g2_ref, b2_ref,
    n1_ref, qkv_ref, probs_ref, att_ref, mid_ref, n2_ref,
):
    image = pl.program_id(0)
    half, width = own_ref.shape[1], own_ref.shape[2]
    rows = 2 * half
    x = jnp.concatenate([own_ref[0].astype(F32), oth_ref[0].astype(F32)], axis=0)
    unit, _ = norm_parts(x)
    n1 = (unit * g1_ref[...] + b1_ref[...]).astype(BF16)
    n1_ref[0] = n1
    qkv_ref[0, :, :width] = ((dot_nn(n1, wqkv_ref[:, :width]) + qb_ref[...]).astype(BF16) * BF16(HEAD_DIM**-0.5))
    qkv_ref[0, :, width : 2 * width] = dot_nn(n1, wqkv_ref[:, width : 2 * width]).astype(BF16)
    qkv_ref[0, :, 2 * width :] = (dot_nn(n1, wqkv_ref[:, 2 * width :]) + vb_ref[...]).astype(BF16)
    fill = jnp.where(row_valid(scal_ref, image, rows, half, 1), 0.0, MASK_FILL)
    low_lane = lax.broadcasted_iota(jnp.int32, (rows, 128), 1) < HEAD_DIM
    for pair in range(width // 128):
        cut = slice(128 * pair, 128 * pair + 128)
        q2 = qkv_ref[0, :, cut]
        k2 = qkv_ref[0, :, width + 128 * pair : width + 128 * pair + 128]
        v2 = qkv_ref[0, :, 2 * width + 128 * pair : 2 * width + 128 * pair + 128]
        total = None
        for side in range(2):
            mine = low_lane if side == 0 else jnp.logical_not(low_lane)
            scores = dot_nt(jnp.where(mine, q2, 0), k2) + fill
            top = jnp.max(scores, axis=-1, keepdims=True)
            weight = jnp.exp(scores - top)
            probs = (weight * (1.0 / jnp.sum(weight, axis=-1, keepdims=True))).astype(BF16)
            probs_ref[0, 2 * pair + side] = probs
            part = dot_nn(probs, jnp.where(mine, v2, 0))
            total = part if total is None else total + part
        att_ref[0, :, cut] = total.astype(BF16)
    keep = scal_ref[image, 4].astype(F32) * KEEP_SCALE
    branch = dot_nn(att_ref[0], wp_ref[...]) + pb_ref[...]
    middle = jnp.concatenate([own_ref[0].astype(F32), oth_ref[0].astype(F32)], axis=0) + keep * branch
    mid_ref[0] = middle
    unit, _ = norm_parts(middle)
    n2_ref[0] = (unit * g2_ref[...] + b2_ref[...]).astype(BF16)


def full(shape):
    zeros = (0,) * len(shape)
    return pl.BlockSpec(shape, lambda *_: zeros, pipeline_mode=pl.Buffered(1))


def front(scal, own, oth, w):
    images, half, width = own.shape
    rows = 2 * half
    heads = width // HEAD_DIM
    per = lambda *tail: pl.BlockSpec((1,) + tail, lambda i, s: (i,) + (0,) * len(tail))
    flops = 2 * images * rows * width * (4 * width + 4 * rows)
    return pl.pallas_call(
        front_kernel,
        grid_spec=pltpu.PrefetchScalarGridSpec(
            num_scalar_prefetch=1,
            grid=(images,),
            in_specs=[
                per(half, width), per(half, width), full((1, width)), full((1, width)),
                full((width, 3 * width)), full((1, width)), full((1, width)),
                full((width, width)), full((1, width)), full((1, width)), full((1, width)),
            ],
            out_specs=[
                per(rows, width), per(rows, 3 * width), per(heads, rows, rows),
                per(rows, width), per(rows, width), per(rows, width),
            ],
        ),
        out_shape=[
            jax.ShapeDtypeStruct((images, rows, width), BF16),
            jax.ShapeDtypeStruct((images, rows, 3 * width), BF16),
            jax.ShapeDtypeStruct((images, heads, rows, rows), BF16),
            jax.ShapeDtypeStruct((images, rows, width), BF16),
            jax.ShapeDtypeStruct((images, rows, width), F32),
            jax.ShapeDtypeStruct((images, rows, width), BF16),
        ],
        compiler_params=pltpu.CompilerParams(vmem_limit_bytes=56 * MIB),
        cost_estimate=pl.CostEstimate(flops=flops, transcendentals=images * heads * rows * rows, bytes_accessed=30_000_000),
        name="front",
    )(scal, own, oth, w["ln1_gain"], w["ln1_bias"], w["qkv_weight"], w["q_bias"], w["v_bias"],
      w["proj_weight"], w["proj_bias"], w["ln2_gain"], w["ln2_bias"])


def mlp_kernel(
    scal_ref, n2_ref, mid_ref, w1_ref, c1_ref, w2_ref, c2_ref,
    hid_ref, slope_ref, own_ref, oth_ref, acc_ref,
):
    step = pl.program_id(0)
    images, half, width = own_ref.shape
    rows = 2 * half
    hidden, slope = gelu_both(dot_nn(n2_ref[...], w1_ref[...]) + c1_ref[...])
    hidden = hidden.astype(BF16)
    hid_ref[...] = hidden
    slope_ref[...] = slope.astype(BF16)
    part = dot_nn(hidden, w2_ref[...])

    @pl.when(step == 0)
    def _():
        acc_ref[...] = part

    @pl.when(step > 0)
    def _():
        acc_ref[...] += part

    @pl.when(step == pl.num_programs(0) - 1)
    def _():
        for image in range(images):
            keep = scal_ref[image, 5].astype(F32) * KEEP_SCALE
            cut = slice(rows * image, rows * image + rows)
            final = mid_ref[cut, :] + keep * (acc_ref[cut, :] + c2_ref[...])
            out = jnp.where(row_valid(scal_ref, image, rows, half, 0), final, 0.0).astype(BF16)
            own_ref[image] = out[:half]
            oth_ref[image] = out[half:]


def mlp(scal, n2, middle, w, images, tile):
    tokens, width = n2.shape
    hidden_width = w["fc1_weight"].shape[1]
    half = tokens // images // 2
    return pl.pallas_call(
        mlp_kernel,
        grid_spec=pltpu.PrefetchScalarGridSpec(
            num_scalar_prefetch=1,
            grid=(hidden_width // tile,),
            in_specs=[
                full((tokens, width)), full((tokens, width)),
                pl.BlockSpec((width, tile), lambda j, s: (0, j)), pl.BlockSpec((1, tile), lambda j, s: (0, j)),
                pl.BlockSpec((tile, width), lambda j, s: (j, 0)), full((1, width)),
            ],
            out_specs=[
                pl.BlockSpec((tokens, tile), lambda j, s: (0, j)), pl.BlockSpec((tokens, tile), lambda j, s: (0, j)),
                full((images, half, width)), full((images, half, width)),
            ],
            scratch_shapes=[pltpu.VMEM((tokens, width), F32)],
        ),
        out_shape=[
            jax.ShapeDtypeStruct((tokens, hidden_width), BF16),
            jax.ShapeDtypeStruct((tokens, hidden_width), BF16),
            jax.ShapeDtypeStruct((images, half, width), BF16),
            jax.ShapeDtypeStruct((images, half, width), BF16),
        ],
        compiler_params=pltpu.CompilerParams(vmem_limit_bytes=56 * MIB),
        cost_estimate=pl.CostEstimate(flops=4 * tokens * width * hidden_width, transcendentals=2 * tokens * hidden_width, bytes_accessed=30_000_000),
        name="mlp",
    )(scal, n2, middle, w["fc1_weight"], w["fc1_bias"], w["fc2_weight"], w["fc2_bias"])


def put_rows(grad_ref, value, send_ref, keep_ref, mine, lead):
    grad_ref[...] = value
    run = 2 * send_ref.shape[-2]
    for k in range(grad_ref.shape[0] // (2 * run)):
        for ref, core in ((send_ref, 1 - mine), (keep_ref, mine)):
            for x in range(2):
                at = pl.multiple_of((2 * k + core) * run + x * (run // 2), 8)
                ref[lead + (k, x)] = grad_ref[pl.ds(at, run // 2), :].astype(BF16)


def put_folded(grad_ref, value, send_ref, keep_ref, mine):
    grad_ref[...] = value
    unit = send_ref.shape[-2] // 2
    side = grad_ref.shape[1] // 2
    for k in range(grad_ref.shape[0] // (4 * unit)):
        for ref, core in ((send_ref, 1 - mine), (keep_ref, mine)):
            for x in range(2):
                at = pl.multiple_of((4 * k + 2 * core + x) * unit, 8)
                piece = grad_ref[pl.ds(at, unit), :]
                ref[k, x] = jnp.concatenate([piece[:, :side], piece[:, side:]], axis=0).astype(BF16)


def mlp_back_kernel(
    scal_ref, mine_ref, own_ref, oth_ref, n2_ref, hid_ref, slope_ref, w1_ref, w2_ref,
    dn2_ref, s2_ref, k2_ref, s1_ref, k1_ref, c2_ref, c1_ref, dmlp_ref, grad_ref, acc_ref,
):
    step = pl.program_id(0)
    images, half, width = own_ref.shape
    rows = 2 * half
    mine = mine_ref[0]

    @pl.when(step == 0)
    def _():
        total = jnp.zeros((1, width), F32)
        for image in range(images):
            keep = scal_ref[image, 5].astype(F32) * KEEP_SCALE
            cot = jnp.concatenate([own_ref[image].astype(F32), oth_ref[image].astype(F32)], axis=0)
            live = row_valid(scal_ref, image, rows, half, 0)
            d_mlp = (jnp.where(live, cot, 0.0) * keep).astype(BF16)
            dmlp_ref[rows * image : rows * image + rows, :] = d_mlp
            total += jnp.sum(d_mlp.astype(F32), axis=0, keepdims=True)
        c2_ref[...] = total

    d_pre = slope_ref[...].astype(F32) * dot_nt(dmlp_ref[...], w2_ref[...])
    d_pre = d_pre.astype(BF16)
    c1_ref[...] = jnp.sum(d_pre.astype(F32), axis=0, keepdims=True)
    part = dot_nt(d_pre, w1_ref[...])
    put_folded(grad_ref, dot_tn(n2_ref[...], d_pre), s1_ref, k1_ref, mine)
    put_rows(grad_ref, dot_tn(hid_ref[...], dmlp_ref[...]), s2_ref, k2_ref, mine, (0,))

    @pl.when(step == 0)
    def _():
        acc_ref[...] = part

    @pl.when(step > 0)
    def _():
        acc_ref[...] += part

    @pl.when(step == pl.num_programs(0) - 1)
    def _():
        dn2_ref[...] = acc_ref[...]


def mlp_back(scal, mine, own, oth, n2, hidden, slope, w, unit1, unit2):
    tokens, width = n2.shape
    images, half, _ = own.shape
    hidden_width = hidden.shape[1]
    tile = width
    steps = hidden_width // tile
    runs1, runs2 = width // (4 * unit1), tile // (4 * unit2)
    col = pl.BlockSpec((tokens, tile), lambda j, s, m: (0, j))
    half1 = pl.BlockSpec((runs1, 2, 2 * unit1, tile // 2), lambda j, s, m: (0, 0, 0, j))
    half2 = pl.BlockSpec((1, runs2, 2, unit2, width), lambda j, s, m: (j, 0, 0, 0, 0))
    return pl.pallas_call(
        mlp_back_kernel,
        grid_spec=pltpu.PrefetchScalarGridSpec(
            num_scalar_prefetch=2,
            grid=(steps,),
            in_specs=[
                full((images, half, width)), full((images, half, width)), full((tokens, width)), col, col,
                pl.BlockSpec((width, tile), lambda j, s, m: (0, j)), pl.BlockSpec((tile, width), lambda j, s, m: (j, 0)),
            ],
            out_specs=[
                full((tokens, width)), half2, half2, half1, half1,
                full((1, width)), pl.BlockSpec((1, tile), lambda j, s, m: (0, j)),
            ],
            scratch_shapes=[
                pltpu.VMEM((tokens, width), BF16), pltpu.VMEM((width, width), F32), pltpu.VMEM((tokens, width), F32),
            ],
        ),
        out_shape=[
            jax.ShapeDtypeStruct((tokens, width), F32),
            jax.ShapeDtypeStruct((steps, runs2, 2, unit2, width), BF16),
            jax.ShapeDtypeStruct((steps, runs2, 2, unit2, width), BF16),
            jax.ShapeDtypeStruct((runs1, 2, 2 * unit1, hidden_width // 2), BF16),
            jax.ShapeDtypeStruct((runs1, 2, 2 * unit1, hidden_width // 2), BF16),
            jax.ShapeDtypeStruct((1, width), F32),
            jax.ShapeDtypeStruct((1, hidden_width), F32),
        ],
        compiler_params=pltpu.CompilerParams(vmem_limit_bytes=58 * MIB),
        cost_estimate=pl.CostEstimate(flops=8 * tokens * width * hidden_width, transcendentals=0, bytes_accessed=35_000_000),
        name="mlp_back",
    )(scal, mine, own, oth, n2, hidden, slope, w["fc1_weight"], w["fc2_weight"])


def attend_back_kernel(
    scal_ref, own_ref, oth_ref, dn2_ref, mid_ref, qkv_ref, probs_ref, wp_ref, g2_ref,
    dmid_ref, dbr_ref, djoin_ref, g2g_ref, g2b_ref, pbg_ref, qbg_ref, vbg_ref, datt_ref,
):
    image = pl.program_id(0)
    half, width = own_ref.shape[1], own_ref.shape[2]
    rows = 2 * half
    live = row_valid(scal_ref, image, rows, half, 0)
    d_final = jnp.where(live, jnp.concatenate([own_ref[0].astype(F32), oth_ref[0].astype(F32)], axis=0), 0.0)
    unit, rstd = norm_parts(mid_ref[0])
    dn2 = dn2_ref[0]
    gain_part = jnp.sum(dn2 * unit, axis=0, keepdims=True)
    bias_part = jnp.sum(dn2, axis=0, keepdims=True)
    d_middle = d_final + norm_back(dn2, g2_ref[...], unit, rstd)
    dmid_ref[0] = d_middle
    keep = scal_ref[image, 4].astype(F32) * KEEP_SCALE
    d_branch = (d_middle * keep).astype(BF16)
    dbr_ref[0] = d_branch
    proj_part = jnp.sum(d_branch.astype(F32), axis=0, keepdims=True)
    datt_ref[...] = dot_nt(d_branch, wp_ref[...]).astype(BF16)
    low_lane = lax.broadcasted_iota(jnp.int32, (rows, 128), 1) < HEAD_DIM
    for pair in range(width // 128):
        cut = slice(128 * pair, 128 * pair + 128)
        q2 = qkv_ref[0, :, cut]
        k2 = qkv_ref[0, :, width + 128 * pair : width + 128 * pair + 128]
        v2 = qkv_ref[0, :, 2 * width + 128 * pair : 2 * width + 128 * pair + 128]
        a2 = datt_ref[:, cut]
        dq = dk = dv = None
        for side in range(2):
            mine = low_lane if side == 0 else jnp.logical_not(low_lane)
            probs_low = probs_ref[0, 2 * pair + side]
            probs = probs_low.astype(F32)
            a_side = jnp.where(mine, a2, 0)
            d_probs = dot_nt(a_side, v2)
            inner = jnp.sum(probs * d_probs, axis=-1, keepdims=True)
            d_scores = (probs * (d_probs - inner)).astype(BF16)
            dq_part = dot_nn(d_scores, jnp.where(mine, k2, 0))
            dk_part = dot_tn(d_scores, jnp.where(mine, q2, 0))
            dv_part = dot_tn(probs_low, a_side)
            dq = dq_part if dq is None else dq + dq_part
            dk = dk_part if dk is None else dk + dk_part
            dv = dv_part if dv is None else dv + dv_part
        djoin_ref[0, :, cut] = (dq * HEAD_DIM**-0.5).astype(BF16)
        djoin_ref[0, :, width + 128 * pair : width + 128 * pair + 128] = dk.astype(BF16)
        djoin_ref[0, :, 2 * width + 128 * pair : 2 * width + 128 * pair + 128] = dv.astype(BF16)
    q_part = jnp.sum(djoin_ref[0, :, :width].astype(F32), axis=0, keepdims=True)
    v_part = jnp.sum(djoin_ref[0, :, 2 * width :].astype(F32), axis=0, keepdims=True)
    sums = ((g2g_ref, gain_part), (g2b_ref, bias_part), (pbg_ref, proj_part), (qbg_ref, q_part), (vbg_ref, v_part))

    @pl.when(image == 0)
    def _():
        for ref, part in sums:
            ref[...] = part

    @pl.when(image > 0)
    def _():
        for ref, part in sums:
            ref[...] += part


def attend_back(scal, own, oth, dn2, middle, qkv, probs, w):
    images, half, width = own.shape
    rows = 2 * half
    heads = width // HEAD_DIM
    per = lambda *tail: pl.BlockSpec((1,) + tail, lambda i, s: (i,) + (0,) * len(tail))
    vec = jax.ShapeDtypeStruct((1, width), F32)
    return pl.pallas_call(
        attend_back_kernel,
        grid_spec=pltpu.PrefetchScalarGridSpec(
            num_scalar_prefetch=1,
            grid=(images,),
            in_specs=[
                per(half, width), per(half, width), per(rows, width), per(rows, width), per(rows, 3 * width),
                per(heads, rows, rows), full((width, width)), full((1, width)),
            ],
            out_specs=[per(rows, width), per(rows, width), per(rows, 3 * width)] + [full((1, width))] * 5,
            scratch_shapes=[pltpu.VMEM((rows, width), BF16)],
        ),
        out_shape=[
            jax.ShapeDtypeStruct((images, rows, width), F32),
            jax.ShapeDtypeStruct((images, rows, width), BF16),
            jax.ShapeDtypeStruct((images, rows, 3 * width), BF16),
            vec, vec, vec, vec, vec,
        ],
        compiler_params=pltpu.CompilerParams(vmem_limit_bytes=56 * MIB),
        cost_estimate=pl.CostEstimate(flops=2 * images * rows * width * (width + 8 * rows), transcendentals=0, bytes_accessed=35_000_000),
        name="attend_back",
    )(scal, own, oth, dn2, middle, qkv, probs, w["proj_weight"], w["ln2_gain"])


def tail_kernel(
    mine_ref, n1_ref, djoin_ref, att_ref, dbr_ref, wqkv_ref, xo_ref, xt_ref, dmid_ref, g1_ref,
    send_ref, keep_ref, go_ref, gt_ref, g1g_ref, g1b_ref, grad_ref, acc_ref,
):
    step = pl.program_id(0)
    last = pl.num_programs(0) - 1
    images, half, width = xo_ref.shape
    rows = 2 * half
    mine = mine_ref[0]

    @pl.when(step < last)
    def _():
        put_folded(grad_ref, dot_tn(n1_ref[...], djoin_ref[...]), send_ref, keep_ref, mine)
        part = dot_nt(djoin_ref[...], wqkv_ref[...])

        @pl.when(step == 0)
        def _():
            acc_ref[...] = part

        @pl.when(step > 0)
        def _():
            acc_ref[...] += part

    @pl.when(step == last)
    def _():
        put_folded(grad_ref, dot_tn(att_ref[...], dbr_ref[...]), send_ref, keep_ref, mine)
        gain_sum = jnp.zeros((1, width), F32)
        bias_sum = jnp.zeros((1, width), F32)
        for image in range(images):
            x = jnp.concatenate([xo_ref[image].astype(F32), xt_ref[image].astype(F32)], axis=0)
            unit, rstd = norm_parts(x)
            dn1 = acc_ref[rows * image : rows * image + rows, :]
            gain_sum += jnp.sum(dn1 * unit, axis=0, keepdims=True)
            bias_sum += jnp.sum(dn1, axis=0, keepdims=True)
            out = dmid_ref[rows * image : rows * image + rows, :] + norm_back(dn1, g1_ref[...], unit, rstd)
            go_ref[image] = out[:half]
            gt_ref[image] = out[half:].astype(BF16)
        g1g_ref[...] = gain_sum
        g1b_ref[...] = bias_sum


def tail(mine, n1, d_join, attended, d_branch, own, oth, d_middle, w, unit):
    tokens, width = n1.shape
    images, half, _ = own.shape
    runs = width // (4 * unit)
    halves = pl.BlockSpec((runs, 2, 2 * unit, width // 2), lambda j, m: (0, 0, 0, j))
    clip = lambda j: jnp.minimum(j, 2)
    return pl.pallas_call(
        tail_kernel,
        grid_spec=pltpu.PrefetchScalarGridSpec(
            num_scalar_prefetch=1,
            grid=(4,),
            in_specs=[
                full((tokens, width)), pl.BlockSpec((tokens, width), lambda j, m: (0, clip(j))), full((tokens, width)),
                full((tokens, width)), pl.BlockSpec((width, width), lambda j, m: (0, clip(j))),
                full((images, half, width)), full((images, half, width)), full((tokens, width)), full((1, width)),
            ],
            out_specs=[
                halves, halves, full((images, half, width)), full((images, half, width)),
                full((1, width)), full((1, width)),
            ],
            scratch_shapes=[pltpu.VMEM((width, width), F32), pltpu.VMEM((tokens, width), F32)],
        ),
        out_shape=[
            jax.ShapeDtypeStruct((runs, 2, 2 * unit, 2 * width), BF16),
            jax.ShapeDtypeStruct((runs, 2, 2 * unit, 2 * width), BF16),
            jax.ShapeDtypeStruct((images, half, width), F32),
            jax.ShapeDtypeStruct((images, half, width), BF16),
            jax.ShapeDtypeStruct((1, width), F32),
            jax.ShapeDtypeStruct((1, width), F32),
        ],
        compiler_params=pltpu.CompilerParams(vmem_limit_bytes=56 * MIB),
        cost_estimate=pl.CostEstimate(flops=14 * tokens * width * width, transcendentals=0, bytes_accessed=35_000_000),
        name="tail",
    )(mine, n1, d_join, attended, d_branch, w["qkv_weight"], own, oth, d_middle, w["ln1_gain"])


MESH = pl.DeviceIdType.MESH
DEPTH, LEVELS = 4, 2
PARTS = 6
GROUP = 32


def reduce_kernel(
    s2_ref, k2_ref, s1_ref, k1_ref, st_ref, kt_ref, small_ref,
    fc2_ref, fc1_ref, qkv_ref, proj_ref, tiny_ref,
    keep_ref, rc_ref, ra_ref, rb_ref, rz_ref, keep_t, rc_t, ra_t, rb_t, rz_t, load_sem, send_sem, recv_sem,
):
    line = lax.axis_index("img")
    x = lax.axis_index("seq")
    core = line % 2
    y = (line // 2) % 2
    z = line // 4
    sibling = (line + 1 - 2 * core, x)
    level = (line + 2 - 4 * y, x)
    across = (line, 1 - x)
    deep = [(((z + d) % DEPTH) * 4 + y * 2 + core, x) for d in range(1, DEPTH)]
    peers = [sibling, level, across] + deep
    barrier = pltpu.get_barrier_semaphore()
    for peer in peers:
        pl.semaphore_signal(barrier, inc=1, device_id=peer, device_id_type=MESH)
    pl.semaphore_wait(barrier, len(peers))

    rows, cols = keep_ref.shape[-2], keep_ref.shape[-1]
    pick = []
    for k in range(2):
        pick.append((s2_ref.at[:, :, :, pl.ds(k * rows, rows), :], k2_ref.at[:, :, :, pl.ds(k * rows, rows), :]))
    for s_ref, k_ref in ((s1_ref, k1_ref), (st_ref, kt_ref)):
        for k in range(2):
            pick.append((s_ref.at[:, :, :, :, pl.ds(k * cols, cols)], k_ref.at[:, :, :, :, pl.ds(k * cols, cols)]))

    def far(src, dst, part, slot, peer):
        copy = pltpu.make_async_remote_copy(
            src_ref=src, dst_ref=dst, send_sem=send_sem.at[part, slot], recv_sem=recv_sem.at[part, slot],
            device_id=peer, device_id_type=MESH,
        )
        copy.start()
        return copy

    pending = {}
    loads = []
    for part, (send, keep) in enumerate(pick):
        pending[part] = far(send, rc_ref.at[part], part, 0, sibling)
        load = pltpu.make_async_copy(keep, keep_ref.at[part], load_sem.at[part])
        load.start()
        loads.append(load)
    keep_t[...] = small_ref[:, :, pl.ds(core, 1)].reshape(keep_t.shape)
    pending[PARTS] = far(small_ref.at[:, :, 1 - core], rc_t, PARTS, 0, sibling)

    def add(target, source):
        target[...] = (target[...].astype(F32) + source[...].astype(F32)).astype(target.dtype)

    def stage_one(part, kept, rc, ra, first_level):
        pending[part].wait()
        if part < PARTS:
            loads[part].wait()

        @pl.loop(0, DEPTH * 2)
        def _(i):
            a, b = i // 2, i % 2
            for c in range(2):
                add(kept.at[a, b, c], rc.at[a, b, c])

        src = kept.at[:, 1 - y] if first_level else kept.at[:, :, 1 - x]
        pending[part] = far(src, ra, part, 1, level if first_level else across)

    def stage_two(part, kept, ra, rb, first_level):
        pending[part].wait()

        @pl.loop(0, DEPTH * 2)
        def _(i):
            a, b = i // 2, i % 2
            add(kept.at[a, y, b] if first_level else kept.at[a, b, x], ra.at[a, b])

        src = kept.at[:, y, 1 - x] if first_level else kept.at[:, 1 - y, x]
        pending[part] = far(src, rb, part, 2, across if first_level else level)

    def stage_three(part, kept, rb, rz):
        pending[part].wait()

        @pl.loop(0, DEPTH)
        def _(a):
            add(kept.at[a, y, x], rb.at[a])

        pending[part] = [
            far(kept.at[(z + d) % DEPTH, y, x], rz.at[d - 1], part, 2 + d, deep[d - 1]) for d in range(1, DEPTH)
        ]

    def stage_four(part, kept, rz):
        for copy in pending[part]:
            copy.wait()
        total = kept[z, y, x].astype(F32)
        for d in range(DEPTH - 1):
            total += rz[d].astype(F32)
        return total

    for part in range(PARTS):
        stage_one(part, keep_ref.at[part], rc_ref.at[part], ra_ref.at[part], part % 2 == 0)
    stage_one(PARTS, keep_t, rc_t, ra_t, True)
    for part in range(PARTS):
        stage_two(part, keep_ref.at[part], ra_ref.at[part], rb_ref.at[part], part % 2 == 0)
    stage_two(PARTS, keep_t, ra_t, rb_t, True)
    for part in range(PARTS):
        stage_three(part, keep_ref.at[part], rb_ref.at[part], rz_ref.at[part])
    stage_three(PARTS, keep_t, rb_t, rz_t)
    unit, side = rows // 2, cols // 2
    for part in range(PARTS):
        total = stage_four(part, keep_ref.at[part], rz_ref.at[part])
        if part < 2:
            fc2_ref[part * rows : part * rows + rows, :] = total
            continue
        for t in range(2):
            for h in range(2):
                piece = total[h * unit : h * unit + unit, t * side : t * side + side]
                at = ((part % 2) * 2 + t) * cols + h * side
                if part < 4:
                    fc1_ref[:, at : at + side] = piece
                elif at < 3 * cols:
                    qkv_ref[:, at : at + side] = piece
                else:
                    proj_ref[:, at - 3 * cols : at - 3 * cols + side] = piece
    tiny_ref[...] = stage_four(PARTS, keep_t, rz_t)


def reduce_all(s2, k2, s1, k1, st, kt, small):
    rows, cols = s1.shape[-2], s1.shape[-1] // 2
    unit = rows // 2
    s2, k2 = s2.reshape(DEPTH, 2, 2, 2 * rows, cols), k2.reshape(DEPTH, 2, 2, 2 * rows, cols)
    s1, k1, st, kt = (v.reshape(DEPTH, 2, 2, rows, 2 * cols) for v in (s1, k1, st, kt))
    small = small.reshape(DEPTH, 2, 2, 2, 8, 128)
    hbm = pl.BlockSpec(memory_space=pl.ANY)
    vmem = pl.BlockSpec(memory_space=pltpu.VMEM)
    return pl.pallas_call(
        reduce_kernel,
        in_specs=[hbm] * 6 + [vmem],
        out_specs=[vmem] * 5,
        out_shape=[
            jax.ShapeDtypeStruct((2 * rows, cols), F32),
            jax.ShapeDtypeStruct((unit, 4 * cols), F32),
            jax.ShapeDtypeStruct((unit, 3 * cols), F32),
            jax.ShapeDtypeStruct((unit, cols), F32),
            jax.ShapeDtypeStruct((8, 128), F32),
        ],
        scratch_shapes=[
            pltpu.VMEM((PARTS, DEPTH, 2, 2, rows, cols), BF16),
            pltpu.VMEM((PARTS, DEPTH, 2, 2, rows, cols), BF16),
            pltpu.VMEM((PARTS, DEPTH, 2, rows, cols), BF16),
            pltpu.VMEM((PARTS, DEPTH, rows, cols), BF16),
            pltpu.VMEM((PARTS, DEPTH - 1, rows, cols), BF16),
            pltpu.VMEM((DEPTH, 2, 2, 8, 128), F32),
            pltpu.VMEM((DEPTH, 2, 2, 8, 128), F32),
            pltpu.VMEM((DEPTH, 2, 8, 128), F32),
            pltpu.VMEM((DEPTH, 8, 128), F32),
            pltpu.VMEM((DEPTH - 1, 8, 128), F32),
            pltpu.SemaphoreType.DMA((PARTS,)),
            pltpu.SemaphoreType.DMA((PARTS + 1, 6)),
            pltpu.SemaphoreType.DMA((PARTS + 1, 6)),
        ],
        compiler_params=pltpu.CompilerParams(collective_id=0, has_side_effects=True, vmem_limit_bytes=48 * MIB),
        name="reduce",
    )(s2, k2, s1, k1, st, kt, small)


def spread(value):
    return lax.psum_scatter(value, ("img", "seq"), scatter_dimension=0, tiled=True)


def unfold(send, keep, core, folds):
    rows, cols = send.shape[-2], send.shape[-1]
    send, keep = (v.reshape(GROUP // 4, 2, rows, cols) for v in (send, keep))
    both = jnp.stack([jnp.where(core == 0, keep, send), jnp.where(core == 0, send, keep)], axis=1).astype(F32)
    if folds == 1:
        return both.reshape(GROUP * rows, cols)
    tiles = 4
    both = both.reshape(GROUP, 2, rows // 2, tiles, cols // tiles)
    return both.transpose(0, 2, 3, 1, 4).reshape(GROUP * rows // 2, 2 * cols)


def swap(value, axis, bit, size):
    return lax.ppermute(value, axis, [(i, i ^ bit) for i in range(size)])


def shards(img_size, args):
    (patches, grid_shape, split_rows, owner_shard, drop_masks, ln1_gain, ln1_bias, qkv_weight, qv_bias, proj_weight,
     proj_bias, ln2_gain, ln2_bias, fc1_weight, fc1_bias, fc2_weight, fc2_bias, cotangent) = args
    all_images, _, half, width = patches.shape
    images = all_images // 2
    rows = 2 * half
    tokens = images * rows
    side = lax.axis_index("seq")
    line = lax.axis_index("img")
    owners = 2 * img_size
    row = lambda v: v.reshape(1, -1)
    w = dict(
        ln1_gain=row(ln1_gain), ln1_bias=row(ln1_bias), qkv_weight=qkv_weight, q_bias=row(qv_bias[:width]),
        v_bias=row(qv_bias[width:]), proj_weight=proj_weight, proj_bias=row(proj_bias), ln2_gain=row(ln2_gain),
        ln2_bias=row(ln2_bias), fc1_weight=fc1_weight, fc1_bias=row(fc1_bias), fc2_weight=fc2_weight, fc2_bias=row(fc2_bias),
    )

    def exchange(value):
        value = value.reshape(all_images, half, width)
        own = lax.dynamic_slice_in_dim(value, side * images, images, axis=0)
        away = lax.dynamic_slice_in_dim(value, (1 - side) * images, images, axis=0)
        return own, swap(away, "seq", 1, 2)

    def restore(own, oth):
        back = swap(oth, "seq", 1, 2).astype(own.dtype)
        first = jnp.where(side == 0, own, back)
        second = jnp.where(side == 0, back, own)
        return jnp.concatenate([first, second], axis=0).reshape(all_images, 1, half, width)

    x_own, x_oth = exchange(patches)
    c_own, c_oth = exchange(cotangent)
    across = grid_shape[:, 1]
    counts = jnp.stack([split_rows * across, (grid_shape[:, 0] - split_rows) * across], axis=0)
    count_own = jnp.where(side == 0, counts[0], counts[1])
    count_oth = jnp.where(side == 0, counts[1], counts[0])
    special = (owner_shard == side).astype(jnp.int32)
    table = jnp.stack([count_own, special, count_oth, 1 - special, drop_masks[:, 0], drop_masks[:, 1]], axis=1)
    scal = lax.dynamic_slice_in_dim(table, side * images, images, axis=0)

    n1, qkv, probs, attended, middle, n2 = front(scal, x_own, x_oth, w)
    flat = lambda v: v.reshape(tokens, v.shape[-1])
    hidden, slope, out_own, out_oth = mlp(scal, flat(n2), flat(middle), w, images, 512)
    layer_out = restore(out_own, out_oth)

    mine = lax.rem(line, 2).reshape(1)
    unit1 = width // GROUP
    unit2 = fc2_weight.shape[0] // GROUP
    dn2, s2, k2, s1, k1, fc2_bias_grad, fc1_bias_grad = mlp_back(
        scal, mine, c_own, c_oth, flat(n2), hidden, slope, w, unit1, unit2
    )
    d_middle, d_branch, d_join, ln2_gain_grad, ln2_bias_grad, proj_bias_grad, q_grad, v_grad = attend_back(
        scal, c_own, c_oth, dn2.reshape(images, rows, width), middle, qkv, probs, w
    )
    st, kt, grad_own, grad_oth, ln1_gain_grad, ln1_bias_grad = tail(
        mine, flat(n1), flat(d_join), flat(attended), flat(d_branch), x_own, x_oth, flat(d_middle), w, unit1
    )
    patches_grad = restore(grad_own, grad_oth)
    vectors = (
        ln1_gain_grad, ln1_bias_grad, jnp.concatenate([q_grad, v_grad], axis=1), proj_bias_grad, ln2_gain_grad,
        ln2_bias_grad, fc1_bias_grad, fc2_bias_grad,
    )
    if owners == GROUP:
        small = jnp.concatenate([v.reshape(owners, -1) for v in vectors], axis=1)
        small = jnp.pad(small, ((0, 0), (0, 1024 - small.shape[1]))).reshape(owners, 8, 128)
        fc2_grad, fc1_grad, qkv_grad, proj_grad, small = reduce_all(s2, k2, s1, k1, st, kt, small)
        small = small.reshape(-1)
        pieces = []
        at = 0
        for v in vectors:
            pieces.append(small[at : at + v.shape[1] // owners])
            at += v.shape[1] // owners
    else:
        fc2_grad = spread(unfold(s2, k2, line % 2, 1))
        fc1_grad = spread(unfold(s1, k1, line % 2, 2))
        tail_grad = spread(unfold(st, kt, line % 2, 2))
        qkv_grad, proj_grad = tail_grad[:, : 3 * width], tail_grad[:, 3 * width :]
        pieces = [spread(v.reshape(-1)) for v in vectors]
    l1g, l1b, qvb, pjb, l2g, l2b, f1b, f2b = pieces
    return (
        layer_out, patches_grad, l1g, l1b, qkv_grad, qvb, proj_grad, pjb, l2g, l2b, fc1_grad, f1b, fc2_grad, f2b,
    )


def solution(mesh):
    rep = [P()] * 12
    vec = P(("img", "seq"))
    mat = P(("img", "seq"), None)
    rows = P("img", "seq", None, None)

    def run(*args):
        return shards(mesh.shape["img"], args)

    return jax.shard_map(
        run,
        mesh=mesh,
        in_specs=(rows, P("img", None), P("img"), P("img"), P("img", None), *rep, rows),
        out_specs=(rows, rows, vec, vec, mat, vec, mat, vec, vec, vec, mat, vec, mat, vec),
        check_vma=False,
    )
```

```python
import functools

import jax
import jax.numpy as jnp
from jax import lax
from jax.experimental import pallas as pl
from jax.experimental.pallas import tpu as pltpu
from jax.sharding import PartitionSpec as P

HEAD_DIM = 64
LN_EPS = 1e-06
KEEP_SCALE = 1.0 / 0.9
MASK_FILL = -1e30
BF16 = jnp.bfloat16
F32 = jnp.float32
MIB = 1024 * 1024


def dot_nn(a, b):
    return lax.dot_general(a, b, (((1,), (0,)), ((), ())), preferred_element_type=F32)


def dot_nt(a, b):
    return lax.dot_general(a, b, (((1,), (1,)), ((), ())), preferred_element_type=F32)


def dot_tn(a, b):
    return lax.dot_general(a, b, (((0,), (0,)), ((), ())), preferred_element_type=F32)


def norm_parts(values):
    row_mean = jnp.mean(values, axis=-1, keepdims=True)
    centred = values - row_mean
    variance = jnp.mean(centred * centred, axis=-1, keepdims=True)
    rstd = lax.rsqrt(variance + LN_EPS)
    return centred * rstd, rstd


def norm_back(d_normed, gain, unit, rstd):
    d_unit = d_normed * gain
    mean_one = jnp.mean(d_unit, axis=-1, keepdims=True)
    mean_two = jnp.mean(d_unit * unit, axis=-1, keepdims=True)
    return rstd * (d_unit - mean_one - unit * mean_two)


def gelu_both(values):
    size = jnp.abs(values)
    t = 1.0 / (1.0 + 0.23164189 * size)
    bell = jnp.exp(-0.5 * values * values)
    poly = t * (
        0.127414796
        + t * (-0.142248368 + t * (0.7107068705 + t * (-0.7265760135 + t * 0.5307027145)))
    )
    tail = poly * bell
    cdf = jnp.where(values >= 0.0, 1.0 - tail, tail)
    return values * cdf, cdf + values * (0.3989422804014327 * bell)


def row_valid(scal_ref, image, rows, half, axis):
    shape = (rows, 1) if axis == 0 else (1, rows)
    slot = lax.broadcasted_iota(jnp.int32, shape, axis)
    other = slot >= half
    place = jnp.where(other, slot - half, slot)
    count = jnp.where(other, scal_ref[image, 2], scal_ref[image, 0])
    special = jnp.where(other, scal_ref[image, 3], scal_ref[image, 1])
    return jnp.where(place < 2, special, (place - 2 < count).astype(jnp.int32)) > 0


def front_kernel(
    scal_ref, own_ref, oth_ref, g1_ref, b1_ref, wqkv_ref, qb_ref, vb_ref, wp_ref, pb_ref, g2_ref, b2_ref,
    n1_ref, qkv_ref, probs_ref, att_ref, mid_ref, n2_ref,
):
    image = pl.program_id(0)
    half, width = own_ref.shape[1], own_ref.shape[2]
    rows = 2 * half
    x = jnp.concatenate([own_ref[0].astype(F32), oth_ref[0].astype(F32)], axis=0)
    unit, _ = norm_parts(x)
    n1 = (unit * g1_ref[...] + b1_ref[...]).astype(BF16)
    n1_ref[0] = n1
    qkv_ref[0, :, :width] = ((dot_nn(n1, wqkv_ref[:, :width]) + qb_ref[...]).astype(BF16) * BF16(HEAD_DIM**-0.5))
    qkv_ref[0, :, width : 2 * width] = dot_nn(n1, wqkv_ref[:, width : 2 * width]).astype(BF16)
    qkv_ref[0, :, 2 * width :] = (dot_nn(n1, wqkv_ref[:, 2 * width :]) + vb_ref[...]).astype(BF16)
    fill = jnp.where(row_valid(scal_ref, image, rows, half, 1), 0.0, MASK_FILL)
    low_lane = lax.broadcasted_iota(jnp.int32, (rows, 128), 1) < HEAD_DIM
    for pair in range(width // 128):
        cut = slice(128 * pair, 128 * pair + 128)
        q2 = qkv_ref[0, :, cut]
        k2 = qkv_ref[0, :, width + 128 * pair : width + 128 * pair + 128]
        v2 = qkv_ref[0, :, 2 * width + 128 * pair : 2 * width + 128 * pair + 128]
        total = None
        for side in range(2):
            mine = low_lane if side == 0 else jnp.logical_not(low_lane)
            scores = dot_nt(jnp.where(mine, q2, 0), k2) + fill
            top = jnp.max(scores, axis=-1, keepdims=True)
            weight = jnp.exp(scores - top)
            probs = (weight * (1.0 / jnp.sum(weight, axis=-1, keepdims=True))).astype(BF16)
            probs_ref[0, 2 * pair + side] = probs
            part = dot_nn(probs, jnp.where(mine, v2, 0))
            total = part if total is None else total + part
        att_ref[0, :, cut] = total.astype(BF16)
    keep = scal_ref[image, 4].astype(F32) * KEEP_SCALE
    branch = dot_nn(att_ref[0], wp_ref[...]) + pb_ref[...]
    middle = jnp.concatenate([own_ref[0].astype(F32), oth_ref[0].astype(F32)], axis=0) + keep * branch
    mid_ref[0] = middle
    unit, _ = norm_parts(middle)
    n2_ref[0] = (unit * g2_ref[...] + b2_ref[...]).astype(BF16)


def full(shape):
    zeros = (0,) * len(shape)
    return pl.BlockSpec(shape, lambda *_: zeros, pipeline_mode=pl.Buffered(1))


def front(scal, own, oth, w):
    images, half, width = own.shape
    rows = 2 * half
    heads = width // HEAD_DIM
    per = lambda *tail: pl.BlockSpec((1,) + tail, lambda i, s: (i,) + (0,) * len(tail))
    flops = 2 * images * rows * width * (4 * width + 4 * rows)
    return pl.pallas_call(
        front_kernel,
        grid_spec=pltpu.PrefetchScalarGridSpec(
            num_scalar_prefetch=1,
            grid=(images,),
            in_specs=[
                per(half, width), per(half, width), full((1, width)), full((1, width)),
                full((width, 3 * width)), full((1, width)), full((1, width)),
                full((width, width)), full((1, width)), full((1, width)), full((1, width)),
            ],
            out_specs=[
                per(rows, width), per(rows, 3 * width), per(heads, rows, rows),
                per(rows, width), per(rows, width), per(rows, width),
            ],
        ),
        out_shape=[
            jax.ShapeDtypeStruct((images, rows, width), BF16),
            jax.ShapeDtypeStruct((images, rows, 3 * width), BF16),
            jax.ShapeDtypeStruct((images, heads, rows, rows), BF16),
            jax.ShapeDtypeStruct((images, rows, width), BF16),
            jax.ShapeDtypeStruct((images, rows, width), F32),
            jax.ShapeDtypeStruct((images, rows, width), BF16),
        ],
        compiler_params=pltpu.CompilerParams(vmem_limit_bytes=56 * MIB),
        cost_estimate=pl.CostEstimate(flops=flops, transcendentals=images * heads * rows * rows, bytes_accessed=30_000_000),
        name="front",
    )(scal, own, oth, w["ln1_gain"], w["ln1_bias"], w["qkv_weight"], w["q_bias"], w["v_bias"],
      w["proj_weight"], w["proj_bias"], w["ln2_gain"], w["ln2_bias"])


def mlp_kernel(
    scal_ref, n2_ref, mid_ref, w1_ref, c1_ref, w2_ref, c2_ref,
    hid_ref, slope_ref, own_ref, oth_ref, acc_ref,
):
    step = pl.program_id(0)
    images, half, width = own_ref.shape
    rows = 2 * half
    hidden, slope = gelu_both(dot_nn(n2_ref[...], w1_ref[...]) + c1_ref[...])
    hidden = hidden.astype(BF16)
    hid_ref[...] = hidden
    slope_ref[...] = slope.astype(BF16)
    part = dot_nn(hidden, w2_ref[...])

    @pl.when(step == 0)
    def _():
        acc_ref[...] = part

    @pl.when(step > 0)
    def _():
        acc_ref[...] += part

    @pl.when(step == pl.num_programs(0) - 1)
    def _():
        for image in range(images):
            keep = scal_ref[image, 5].astype(F32) * KEEP_SCALE
            cut = slice(rows * image, rows * image + rows)
            final = mid_ref[cut, :] + keep * (acc_ref[cut, :] + c2_ref[...])
            out = jnp.where(row_valid(scal_ref, image, rows, half, 0), final, 0.0).astype(BF16)
            own_ref[image] = out[:half]
            oth_ref[image] = out[half:]


def mlp(scal, n2, middle, w, images, tile):
    tokens, width = n2.shape
    hidden_width = w["fc1_weight"].shape[1]
    half = tokens // images // 2
    return pl.pallas_call(
        mlp_kernel,
        grid_spec=pltpu.PrefetchScalarGridSpec(
            num_scalar_prefetch=1,
            grid=(hidden_width // tile,),
            in_specs=[
                full((tokens, width)), full((tokens, width)),
                pl.BlockSpec((width, tile), lambda j, s: (0, j)), pl.BlockSpec((1, tile), lambda j, s: (0, j)),
                pl.BlockSpec((tile, width), lambda j, s: (j, 0)), full((1, width)),
            ],
            out_specs=[
                pl.BlockSpec((tokens, tile), lambda j, s: (0, j)), pl.BlockSpec((tokens, tile), lambda j, s: (0, j)),
                full((images, half, width)), full((images, half, width)),
            ],
            scratch_shapes=[pltpu.VMEM((tokens, width), F32)],
        ),
        out_shape=[
            jax.ShapeDtypeStruct((tokens, hidden_width), BF16),
            jax.ShapeDtypeStruct((tokens, hidden_width), BF16),
            jax.ShapeDtypeStruct((images, half, width), BF16),
            jax.ShapeDtypeStruct((images, half, width), BF16),
        ],
        compiler_params=pltpu.CompilerParams(vmem_limit_bytes=56 * MIB),
        cost_estimate=pl.CostEstimate(flops=4 * tokens * width * hidden_width, transcendentals=2 * tokens * hidden_width, bytes_accessed=30_000_000),
        name="mlp",
    )(scal, n2, middle, w["fc1_weight"], w["fc1_bias"], w["fc2_weight"], w["fc2_bias"])


def put_rows(grad_ref, value, send_ref, keep_ref, mine, lead):
    grad_ref[...] = value
    run = 2 * send_ref.shape[-2]
    for k in range(grad_ref.shape[0] // (2 * run)):
        for ref, core in ((send_ref, 1 - mine), (keep_ref, mine)):
            for x in range(2):
                at = pl.multiple_of((2 * k + core) * run + x * (run // 2), 8)
                ref[lead + (k, x)] = grad_ref[pl.ds(at, run // 2), :].astype(BF16)


def put_folded(grad_ref, value, send_ref, keep_ref, mine):
    grad_ref[...] = value
    unit = send_ref.shape[-2] // 2
    side = grad_ref.shape[1] // 2
    for k in range(grad_ref.shape[0] // (4 * unit)):
        for ref, core in ((send_ref, 1 - mine), (keep_ref, mine)):
            for x in range(2):
                at = pl.multiple_of((4 * k + 2 * core + x) * unit, 8)
                piece = grad_ref[pl.ds(at, unit), :]
                ref[k, x] = jnp.concatenate([piece[:, :side], piece[:, side:]], axis=0).astype(BF16)


def mlp_back_kernel(
    scal_ref, mine_ref, own_ref, oth_ref, n2_ref, hid_ref, slope_ref, w1_ref, w2_ref,
    dn2_ref, s2_ref, k2_ref, s1_ref, k1_ref, c2_ref, c1_ref, dmlp_ref, grad_ref, acc_ref,
):
    step = pl.program_id(0)
    images, half, width = own_ref.shape
    rows = 2 * half
    mine = mine_ref[0]

    @pl.when(step == 0)
    def _():
        total = jnp.zeros((1, width), F32)
        for image in range(images):
            keep = scal_ref[image, 5].astype(F32) * KEEP_SCALE
            cot = jnp.concatenate([own_ref[image].astype(F32), oth_ref[image].astype(F32)], axis=0)
            live = row_valid(scal_ref, image, rows, half, 0)
            d_mlp = (jnp.where(live, cot, 0.0) * keep).astype(BF16)
            dmlp_ref[rows * image : rows * image + rows, :] = d_mlp
            total += jnp.sum(d_mlp.astype(F32), axis=0, keepdims=True)
        c2_ref[...] = total

    d_pre = slope_ref[...].astype(F32) * dot_nt(dmlp_ref[...], w2_ref[...])
    d_pre = d_pre.astype(BF16)
    c1_ref[...] = jnp.sum(d_pre.astype(F32), axis=0, keepdims=True)
    part = dot_nt(d_pre, w1_ref[...])
    put_folded(grad_ref, dot_tn(n2_ref[...], d_pre), s1_ref, k1_ref, mine)
    put_rows(grad_ref, dot_tn(hid_ref[...], dmlp_ref[...]), s2_ref, k2_ref, mine, (0,))

    @pl.when(step == 0)
    def _():
        acc_ref[...] = part

    @pl.when(step > 0)
    def _():
        acc_ref[...] += part

    @pl.when(step == pl.num_programs(0) - 1)
    def _():
        dn2_ref[...] = acc_ref[...]


def mlp_back(scal, mine, own, oth, n2, hidden, slope, w, unit1, unit2):
    tokens, width = n2.shape
    images, half, _ = own.shape
    hidden_width = hidden.shape[1]
    tile = width
    steps = hidden_width // tile
    runs1, runs2 = width // (4 * unit1), tile // (4 * unit2)
    col = pl.BlockSpec((tokens, tile), lambda j, s, m: (0, j))
    half1 = pl.BlockSpec((runs1, 2, 2 * unit1, tile // 2), lambda j, s, m: (0, 0, 0, j))
    half2 = pl.BlockSpec((1, runs2, 2, unit2, width), lambda j, s, m: (j, 0, 0, 0, 0))
    return pl.pallas_call(
        mlp_back_kernel,
        grid_spec=pltpu.PrefetchScalarGridSpec(
            num_scalar_prefetch=2,
            grid=(steps,),
            in_specs=[
                full((images, half, width)), full((images, half, width)), full((tokens, width)), col, col,
                pl.BlockSpec((width, tile), lambda j, s, m: (0, j)), pl.BlockSpec((tile, width), lambda j, s, m: (j, 0)),
            ],
            out_specs=[
                full((tokens, width)), half2, half2, half1, half1,
                full((1, width)), pl.BlockSpec((1, tile), lambda j, s, m: (0, j)),
            ],
            scratch_shapes=[
                pltpu.VMEM((tokens, width), BF16), pltpu.VMEM((width, width), F32), pltpu.VMEM((tokens, width), F32),
            ],
        ),
        out_shape=[
            jax.ShapeDtypeStruct((tokens, width), F32),
            jax.ShapeDtypeStruct((steps, runs2, 2, unit2, width), BF16),
            jax.ShapeDtypeStruct((steps, runs2, 2, unit2, width), BF16),
            jax.ShapeDtypeStruct((runs1, 2, 2 * unit1, hidden_width // 2), BF16),
            jax.ShapeDtypeStruct((runs1, 2, 2 * unit1, hidden_width // 2), BF16),
            jax.ShapeDtypeStruct((1, width), F32),
            jax.ShapeDtypeStruct((1, hidden_width), F32),
        ],
        compiler_params=pltpu.CompilerParams(vmem_limit_bytes=58 * MIB),
        cost_estimate=pl.CostEstimate(flops=8 * tokens * width * hidden_width, transcendentals=0, bytes_accessed=35_000_000),
        name="mlp_back",
    )(scal, mine, own, oth, n2, hidden, slope, w["fc1_weight"], w["fc2_weight"])


def attend_back_kernel(
    scal_ref, own_ref, oth_ref, dn2_ref, mid_ref, qkv_ref, probs_ref, wp_ref, g2_ref,
    dmid_ref, dbr_ref, djoin_ref, g2g_ref, g2b_ref, pbg_ref, qbg_ref, vbg_ref, datt_ref,
):
    image = pl.program_id(0)
    half, width = own_ref.shape[1], own_ref.shape[2]
    rows = 2 * half
    live = row_valid(scal_ref, image, rows, half, 0)
    d_final = jnp.where(live, jnp.concatenate([own_ref[0].astype(F32), oth_ref[0].astype(F32)], axis=0), 0.0)
    unit, rstd = norm_parts(mid_ref[0])
    dn2 = dn2_ref[0]
    gain_part = jnp.sum(dn2 * unit, axis=0, keepdims=True)
    bias_part = jnp.sum(dn2, axis=0, keepdims=True)
    d_middle = d_final + norm_back(dn2, g2_ref[...], unit, rstd)
    dmid_ref[0] = d_middle
    keep = scal_ref[image, 4].astype(F32) * KEEP_SCALE
    d_branch = (d_middle * keep).astype(BF16)
    dbr_ref[0] = d_branch
    proj_part = jnp.sum(d_branch.astype(F32), axis=0, keepdims=True)
    datt_ref[...] = dot_nt(d_branch, wp_ref[...]).astype(BF16)
    low_lane = lax.broadcasted_iota(jnp.int32, (rows, 128), 1) < HEAD_DIM
    for pair in range(width // 128):
        cut = slice(128 * pair, 128 * pair + 128)
        q2 = qkv_ref[0, :, cut]
        k2 = qkv_ref[0, :, width + 128 * pair : width + 128 * pair + 128]
        v2 = qkv_ref[0, :, 2 * width + 128 * pair : 2 * width + 128 * pair + 128]
        a2 = datt_ref[:, cut]
        dq = dk = dv = None
        for side in range(2):
            mine = low_lane if side == 0 else jnp.logical_not(low_lane)
            probs_low = probs_ref[0, 2 * pair + side]
            probs = probs_low.astype(F32)
            a_side = jnp.where(mine, a2, 0)
            d_probs = dot_nt(a_side, v2)
            inner = jnp.sum(probs * d_probs, axis=-1, keepdims=True)
            d_scores = (probs * (d_probs - inner)).astype(BF16)
            dq_part = dot_nn(d_scores, jnp.where(mine, k2, 0))
            dk_part = dot_tn(d_scores, jnp.where(mine, q2, 0))
            dv_part = dot_tn(probs_low, a_side)
            dq = dq_part if dq is None else dq + dq_part
            dk = dk_part if dk is None else dk + dk_part
            dv = dv_part if dv is None else dv + dv_part
        djoin_ref[0, :, cut] = (dq * HEAD_DIM**-0.5).astype(BF16)
        djoin_ref[0, :, width + 128 * pair : width + 128 * pair + 128] = dk.astype(BF16)
        djoin_ref[0, :, 2 * width + 128 * pair : 2 * width + 128 * pair + 128] = dv.astype(BF16)
    q_part = jnp.sum(djoin_ref[0, :, :width].astype(F32), axis=0, keepdims=True)
    v_part = jnp.sum(djoin_ref[0, :, 2 * width :].astype(F32), axis=0, keepdims=True)
    sums = ((g2g_ref, gain_part), (g2b_ref, bias_part), (pbg_ref, proj_part), (qbg_ref, q_part), (vbg_ref, v_part))

    @pl.when(image == 0)
    def _():
        for ref, part in sums:
            ref[...] = part

    @pl.when(image > 0)
    def _():
        for ref, part in sums:
            ref[...] += part


def attend_back(scal, own, oth, dn2, middle, qkv, probs, w):
    images, half, width = own.shape
    rows = 2 * half
    heads = width // HEAD_DIM
    per = lambda *tail: pl.BlockSpec((1,) + tail, lambda i, s: (i,) + (0,) * len(tail))
    vec = jax.ShapeDtypeStruct((1, width), F32)
    return pl.pallas_call(
        attend_back_kernel,
        grid_spec=pltpu.PrefetchScalarGridSpec(
            num_scalar_prefetch=1,
            grid=(images,),
            in_specs=[
                per(half, width), per(half, width), per(rows, width), per(rows, width), per(rows, 3 * width),
                per(heads, rows, rows), full((width, width)), full((1, width)),
            ],
            out_specs=[per(rows, width), per(rows, width), per(rows, 3 * width)] + [full((1, width))] * 5,
            scratch_shapes=[pltpu.VMEM((rows, width), BF16)],
        ),
        out_shape=[
            jax.ShapeDtypeStruct((images, rows, width), F32),
            jax.ShapeDtypeStruct((images, rows, width), BF16),
            jax.ShapeDtypeStruct((images, rows, 3 * width), BF16),
            vec, vec, vec, vec, vec,
        ],
        compiler_params=pltpu.CompilerParams(vmem_limit_bytes=56 * MIB),
        cost_estimate=pl.CostEstimate(flops=2 * images * rows * width * (width + 8 * rows), transcendentals=0, bytes_accessed=35_000_000),
        name="attend_back",
    )(scal, own, oth, dn2, middle, qkv, probs, w["proj_weight"], w["ln2_gain"])


def tail_kernel(
    mine_ref, n1_ref, djoin_ref, att_ref, dbr_ref, wqkv_ref, xo_ref, xt_ref, dmid_ref, g1_ref,
    send_ref, keep_ref, go_ref, gt_ref, g1g_ref, g1b_ref, grad_ref, acc_ref,
):
    step = pl.program_id(0)
    last = pl.num_programs(0) - 1
    images, half, width = xo_ref.shape
    rows = 2 * half
    mine = mine_ref[0]

    @pl.when(step < last)
    def _():
        put_folded(grad_ref, dot_tn(n1_ref[...], djoin_ref[...]), send_ref, keep_ref, mine)
        part = dot_nt(djoin_ref[...], wqkv_ref[...])

        @pl.when(step == 0)
        def _():
            acc_ref[...] = part

        @pl.when(step > 0)
        def _():
            acc_ref[...] += part

    @pl.when(step == last)
    def _():
        put_folded(grad_ref, dot_tn(att_ref[...], dbr_ref[...]), send_ref, keep_ref, mine)
        gain_sum = jnp.zeros((1, width), F32)
        bias_sum = jnp.zeros((1, width), F32)
        for image in range(images):
            x = jnp.concatenate([xo_ref[image].astype(F32), xt_ref[image].astype(F32)], axis=0)
            unit, rstd = norm_parts(x)
            dn1 = acc_ref[rows * image : rows * image + rows, :]
            gain_sum += jnp.sum(dn1 * unit, axis=0, keepdims=True)
            bias_sum += jnp.sum(dn1, axis=0, keepdims=True)
            out = dmid_ref[rows * image : rows * image + rows, :] + norm_back(dn1, g1_ref[...], unit, rstd)
            go_ref[image] = out[:half]
            gt_ref[image] = out[half:].astype(BF16)
        g1g_ref[...] = gain_sum
        g1b_ref[...] = bias_sum


def tail(mine, n1, d_join, attended, d_branch, own, oth, d_middle, w, unit):
    tokens, width = n1.shape
    images, half, _ = own.shape
    runs = width // (4 * unit)
    halves = pl.BlockSpec((runs, 2, 2 * unit, width // 2), lambda j, m: (0, 0, 0, j))
    clip = lambda j: jnp.minimum(j, 2)
    return pl.pallas_call(
        tail_kernel,
        grid_spec=pltpu.PrefetchScalarGridSpec(
            num_scalar_prefetch=1,
            grid=(4,),
            in_specs=[
                full((tokens, width)), pl.BlockSpec((tokens, width), lambda j, m: (0, clip(j))), full((tokens, width)),
                full((tokens, width)), pl.BlockSpec((width, width), lambda j, m: (0, clip(j))),
                full((images, half, width)), full((images, half, width)), full((tokens, width)), full((1, width)),
            ],
            out_specs=[
                halves, halves, full((images, half, width)), full((images, half, width)),
                full((1, width)), full((1, width)),
            ],
            scratch_shapes=[pltpu.VMEM((width, width), F32), pltpu.VMEM((tokens, width), F32)],
        ),
        out_shape=[
            jax.ShapeDtypeStruct((runs, 2, 2 * unit, 2 * width), BF16),
            jax.ShapeDtypeStruct((runs, 2, 2 * unit, 2 * width), BF16),
            jax.ShapeDtypeStruct((images, half, width), F32),
            jax.ShapeDtypeStruct((images, half, width), BF16),
            jax.ShapeDtypeStruct((1, width), F32),
            jax.ShapeDtypeStruct((1, width), F32),
        ],
        compiler_params=pltpu.CompilerParams(vmem_limit_bytes=56 * MIB),
        cost_estimate=pl.CostEstimate(flops=14 * tokens * width * width, transcendentals=0, bytes_accessed=35_000_000),
        name="tail",
    )(mine, n1, d_join, attended, d_branch, w["qkv_weight"], own, oth, d_middle, w["ln1_gain"])


MESH = pl.DeviceIdType.MESH
DEPTH, LEVELS = 4, 2
PARTS = 6
SLOTS = 3
GROUP = 32


class Far:
    def __init__(self, ends, send_sem, recv_sem, peer):
        self.parts = (ends, send_sem, recv_sem, peer)
        self.build().start()

    def build(self):
        ends, send_sem, recv_sem, peer = self.parts
        src, dst = ends()
        return pltpu.make_async_remote_copy(
            src_ref=src, dst_ref=dst, send_sem=send_sem(), recv_sem=recv_sem(), device_id=peer, device_id_type=MESH
        )

    def wait(self):
        self.build().wait()


def finish_kernel(
    scal_ref, cot_own, cot_oth, dn2_hbm, mid_hbm, qkv_hbm, probs_hbm, wp_hbm, wqkv_hbm, n1_hbm, att_hbm, x_own, x_oth,
    s2_ref, k2_ref, s1_ref, k1_ref, g1_ref, g2_ref, c1_ref, c2_ref,
    fc2_ref, fc1_ref, qkvg_ref, projg_ref, vec_ref, grad_ref, back_ref,
    cot, xin, dn2, mid, qkv, probs, wp, wqkv, n1, att, dbr, djoin, datt, tile, gout, gsend, grecv, vec, vget,
    keep, send, rc, ra, rb, rz,
    load_sem, probs_sem, send_sem, recv_sem, side_send, side_recv, vec_send, vec_recv, out_sem, free_sem,
):
    images, rows, width = dn2.shape
    half = rows // 2
    pairs = width // 128
    line = lax.axis_index("img")
    x = lax.axis_index("seq")
    core = line % 2
    y = (line // 2) % 2
    z = line // 4
    sibling = (line + 1 - 2 * core, x)
    level = (line + 2 - 4 * y, x)
    across = (line, 1 - x)
    deep = [(((z + d) % DEPTH) * 4 + y * 2 + core, x) for d in range(1, DEPTH)]
    peers = [sibling, level, across] + deep
    barrier = pltpu.get_barrier_semaphore()
    for peer in peers:
        pl.semaphore_signal(barrier, inc=1, device_id=peer, device_id_type=MESH)

    loads = []

    def fetch(src, dst):
        copy = pltpu.make_async_copy(src, dst, load_sem.at[len(loads)])
        copy.start()
        loads.append(copy)
        return copy

    def probs_copy(index, slot):
        return pltpu.make_async_copy(
            probs_hbm.at[index // pairs, pl.ds(2 * (index % pairs), 2)], probs.at[slot], probs_sem.at[slot]
        )

    first = [fetch(cot_own, cot.at[:, pl.ds(0, half)]), fetch(cot_oth, cot.at[:, pl.ds(half, half)])]
    first += [fetch(mid_hbm, mid), fetch(dn2_hbm, dn2), fetch(wp_hbm, wp), fetch(qkv_hbm, qkv)]
    for slot in range(SLOTS):
        probs_copy(slot, slot).start()
    r, c = keep.shape[-2], keep.shape[-1]
    keep_src = [k2_ref.at[:, :, :, pl.ds(k * r, r), :] for k in range(2)]
    keep_src += [k1_ref.at[:, :, :, :, pl.ds(k * c, c)] for k in range(2)]
    send_src = [s2_ref.at[:, :, :, pl.ds(k * r, r), :] for k in range(2)]
    send_src += [s1_ref.at[:, :, :, :, pl.ds(k * c, c)] for k in range(2)]
    keep_in = [fetch(keep_src[k], keep.at[k]) for k in range(4)]
    late = [fetch(n1_hbm, n1), fetch(att_hbm, att), fetch(wqkv_hbm, wqkv)]
    late += [fetch(x_own, xin.at[:, pl.ds(0, half)]), fetch(x_oth, xin.at[:, pl.ds(half, half)])]
    pl.semaphore_wait(barrier, len(peers))

    def far(ends, part, slot, peer):
        return Far(ends, lambda: send_sem.at[part, slot], lambda: recv_sem.at[part, slot], peer)

    pending = {}
    rc_slot = [0, 1, 2, 3, 0, 1]
    for part in range(4):
        pending[part] = far(lambda part=part: (send_src[part], rc.at[part]), part, 0, sibling)

    def add(target, source):
        target[...] = (target[...].astype(F32) + source[...].astype(F32)).astype(target.dtype)

    def stage_one(part):
        pending[part].wait()
        if part < 4:
            keep_in[part].wait()
        first_level = part % 2 == 0
        kept, arrived = keep.at[part], rc.at[rc_slot[part]]

        @pl.loop(0, DEPTH * 2)
        def _(i):
            p, q = i // 2, i % 2
            for e in range(2):
                add(kept.at[p, q, e], arrived.at[p, q, e])

        if part < 2:
            pl.semaphore_signal(free_sem.at[part], inc=1, device_id=sibling, device_id_type=MESH)
        def ends():
            src = keep.at[part, :, 1 - y] if first_level else keep.at[part, :, :, 1 - x]
            return src, ra.at[part]

        pending[part] = far(ends, part, 1, level if first_level else across)

    def stage_two(part):
        pending[part].wait()
        first_level = part % 2 == 0
        kept, arrived = keep.at[part], ra.at[part]

        @pl.loop(0, DEPTH * 2)
        def _(i):
            p, q = i // 2, i % 2
            add(kept.at[p, y, q] if first_level else kept.at[p, q, x], arrived.at[p, q])

        def ends():
            src = keep.at[part, :, y, 1 - x] if first_level else keep.at[part, :, 1 - y, x]
            return src, rb.at[part]

        pending[part] = far(ends, part, 2, across if first_level else level)

    def stage_three(part):
        pending[part].wait()
        kept, arrived = keep.at[part], rb.at[part]

        @pl.loop(0, DEPTH)
        def _(p):
            add(kept.at[p, y, x], arrived.at[p])

        pending[part] = [
            far(lambda d=d: (keep.at[part, (z + d) % DEPTH, y, x], rz.at[part, d - 1]), part, 2 + d, deep[d - 1])
            for d in range(1, DEPTH)
        ]

    def stage_four(part):
        for copy in pending[part]:
            copy.wait()
        total = keep[part, z, y, x].astype(F32)
        for d in range(DEPTH - 1):
            total += rz[part, d].astype(F32)
        unit, side = r // 2, c // 2
        if part < 2:
            fc2_ref[part * r : part * r + r, :] = total
            return
        for t in range(2):
            for h in range(2):
                piece = total[h * unit : h * unit + unit, t * side : t * side + side]
                at = ((part % 2) * 2 + t) * c + h * side
                if part < 4:
                    fc1_ref[:, at : at + side] = piece
                elif at < 3 * c:
                    qkvg_ref[:, at : at + side] = piece
                else:
                    projg_ref[:, at - 3 * c : at - 3 * c + side] = piece

    vec[...] = jnp.zeros_like(vec)
    for k in range(4):
        vec[7 + k : 8 + k, :] = c1_ref[:, k * width : k * width + width]
    vec[11:12, :] = c2_ref[...]
    for copy in first:
        copy.wait()
    low_lane = lax.broadcasted_iota(jnp.int32, (rows, 128), 1) < HEAD_DIM
    plan = {
        (0, 0): [(stage_one, 0)], (0, 1): [(stage_one, 1)], (0, 2): [(stage_one, 2)], (0, 3): [(stage_one, 3)],
        (2, 0): [(stage_two, 0)], (2, 1): [(stage_two, 1)],
    }
    def image_body(i):
        live = row_valid(scal_ref, i, rows, half, 0)
        d_final = jnp.where(live, cot[i].astype(F32), 0.0)
        unit, rstd = norm_parts(mid[i])
        d_normed = dn2[i]
        vec[5:6, :] += jnp.sum(d_normed * unit, axis=0, keepdims=True)
        vec[6:7, :] += jnp.sum(d_normed, axis=0, keepdims=True)
        d_middle = d_final + norm_back(d_normed, g2_ref[...], unit, rstd)
        dn2[i] = d_middle
        gate = scal_ref[i, 4].astype(F32) * KEEP_SCALE
        d_branch = (d_middle * gate).astype(BF16)
        dbr[i] = d_branch
        vec[4:5, :] += jnp.sum(d_branch.astype(F32), axis=0, keepdims=True)
        datt[...] = dot_nt(d_branch, wp[...]).astype(BF16)
        for pair in range(pairs):
            index = i * pairs + pair
            slot = index % SLOTS
            probs_copy(index, slot).wait()
            cut = slice(128 * pair, 128 * pair + 128)
            k_cut = slice(width + 128 * pair, width + 128 * pair + 128)
            v_cut = slice(2 * width + 128 * pair, 2 * width + 128 * pair + 128)
            q2, k2, v2, a2 = qkv[i, :, cut], qkv[i, :, k_cut], qkv[i, :, v_cut], datt[:, cut]
            dq = dk = dv = None
            for side in range(2):
                mine = low_lane if side == 0 else jnp.logical_not(low_lane)
                low = probs[slot, side]
                high = low.astype(F32)
                a_side = jnp.where(mine, a2, 0)
                d_probs = dot_nt(a_side, v2)
                inner = jnp.sum(high * d_probs, axis=-1, keepdims=True)
                d_scores = (high * (d_probs - inner)).astype(BF16)
                parts = (dot_nn(d_scores, jnp.where(mine, k2, 0)), dot_tn(d_scores, jnp.where(mine, q2, 0)), dot_tn(low, a_side))
                dq, dk, dv = parts if dq is None else (dq + parts[0], dk + parts[1], dv + parts[2])
            djoin[i, :, cut] = (dq * HEAD_DIM**-0.5).astype(BF16)
            djoin[i, :, k_cut] = dk.astype(BF16)
            djoin[i, :, v_cut] = dv.astype(BF16)

            @pl.when(index + SLOTS < images * pairs)
            def _():
                probs_copy(index + SLOTS, slot).start()

            yield pair
        vec[2:3, :] += jnp.sum(djoin[i, :, :width].astype(F32), axis=0, keepdims=True)
        vec[3:4, :] += jnp.sum(djoin[i, :, 2 * width :].astype(F32), axis=0, keepdims=True)

    @pl.loop(0, images)
    def _(i):
        for pair in image_body(i):
            for (image, at), jobs in plan.items():
                if at != pair:
                    continue

                @pl.when(i == image)
                def _():
                    for job, part in jobs:
                        job(part)

    for copy in late:
        copy.wait()
    flat = lambda ref: ref[...].reshape(images * rows, ref.shape[-1])

    def weight_tile(t):
        if t < 3:
            value = dot_tn(flat(n1), djoin[:, :, t * width : t * width + width].reshape(images * rows, width))
        else:
            value = dot_tn(flat(att), flat(dbr))
        tile[...] = value
        part = 4 + t // 2
        unit, side = r // 2, c // 2
        spot = slice((t % 2) * side, (t % 2) * side + side)
        for k in range(DEPTH * 2):
            for ref, who in ((send.at[part - 4], 1 - core), (keep.at[part], core)):
                for e in range(2):
                    at = pl.multiple_of((4 * k + 2 * who + e) * unit, 8)
                    piece = tile[pl.ds(at, unit), :]
                    folded = jnp.concatenate([piece[:, :side], piece[:, side:]], axis=0).astype(BF16)
                    ref[k // 2, k % 2, e, :, spot] = folded

    def start_part(part):
        pl.semaphore_wait(free_sem.at[part - 4], 1)
        pending[part] = far(lambda: (send.at[part - 4], rc.at[rc_slot[part]]), part, 0, sibling)

    weight_tile(3)
    weight_tile(2)
    start_part(5)
    stage_two(2)
    weight_tile(0)
    stage_three(0)
    weight_tile(1)
    start_part(4)
    stage_two(3)
    stage_three(1)

    def input_grad(i):
        unit, rstd = norm_parts(xin[i].astype(F32))
        d_normed = dot_nt(djoin[i], wqkv[...])
        vec[0:1, :] += jnp.sum(d_normed * unit, axis=0, keepdims=True)
        vec[1:2, :] += jnp.sum(d_normed, axis=0, keepdims=True)
        out = dn2[i] + norm_back(d_normed, g1_ref[...], unit, rstd)
        gout[i] = out[:half]
        gsend[i] = out[half:].astype(BF16)

    moves = []
    swaps = []
    for i in range(images):
        input_grad(i)
        swaps.append(
            Far(lambda i=i: (gsend.at[i], grecv.at[i]), lambda i=i: side_send.at[i], lambda i=i: side_recv.at[i], across)
        )
        if i == 0:
            stage_one(5)
        if i == 1:
            stage_one(4)
            stage_three(2)
    local = pltpu.make_async_copy(gout, grad_ref, out_sem.at[0])
    local.start()
    stage_three(3)

    def exchange(k, peer):
        return Far(lambda: (vec, vget.at[k]), lambda: vec_send.at[k], lambda: vec_recv.at[k], peer)

    for k, peer in enumerate((sibling, level, across)):
        exchange(k, peer).wait()
        vec[...] += vget[k]
        if k == 0:
            stage_two(5)
        if k == 1:
            stage_two(4)
    rest = [exchange(2 + d, deep[d - 1]) for d in range(1, DEPTH)]
    stage_four(0)
    stage_four(1)
    stage_three(5)
    stage_three(4)
    stage_four(2)
    stage_four(3)
    for copy in rest:
        copy.wait()
    vec_ref[...] = vec[...] + vget[3] + vget[4] + vget[5]
    for copy in swaps:
        copy.wait()
    other = pltpu.make_async_copy(grecv, back_ref, out_sem.at[1])
    other.start()
    stage_four(5)
    stage_four(4)
    local.wait()
    other.wait()


def finish(scal, cot_own, cot_oth, dn2, middle, qkv, probs, n1, attended, x_own, x_oth, s2, k2, s1, k1, c1, c2, w):
    images, half, width = cot_own.shape
    rows = 2 * half
    heads = width // HEAD_DIM
    r, c = s1.shape[-2], s1.shape[-1] // 2
    s2, k2 = (v.reshape(DEPTH, 2, 2, 2 * r, c) for v in (s2, k2))
    s1, k1 = (v.reshape(DEPTH, 2, 2, r, 2 * c) for v in (s1, k1))
    hbm = pl.BlockSpec(memory_space=pl.ANY)
    vmem = pl.BlockSpec(memory_space=pltpu.VMEM)
    smem = pl.BlockSpec(memory_space=pltpu.SMEM)
    dma = pltpu.SemaphoreType.DMA
    block = lambda dtype, *lead: pltpu.VMEM(lead + (r, c), dtype)
    return pl.pallas_call(
        finish_kernel,
        in_specs=[smem] + [hbm] * 16 + [vmem] * 4,
        out_specs=[vmem] * 5 + [hbm] * 2,
        out_shape=[
            jax.ShapeDtypeStruct((2 * r, c), F32),
            jax.ShapeDtypeStruct((r // 2, 4 * c), F32),
            jax.ShapeDtypeStruct((r // 2, 3 * c), F32),
            jax.ShapeDtypeStruct((r // 2, c), F32),
            jax.ShapeDtypeStruct((16, width), F32),
            jax.ShapeDtypeStruct((images, half, width), F32),
            jax.ShapeDtypeStruct((images, half, width), BF16),
        ],
        scratch_shapes=[
            pltpu.VMEM((images, rows, width), BF16),
            pltpu.VMEM((images, rows, width), BF16),
            pltpu.VMEM((images, rows, width), F32),
            pltpu.VMEM((images, rows, width), F32),
            pltpu.VMEM((images, rows, 3 * width), BF16),
            pltpu.VMEM((SLOTS, 2, rows, rows), BF16),
            pltpu.VMEM((width, width), BF16),
            pltpu.VMEM((width, 3 * width), BF16),
            pltpu.VMEM((images, rows, width), BF16),
            pltpu.VMEM((images, rows, width), BF16),
            pltpu.VMEM((images, rows, width), BF16),
            pltpu.VMEM((images, rows, 3 * width), BF16),
            pltpu.VMEM((rows, width), BF16),
            pltpu.VMEM((width, width), F32),
            pltpu.VMEM((images, half, width), F32),
            pltpu.VMEM((images, half, width), BF16),
            pltpu.VMEM((images, half, width), BF16),
            pltpu.VMEM((16, width), F32),
            pltpu.VMEM((6, 16, width), F32),
            block(BF16, PARTS, DEPTH, 2, 2),
            block(BF16, 2, DEPTH, 2, 2),
            block(BF16, 4, DEPTH, 2, 2),
            block(BF16, PARTS, DEPTH, 2),
            block(BF16, PARTS, DEPTH),
            block(BF16, PARTS, DEPTH - 1),
            dma((16,)), dma((SLOTS,)), dma((PARTS, 6)), dma((PARTS, 6)), dma((images,)), dma((images,)),
            dma((6,)), dma((6,)), dma((2,)), pltpu.SemaphoreType.REGULAR((2,)),
        ],
        compiler_params=pltpu.CompilerParams(collective_id=0, has_side_effects=True, vmem_limit_bytes=63 * MIB),
        name="finish",
    )(scal, cot_own, cot_oth, dn2, middle, qkv, probs, w["proj_weight"], w["qkv_weight"], n1, attended, x_own, x_oth,
      s2, k2, s1, k1, w["ln1_gain"], w["ln2_gain"], c1, c2)


def spread(value):
    return lax.psum_scatter(value, ("img", "seq"), scatter_dimension=0, tiled=True)


def unfold(send, keep, core, folds):
    rows, cols = send.shape[-2], send.shape[-1]
    send, keep = (v.reshape(GROUP // 4, 2, rows, cols) for v in (send, keep))
    both = jnp.stack([jnp.where(core == 0, keep, send), jnp.where(core == 0, send, keep)], axis=1).astype(F32)
    if folds == 1:
        return both.reshape(GROUP * rows, cols)
    tiles = 4
    both = both.reshape(GROUP, 2, rows // 2, tiles, cols // tiles)
    return both.transpose(0, 2, 3, 1, 4).reshape(GROUP * rows // 2, 2 * cols)


def swap(value, axis, bit, size):
    return lax.ppermute(value, axis, [(i, i ^ bit) for i in range(size)])


def shards(img_size, args):
    (patches, grid_shape, split_rows, owner_shard, drop_masks, ln1_gain, ln1_bias, qkv_weight, qv_bias, proj_weight,
     proj_bias, ln2_gain, ln2_bias, fc1_weight, fc1_bias, fc2_weight, fc2_bias, cotangent) = args
    all_images, _, half, width = patches.shape
    images = all_images // 2
    rows = 2 * half
    tokens = images * rows
    side = lax.axis_index("seq")
    line = lax.axis_index("img")
    owners = 2 * img_size
    row = lambda v: v.reshape(1, -1)
    w = dict(
        ln1_gain=row(ln1_gain), ln1_bias=row(ln1_bias), qkv_weight=qkv_weight, q_bias=row(qv_bias[:width]),
        v_bias=row(qv_bias[width:]), proj_weight=proj_weight, proj_bias=row(proj_bias), ln2_gain=row(ln2_gain),
        ln2_bias=row(ln2_bias), fc1_weight=fc1_weight, fc1_bias=row(fc1_bias), fc2_weight=fc2_weight, fc2_bias=row(fc2_bias),
    )

    def exchange(value):
        value = value.reshape(all_images, half, width)
        own = lax.dynamic_slice_in_dim(value, side * images, images, axis=0)
        away = lax.dynamic_slice_in_dim(value, (1 - side) * images, images, axis=0)
        return own, swap(away, "seq", 1, 2)

    x_own, x_oth = exchange(patches)
    c_own, c_oth = exchange(cotangent)

    def place(own, back):
        back = back.astype(own.dtype)
        first = jnp.where(side == 0, own, back)
        second = jnp.where(side == 0, back, own)
        return jnp.concatenate([first, second], axis=0).reshape(all_images, 1, half, width)

    def restore(own, oth):
        return place(own, swap(oth, "seq", 1, 2))

    across = grid_shape[:, 1]
    counts = jnp.stack([split_rows * across, (grid_shape[:, 0] - split_rows) * across], axis=0)
    count_own = jnp.where(side == 0, counts[0], counts[1])
    count_oth = jnp.where(side == 0, counts[1], counts[0])
    special = (owner_shard == side).astype(jnp.int32)
    table = jnp.stack([count_own, special, count_oth, 1 - special, drop_masks[:, 0], drop_masks[:, 1]], axis=1)
    scal = lax.dynamic_slice_in_dim(table, side * images, images, axis=0)

    n1, qkv, probs, attended, middle, n2 = front(scal, x_own, x_oth, w)
    flat = lambda v: v.reshape(tokens, v.shape[-1])
    hidden, slope, out_own, out_oth = mlp(scal, flat(n2), flat(middle), w, images, 512)
    layer_out = restore(out_own, out_oth)

    mine = lax.rem(line, 2).reshape(1)
    unit1 = width // GROUP
    unit2 = fc2_weight.shape[0] // GROUP
    dn2, s2, k2, s1, k1, fc2_bias_grad, fc1_bias_grad = mlp_back(
        scal, mine, c_own, c_oth, flat(n2), hidden, slope, w, unit1, unit2
    )
    dn2 = dn2.reshape(images, rows, width)
    if owners == GROUP:
        fc2_grad, fc1_grad, qkv_grad, proj_grad, sums, grad_own, back = finish(
            scal, c_own, c_oth, dn2, middle, qkv, probs, n1, attended, x_own, x_oth, s2, k2, s1, k1,
            fc1_bias_grad, fc2_bias_grad, w
        )
        patches_grad = place(grad_own, back)
        owner = 2 * line + side
        pieces = []
        for at, count in ((0, 1), (1, 1), (2, 2), (4, 1), (5, 1), (6, 1), (7, 4), (11, 1)):
            vector = sums[at : at + count].reshape(-1)
            pieces.append(lax.dynamic_slice_in_dim(vector, owner * count * unit1, count * unit1))
    else:
        d_middle, d_branch, d_join, ln2_gain_grad, ln2_bias_grad, proj_bias_grad, q_grad, v_grad = attend_back(
            scal, c_own, c_oth, dn2, middle, qkv, probs, w
        )
        st, kt, grad_own, grad_oth, ln1_gain_grad, ln1_bias_grad = tail(
            mine, flat(n1), flat(d_join), flat(attended), flat(d_branch), x_own, x_oth, flat(d_middle), w, unit1
        )
        patches_grad = restore(grad_own, grad_oth)
        vectors = (
            ln1_gain_grad, ln1_bias_grad, jnp.concatenate([q_grad, v_grad], axis=1), proj_bias_grad, ln2_gain_grad,
            ln2_bias_grad, fc1_bias_grad, fc2_bias_grad,
        )
        fc2_grad = spread(unfold(s2, k2, line % 2, 1))
        fc1_grad = spread(unfold(s1, k1, line % 2, 2))
        tail_grad = spread(unfold(st, kt, line % 2, 2))
        qkv_grad, proj_grad = tail_grad[:, : 3 * width], tail_grad[:, 3 * width :]
        pieces = [spread(v.reshape(-1)) for v in vectors]
    l1g, l1b, qvb, pjb, l2g, l2b, f1b, f2b = pieces
    return (
        layer_out, patches_grad, l1g, l1b, qkv_grad, qvb, proj_grad, pjb, l2g, l2b, fc1_grad, f1b, fc2_grad, f2b,
    )


def solution(mesh):
    rep = [P()] * 12
    vec = P(("img", "seq"))
    mat = P(("img", "seq"), None)
    rows = P("img", "seq", None, None)

    def run(*args):
        return shards(mesh.shape["img"], args)

    return jax.shard_map(
        run,
        mesh=mesh,
        in_specs=(rows, P("img", None), P("img"), P("img"), P("img", None), *rep, rows),
        out_specs=(rows, rows, vec, vec, mat, vec, mat, vec, vec, vec, mat, vec, mat, vec),
        check_vma=False,
    )
```

```python
import functools

import jax
import jax.numpy as jnp
from jax import lax
from jax.experimental import pallas as pl
from jax.experimental.pallas import tpu as pltpu
from jax.sharding import PartitionSpec as P

HEAD_DIM = 64
LN_EPS = 1e-06
KEEP_SCALE = 1.0 / 0.9
MASK_FILL = -1e30
BF16 = jnp.bfloat16
F32 = jnp.float32
MIB = 1024 * 1024


def dot_nn(a, b):
    return lax.dot_general(a, b, (((1,), (0,)), ((), ())), preferred_element_type=F32)


def dot_nt(a, b):
    return lax.dot_general(a, b, (((1,), (1,)), ((), ())), preferred_element_type=F32)


def dot_tn(a, b):
    return lax.dot_general(a, b, (((0,), (0,)), ((), ())), preferred_element_type=F32)


def norm_parts(values):
    row_mean = jnp.mean(values, axis=-1, keepdims=True)
    centred = values - row_mean
    variance = jnp.mean(centred * centred, axis=-1, keepdims=True)
    rstd = lax.rsqrt(variance + LN_EPS)
    return centred * rstd, rstd


def norm_back(d_normed, gain, unit, rstd):
    d_unit = d_normed * gain
    mean_one = jnp.mean(d_unit, axis=-1, keepdims=True)
    mean_two = jnp.mean(d_unit * unit, axis=-1, keepdims=True)
    return rstd * (d_unit - mean_one - unit * mean_two)


def gelu_both(values):
    cdf = 0.5 + 0.5 * lax.erf(values * 0.7071067811865476)
    return values * cdf, cdf + values * (0.3989422804014327 * jnp.exp(-0.5 * values * values))


def row_valid(scal_ref, image, rows, half, axis):
    shape = (rows, 1) if axis == 0 else (1, rows)
    slot = lax.broadcasted_iota(jnp.int32, shape, axis)
    other = slot >= half
    place = jnp.where(other, slot - half, slot)
    count = jnp.where(other, scal_ref[image, 2], scal_ref[image, 0])
    special = jnp.where(other, scal_ref[image, 3], scal_ref[image, 1])
    return jnp.where(place < 2, special, (place - 2 < count).astype(jnp.int32)) > 0


def front_kernel(
    scal_ref, own_ref, oth_ref, g1_ref, b1_ref, wqkv_ref, qb_ref, vb_ref, wp_ref, pb_ref, g2_ref, b2_ref,
    n1_ref, qkv_ref, probs_ref, att_ref, mid_ref, n2_ref,
):
    image = pl.program_id(0)
    half, width = own_ref.shape[1], own_ref.shape[2]
    rows = 2 * half
    x = jnp.concatenate([own_ref[0].astype(F32), oth_ref[0].astype(F32)], axis=0)
    unit, _ = norm_parts(x)
    n1 = (unit * g1_ref[...] + b1_ref[...]).astype(BF16)
    n1_ref[0] = n1
    qkv_ref[0, :, :width] = ((dot_nn(n1, wqkv_ref[:, :width]) + qb_ref[...]).astype(BF16) * BF16(HEAD_DIM**-0.5))
    qkv_ref[0, :, width : 2 * width] = dot_nn(n1, wqkv_ref[:, width : 2 * width]).astype(BF16)
    qkv_ref[0, :, 2 * width :] = (dot_nn(n1, wqkv_ref[:, 2 * width :]) + vb_ref[...]).astype(BF16)
    fill = jnp.where(row_valid(scal_ref, image, rows, half, 0), 0.0, MASK_FILL)
    low_lane = lax.broadcasted_iota(jnp.int32, (rows, 128), 1) < HEAD_DIM
    for pair in range(width // 128):
        cut = slice(128 * pair, 128 * pair + 128)
        q2 = qkv_ref[0, :, cut]
        k2 = qkv_ref[0, :, width + 128 * pair : width + 128 * pair + 128]
        v2 = qkv_ref[0, :, 2 * width + 128 * pair : 2 * width + 128 * pair + 128]
        total = None
        for side in range(2):
            mine = low_lane if side == 0 else jnp.logical_not(low_lane)
            scores = dot_nt(k2, jnp.where(mine, q2, 0)) + fill
            top = jnp.max(scores, axis=0, keepdims=True)
            weight = jnp.exp(scores - top)
            probs = (weight * (1.0 / jnp.sum(weight, axis=0, keepdims=True))).astype(BF16)
            probs_ref[0, 2 * pair + side] = probs
            part = dot_tn(probs, jnp.where(mine, v2, 0))
            total = part if total is None else total + part
        att_ref[0, :, cut] = total.astype(BF16)
    keep = scal_ref[image, 4].astype(F32) * KEEP_SCALE
    branch = dot_nn(att_ref[0], wp_ref[...]) + pb_ref[...]
    middle = jnp.concatenate([own_ref[0].astype(F32), oth_ref[0].astype(F32)], axis=0) + keep * branch
    mid_ref[0] = middle
    unit, _ = norm_parts(middle)
    n2_ref[0] = (unit * g2_ref[...] + b2_ref[...]).astype(BF16)


def full(shape):
    zeros = (0,) * len(shape)
    return pl.BlockSpec(shape, lambda *_: zeros, pipeline_mode=pl.Buffered(1))


def front(scal, own, oth, w):
    images, half, width = own.shape
    rows = 2 * half
    heads = width // HEAD_DIM
    per = lambda *tail: pl.BlockSpec((1,) + tail, lambda i, s: (i,) + (0,) * len(tail))
    flops = 2 * images * rows * width * (4 * width + 4 * rows)
    return pl.pallas_call(
        front_kernel,
        grid_spec=pltpu.PrefetchScalarGridSpec(
            num_scalar_prefetch=1,
            grid=(images,),
            in_specs=[
                per(half, width), per(half, width), full((1, width)), full((1, width)),
                full((width, 3 * width)), full((1, width)), full((1, width)),
                full((width, width)), full((1, width)), full((1, width)), full((1, width)),
            ],
            out_specs=[
                per(rows, width), per(rows, 3 * width), per(heads, rows, rows),
                per(rows, width), per(rows, width), per(rows, width),
            ],
        ),
        out_shape=[
            jax.ShapeDtypeStruct((images, rows, width), BF16),
            jax.ShapeDtypeStruct((images, rows, 3 * width), BF16),
            jax.ShapeDtypeStruct((images, heads, rows, rows), BF16),
            jax.ShapeDtypeStruct((images, rows, width), BF16),
            jax.ShapeDtypeStruct((images, rows, width), F32),
            jax.ShapeDtypeStruct((images, rows, width), BF16),
        ],
        compiler_params=pltpu.CompilerParams(vmem_limit_bytes=56 * MIB),
        cost_estimate=pl.CostEstimate(flops=flops, transcendentals=images * heads * rows * rows, bytes_accessed=30_000_000),
        name="front",
    )(scal, own, oth, w["ln1_gain"], w["ln1_bias"], w["qkv_weight"], w["q_bias"], w["v_bias"],
      w["proj_weight"], w["proj_bias"], w["ln2_gain"], w["ln2_bias"])


def mlp_kernel(
    scal_ref, n2_ref, mid_ref, w1_ref, c1_ref, w2_ref, c2_ref,
    hid_ref, slope_ref, own_ref, oth_ref, acc_ref,
):
    step = pl.program_id(0)
    images, half, width = own_ref.shape
    rows = 2 * half
    hidden, slope = gelu_both(dot_nn(n2_ref[...], w1_ref[...]) + c1_ref[...])
    hidden = hidden.astype(BF16)
    hid_ref[...] = hidden
    slope_ref[...] = slope.astype(BF16)
    part = dot_nn(hidden, w2_ref[...])

    @pl.when(step == 0)
    def _():
        acc_ref[...] = part

    @pl.when(step > 0)
    def _():
        acc_ref[...] += part

    @pl.when(step == pl.num_programs(0) - 1)
    def _():
        for image in range(images):
            keep = scal_ref[image, 5].astype(F32) * KEEP_SCALE
            cut = slice(rows * image, rows * image + rows)
            final = mid_ref[cut, :] + keep * (acc_ref[cut, :] + c2_ref[...])
            out = jnp.where(row_valid(scal_ref, image, rows, half, 0), final, 0.0).astype(BF16)
            own_ref[image] = out[:half]
            oth_ref[image] = out[half:]


def mlp(scal, n2, middle, w, images, tile):
    tokens, width = n2.shape
    hidden_width = w["fc1_weight"].shape[1]
    half = tokens // images // 2
    return pl.pallas_call(
        mlp_kernel,
        grid_spec=pltpu.PrefetchScalarGridSpec(
            num_scalar_prefetch=1,
            grid=(hidden_width // tile,),
            in_specs=[
                full((tokens, width)), full((tokens, width)),
                pl.BlockSpec((width, tile), lambda j, s: (0, j)), pl.BlockSpec((1, tile), lambda j, s: (0, j)),
                pl.BlockSpec((tile, width), lambda j, s: (j, 0)), full((1, width)),
            ],
            out_specs=[
                pl.BlockSpec((tokens, tile), lambda j, s: (0, j)), pl.BlockSpec((tokens, tile), lambda j, s: (0, j)),
                full((images, half, width)), full((images, half, width)),
            ],
            scratch_shapes=[pltpu.VMEM((tokens, width), F32)],
        ),
        out_shape=[
            jax.ShapeDtypeStruct((tokens, hidden_width), BF16),
            jax.ShapeDtypeStruct((tokens, hidden_width), BF16),
            jax.ShapeDtypeStruct((images, half, width), BF16),
            jax.ShapeDtypeStruct((images, half, width), BF16),
        ],
        compiler_params=pltpu.CompilerParams(vmem_limit_bytes=56 * MIB),
        cost_estimate=pl.CostEstimate(flops=4 * tokens * width * hidden_width, transcendentals=2 * tokens * hidden_width, bytes_accessed=30_000_000),
        name="mlp",
    )(scal, n2, middle, w["fc1_weight"], w["fc1_bias"], w["fc2_weight"], w["fc2_bias"])


def put_rows(grad_ref, value, send_ref, keep_ref, mine, lead):
    grad_ref[...] = value
    run = 2 * send_ref.shape[-2]
    for k in range(grad_ref.shape[0] // (2 * run)):
        for ref, core in ((send_ref, 1 - mine), (keep_ref, mine)):
            for x in range(2):
                at = pl.multiple_of((2 * k + core) * run + x * (run // 2), 8)
                ref[lead + (k, x)] = grad_ref[pl.ds(at, run // 2), :].astype(BF16)


def put_folded(grad_ref, value, send_ref, keep_ref, mine):
    grad_ref[...] = value
    unit = send_ref.shape[-2] // 2
    side = grad_ref.shape[1] // 2
    for k in range(grad_ref.shape[0] // (4 * unit)):
        for ref, core in ((send_ref, 1 - mine), (keep_ref, mine)):
            for x in range(2):
                at = pl.multiple_of((4 * k + 2 * core + x) * unit, 8)
                piece = grad_ref[pl.ds(at, unit), :]
                ref[k, x] = jnp.concatenate([piece[:, :side], piece[:, side:]], axis=0).astype(BF16)


def mlp_back_kernel(
    scal_ref, mine_ref, own_ref, oth_ref, n2_ref, hid_ref, slope_ref, w1_ref, w2_ref,
    dn2_ref, s2_ref, k2_ref, s1_ref, k1_ref, c2_ref, c1_ref, dmlp_ref, grad_ref, acc_ref,
):
    step = pl.program_id(0)
    images, half, width = own_ref.shape
    rows = 2 * half
    mine = mine_ref[0]

    @pl.when(step == 0)
    def _():
        total = jnp.zeros((1, width), F32)
        for image in range(images):
            keep = scal_ref[image, 5].astype(F32) * KEEP_SCALE
            cot = jnp.concatenate([own_ref[image].astype(F32), oth_ref[image].astype(F32)], axis=0)
            live = row_valid(scal_ref, image, rows, half, 0)
            d_mlp = (jnp.where(live, cot, 0.0) * keep).astype(BF16)
            dmlp_ref[rows * image : rows * image + rows, :] = d_mlp
            total += jnp.sum(d_mlp.astype(F32), axis=0, keepdims=True)
        c2_ref[...] = total

    d_pre = slope_ref[...].astype(F32) * dot_nt(dmlp_ref[...], w2_ref[...])
    d_pre = d_pre.astype(BF16)
    c1_ref[...] = jnp.sum(d_pre.astype(F32), axis=0, keepdims=True)
    part = dot_nt(d_pre, w1_ref[...])
    put_folded(grad_ref, dot_tn(n2_ref[...], d_pre), s1_ref, k1_ref, mine)
    put_rows(grad_ref, dot_tn(hid_ref[...], dmlp_ref[...]), s2_ref, k2_ref, mine, (0,))

    @pl.when(step == 0)
    def _():
        acc_ref[...] = part

    @pl.when(step > 0)
    def _():
        acc_ref[...] += part

    @pl.when(step == pl.num_programs(0) - 1)
    def _():
        dn2_ref[...] = acc_ref[...]


def mlp_back(scal, mine, own, oth, n2, hidden, slope, w, unit1, unit2):
    tokens, width = n2.shape
    images, half, _ = own.shape
    hidden_width = hidden.shape[1]
    tile = width
    steps = hidden_width // tile
    runs1, runs2 = width // (4 * unit1), tile // (4 * unit2)
    col = pl.BlockSpec((tokens, tile), lambda j, s, m: (0, j))
    half1 = pl.BlockSpec((runs1, 2, 2 * unit1, tile // 2), lambda j, s, m: (0, 0, 0, j))
    half2 = pl.BlockSpec((1, runs2, 2, unit2, width), lambda j, s, m: (j, 0, 0, 0, 0))
    return pl.pallas_call(
        mlp_back_kernel,
        grid_spec=pltpu.PrefetchScalarGridSpec(
            num_scalar_prefetch=2,
            grid=(steps,),
            in_specs=[
                full((images, half, width)), full((images, half, width)), full((tokens, width)), col, col,
                pl.BlockSpec((width, tile), lambda j, s, m: (0, j)), pl.BlockSpec((tile, width), lambda j, s, m: (j, 0)),
            ],
            out_specs=[
                full((tokens, width)), half2, half2, half1, half1,
                full((1, width)), pl.BlockSpec((1, tile), lambda j, s, m: (0, j)),
            ],
            scratch_shapes=[
                pltpu.VMEM((tokens, width), BF16), pltpu.VMEM((width, width), F32), pltpu.VMEM((tokens, width), F32),
            ],
        ),
        out_shape=[
            jax.ShapeDtypeStruct((tokens, width), F32),
            jax.ShapeDtypeStruct((steps, runs2, 2, unit2, width), BF16),
            jax.ShapeDtypeStruct((steps, runs2, 2, unit2, width), BF16),
            jax.ShapeDtypeStruct((runs1, 2, 2 * unit1, hidden_width // 2), BF16),
            jax.ShapeDtypeStruct((runs1, 2, 2 * unit1, hidden_width // 2), BF16),
            jax.ShapeDtypeStruct((1, width), F32),
            jax.ShapeDtypeStruct((1, hidden_width), F32),
        ],
        compiler_params=pltpu.CompilerParams(vmem_limit_bytes=58 * MIB),
        cost_estimate=pl.CostEstimate(flops=8 * tokens * width * hidden_width, transcendentals=0, bytes_accessed=35_000_000),
        name="mlp_back",
    )(scal, mine, own, oth, n2, hidden, slope, w["fc1_weight"], w["fc2_weight"])


def attend_back_kernel(
    scal_ref, own_ref, oth_ref, dn2_ref, mid_ref, qkv_ref, probs_ref, wp_ref, g2_ref,
    dmid_ref, dbr_ref, djoin_ref, g2g_ref, g2b_ref, pbg_ref, qbg_ref, vbg_ref, datt_ref,
):
    image = pl.program_id(0)
    half, width = own_ref.shape[1], own_ref.shape[2]
    rows = 2 * half
    live = row_valid(scal_ref, image, rows, half, 0)
    d_final = jnp.where(live, jnp.concatenate([own_ref[0].astype(F32), oth_ref[0].astype(F32)], axis=0), 0.0)
    unit, rstd = norm_parts(mid_ref[0])
    dn2 = dn2_ref[0]
    gain_part = jnp.sum(dn2 * unit, axis=0, keepdims=True)
    bias_part = jnp.sum(dn2, axis=0, keepdims=True)
    d_middle = d_final + norm_back(dn2, g2_ref[...], unit, rstd)
    dmid_ref[0] = d_middle
    keep = scal_ref[image, 4].astype(F32) * KEEP_SCALE
    d_branch = (d_middle * keep).astype(BF16)
    dbr_ref[0] = d_branch
    proj_part = jnp.sum(d_branch.astype(F32), axis=0, keepdims=True)
    datt_ref[...] = dot_nt(d_branch, wp_ref[...]).astype(BF16)
    low_lane = lax.broadcasted_iota(jnp.int32, (rows, 128), 1) < HEAD_DIM
    for pair in range(width // 128):
        cut = slice(128 * pair, 128 * pair + 128)
        q2 = qkv_ref[0, :, cut]
        k2 = qkv_ref[0, :, width + 128 * pair : width + 128 * pair + 128]
        v2 = qkv_ref[0, :, 2 * width + 128 * pair : 2 * width + 128 * pair + 128]
        a2 = datt_ref[:, cut]
        dq = dk = dv = None
        for side in range(2):
            mine = low_lane if side == 0 else jnp.logical_not(low_lane)
            probs_low = probs_ref[0, 2 * pair + side]
            probs = probs_low.astype(F32)
            a_side = jnp.where(mine, a2, 0)
            d_probs = dot_nt(v2, a_side)
            inner = jnp.sum(probs * d_probs, axis=0, keepdims=True)
            d_scores = (probs * (d_probs - inner)).astype(BF16)
            dq_part = dot_tn(d_scores, jnp.where(mine, k2, 0))
            dk_part = dot_nn(d_scores, jnp.where(mine, q2, 0))
            dv_part = dot_nn(probs_low, a_side)
            dq = dq_part if dq is None else dq + dq_part
            dk = dk_part if dk is None else dk + dk_part
            dv = dv_part if dv is None else dv + dv_part
        djoin_ref[0, :, cut] = (dq * HEAD_DIM**-0.5).astype(BF16)
        djoin_ref[0, :, width + 128 * pair : width + 128 * pair + 128] = dk.astype(BF16)
        djoin_ref[0, :, 2 * width + 128 * pair : 2 * width + 128 * pair + 128] = dv.astype(BF16)
    q_part = jnp.sum(djoin_ref[0, :, :width].astype(F32), axis=0, keepdims=True)
    v_part = jnp.sum(djoin_ref[0, :, 2 * width :].astype(F32), axis=0, keepdims=True)
    sums = ((g2g_ref, gain_part), (g2b_ref, bias_part), (pbg_ref, proj_part), (qbg_ref, q_part), (vbg_ref, v_part))

    @pl.when(image == 0)
    def _():
        for ref, part in sums:
            ref[...] = part

    @pl.when(image > 0)
    def _():
        for ref, part in sums:
            ref[...] += part


def attend_back(scal, own, oth, dn2, middle, qkv, probs, w):
    images, half, width = own.shape
    rows = 2 * half
    heads = width // HEAD_DIM
    per = lambda *tail: pl.BlockSpec((1,) + tail, lambda i, s: (i,) + (0,) * len(tail))
    vec = jax.ShapeDtypeStruct((1, width), F32)
    return pl.pallas_call(
        attend_back_kernel,
        grid_spec=pltpu.PrefetchScalarGridSpec(
            num_scalar_prefetch=1,
            grid=(images,),
            in_specs=[
                per(half, width), per(half, width), per(rows, width), per(rows, width), per(rows, 3 * width),
                per(heads, rows, rows), full((width, width)), full((1, width)),
            ],
            out_specs=[per(rows, width), per(rows, width), per(rows, 3 * width)] + [full((1, width))] * 5,
            scratch_shapes=[pltpu.VMEM((rows, width), BF16)],
        ),
        out_shape=[
            jax.ShapeDtypeStruct((images, rows, width), F32),
            jax.ShapeDtypeStruct((images, rows, width), BF16),
            jax.ShapeDtypeStruct((images, rows, 3 * width), BF16),
            vec, vec, vec, vec, vec,
        ],
        compiler_params=pltpu.CompilerParams(vmem_limit_bytes=56 * MIB),
        cost_estimate=pl.CostEstimate(flops=2 * images * rows * width * (width + 8 * rows), transcendentals=0, bytes_accessed=35_000_000),
        name="attend_back",
    )(scal, own, oth, dn2, middle, qkv, probs, w["proj_weight"], w["ln2_gain"])


def tail_kernel(
    mine_ref, n1_ref, djoin_ref, att_ref, dbr_ref, wqkv_ref, xo_ref, xt_ref, dmid_ref, g1_ref,
    send_ref, keep_ref, go_ref, gt_ref, g1g_ref, g1b_ref, grad_ref, acc_ref,
):
    step = pl.program_id(0)
    last = pl.num_programs(0) - 1
    images, half, width = xo_ref.shape
    rows = 2 * half
    mine = mine_ref[0]

    @pl.when(step < last)
    def _():
        put_folded(grad_ref, dot_tn(n1_ref[...], djoin_ref[...]), send_ref, keep_ref, mine)
        part = dot_nt(djoin_ref[...], wqkv_ref[...])

        @pl.when(step == 0)
        def _():
            acc_ref[...] = part

        @pl.when(step > 0)
        def _():
            acc_ref[...] += part

    @pl.when(step == last)
    def _():
        put_folded(grad_ref, dot_tn(att_ref[...], dbr_ref[...]), send_ref, keep_ref, mine)
        gain_sum = jnp.zeros((1, width), F32)
        bias_sum = jnp.zeros((1, width), F32)
        for image in range(images):
            x = jnp.concatenate([xo_ref[image].astype(F32), xt_ref[image].astype(F32)], axis=0)
            unit, rstd = norm_parts(x)
            dn1 = acc_ref[rows * image : rows * image + rows, :]
            gain_sum += jnp.sum(dn1 * unit, axis=0, keepdims=True)
            bias_sum += jnp.sum(dn1, axis=0, keepdims=True)
            out = dmid_ref[rows * image : rows * image + rows, :] + norm_back(dn1, g1_ref[...], unit, rstd)
            go_ref[image] = out[:half]
            gt_ref[image] = out[half:].astype(BF16)
        g1g_ref[...] = gain_sum
        g1b_ref[...] = bias_sum


def tail(mine, n1, d_join, attended, d_branch, own, oth, d_middle, w, unit):
    tokens, width = n1.shape
    images, half, _ = own.shape
    runs = width // (4 * unit)
    halves = pl.BlockSpec((runs, 2, 2 * unit, width // 2), lambda j, m: (0, 0, 0, j))
    clip = lambda j: jnp.minimum(j, 2)
    return pl.pallas_call(
        tail_kernel,
        grid_spec=pltpu.PrefetchScalarGridSpec(
            num_scalar_prefetch=1,
            grid=(4,),
            in_specs=[
                full((tokens, width)), pl.BlockSpec((tokens, width), lambda j, m: (0, clip(j))), full((tokens, width)),
                full((tokens, width)), pl.BlockSpec((width, width), lambda j, m: (0, clip(j))),
                full((images, half, width)), full((images, half, width)), full((tokens, width)), full((1, width)),
            ],
            out_specs=[
                halves, halves, full((images, half, width)), full((images, half, width)),
                full((1, width)), full((1, width)),
            ],
            scratch_shapes=[pltpu.VMEM((width, width), F32), pltpu.VMEM((tokens, width), F32)],
        ),
        out_shape=[
            jax.ShapeDtypeStruct((runs, 2, 2 * unit, 2 * width), BF16),
            jax.ShapeDtypeStruct((runs, 2, 2 * unit, 2 * width), BF16),
            jax.ShapeDtypeStruct((images, half, width), F32),
            jax.ShapeDtypeStruct((images, half, width), BF16),
            jax.ShapeDtypeStruct((1, width), F32),
            jax.ShapeDtypeStruct((1, width), F32),
        ],
        compiler_params=pltpu.CompilerParams(vmem_limit_bytes=56 * MIB),
        cost_estimate=pl.CostEstimate(flops=14 * tokens * width * width, transcendentals=0, bytes_accessed=35_000_000),
        name="tail",
    )(mine, n1, d_join, attended, d_branch, w["qkv_weight"], own, oth, d_middle, w["ln1_gain"])


MESH = pl.DeviceIdType.MESH
PARTS = 7
SLOTS = 3
GROUP = 32


class Far:
    def __init__(self, ends, send_sem, recv_sem, peer):
        self.parts = (ends, send_sem, recv_sem, peer)
        self.build().start()

    def build(self):
        ends, send_sem, recv_sem, peer = self.parts
        src, dst = ends()
        return pltpu.make_async_remote_copy(
            src_ref=src, dst_ref=dst, send_sem=send_sem(), recv_sem=recv_sem(), device_id=peer, device_id_type=MESH
        )

    def wait(self):
        self.build().wait()


class Parcel:
    def __init__(self, keep, send, landing, levels, sems, order, place, names="wvyx"):
        self.keep, self.send, self.landing, self.levels, self.sems = keep, send, landing, levels, sems
        self.order, self.place, self.names = order, place, names

    def copy(self, src, dst, slot, peer):
        send_sem, recv_sem = self.sems
        return pltpu.make_async_remote_copy(
            src_ref=src, dst_ref=dst, send_sem=send_sem(slot), recv_sem=recv_sem(slot), device_id=peer, device_id_type=MESH
        )

    def bring(self, step):
        if step == 0:
            return self.copy(self.send(), self.landing(), 0, self.place["core"][1])
        name, used = self.order[step - 1], self.order[:step]
        spot = tuple(
            self.place[n][2] if n == name else self.place[n][0] if n in used else slice(None) for n in self.names
        )
        return self.copy(self.keep().at[spot], self.levels(step - 1), step, self.place[name][1])

    def start(self):
        self.bring(0).start()

    def gather(self, step):
        self.bring(step).wait()
        return self.add(step)

    def add(self, step):
        used = self.order[:step]
        left = [n for n in self.names if n not in used]
        arrived = self.levels(step - 1) if step else self.landing()

        def one(i):
            at = {}
            for n in reversed(left):
                at[n] = i % 2
                i = i // 2
            inner = tuple(at[n] for n in left)
            spot = tuple(at[n] if n in at else self.place[n][0] for n in self.names)
            total = self.keep()[spot].astype(F32) + arrived[inner].astype(F32)
            if step == len(self.order):
                return total
            self.keep()[spot] = total.astype(BF16)

        if not left:
            return one(0)
        pl.loop(0, 2 ** len(left))(lambda i: one(i) and None)

    def launch(self, step):
        self.bring(step + 1).start()

    def move(self, step):
        self.gather(step)
        self.launch(step)


class HalfParcel(Parcel):
    def launch(self, step):
        if step < 3:
            return super().launch(step)

        @pl.when(self.goes)
        def _():
            self.bring(4).start()

    def finish(self, write):
        @pl.when(self.goes)
        def _():
            self.bring(4).wait_send()

        @pl.when(self.mine)
        def _():
            self.bring(4).wait_recv()
            write(self.add(4))


def level_shapes(names, order, rows, cols):
    return [
        (2,) * len([n for n in names if n not in order[: step + 1]]) + (rows, cols) for step in range(len(order))
    ]


ORDERS = ("yxvw", "vyxw", "xyvw", "yvwx", "yvwx", "yxvw", "vwyx")
FC2_A, FC2_B, FC1_A, FC1_B, VAL_PROJ, QUERY, KEY = range(7)


def rest_kernel(
    scal_ref, cot_own, cot_oth, n2_hbm, mid_hbm, qkv_hbm, probs_hbm, w1_hbm, w2_hbm, wp_hbm, wqkv_hbm, n1_hbm, att_hbm,
    x_own, x_oth, g1_ref, g2_ref, c1_ref, c2_ref,
    fc2_ref, fc1_ref, qkvg_ref, projg_ref, vec_ref, out_ref, grad_ref,
    cot, dn2, mid, acc, left, right, wbuf, qkv, probs, djoin, datt, tile, ost, gsend, grecv, vec, vget,
    keep_a, send_a, land_a, keep_b, send_b, land_b, keep_c, send_c, land_c, *others,
):
    levels = [others[4 * k : 4 * k + 4] for k in range(PARTS)]
    (load_sem, probs_sem, qkv_sem, w_sem, send_sem, recv_sem, side_send, side_recv, vec_send, vec_recv, out_sem,
     free_sem) = others[4 * PARTS :]
    images, rows, width = dn2.shape
    half = rows // 2
    pairs = width // 128
    steps = c1_ref.shape[0]
    line = lax.axis_index("img")
    x = lax.axis_index("seq")
    core = line % 2
    y = (line // 2) % 2
    z = line // 4
    sibling = (line + 1 - 2 * core, x)
    level = (line + 2 - 4 * y, x)
    across = (line, 1 - x)
    zv, zw = z % 2, z // 2
    near_z = (line + 4 - 8 * zv, x)
    far_z = (line + 8 - 16 * zw, x)
    peers = [sibling, level, across, near_z, far_z]
    barrier = pltpu.get_barrier_semaphore()
    for peer in peers:
        pl.semaphore_signal(barrier, inc=1, device_id=peer, device_id_type=MESH)

    loads = []

    def fetch(src, dst):
        copy = pltpu.make_async_copy(src, dst, load_sem.at[len(loads)])
        copy.start()
        loads.append(copy)
        return copy

    def probs_copy(index, slot):
        return pltpu.make_async_copy(
            probs_hbm.at[index // pairs, pl.ds(2 * (index % pairs), 2)], probs.at[slot], probs_sem.at[slot]
        )

    def qkv_copy(i, slot):
        return pltpu.make_async_copy(qkv_hbm.at[i], qkv.at[slot], qkv_sem.at[slot])

    def w1_copy(t, slot):
        at = pl.multiple_of(t * width, 128)
        return pltpu.make_async_copy(w1_hbm.at[:, pl.ds(at, width)], wbuf.at[slot], w_sem.at[slot])

    def w2_copy(t, slot):
        at = pl.multiple_of(t * width, 128)
        return pltpu.make_async_copy(w2_hbm.at[pl.ds(at, width), :], wbuf.at[2 + slot], w_sem.at[2 + slot])

    first = [fetch(cot_own, cot.at[:, pl.ds(0, half)]), fetch(cot_oth, cot.at[:, pl.ds(half, half)]), fetch(n2_hbm, left)]
    w1_copy(0, 0).start()
    w2_copy(0, 0).start()
    mid_in = fetch(mid_hbm, mid)
    for slot in range(SLOTS):
        probs_copy(slot, slot).start()
    for slot in range(2):
        qkv_copy(slot, slot).start()

    place = {
        "core": (core, sibling), "y": (y, level, 1 - y), "x": (x, across, 1 - x),
        "v": (zv, near_z, 1 - zv), "w": (zw, far_z, 1 - zw),
    }
    homes = [
        (keep_a.at[0], send_a, land_a), (keep_a.at[1], send_a, land_a),
        (keep_b.at[0], send_b.at[0], land_b.at[0]), (keep_b.at[1], send_b.at[1], land_b.at[1]),
        (keep_b.at[2], send_b.at[0], land_b.at[0]),
        (keep_c.at[0], send_c.at[0], land_c.at[0]), (keep_c.at[1], send_c.at[1], land_c.at[1]),
    ]
    parcels = []
    for k in range(PARTS):
        keep, send, land = (lambda k=k, n=n: homes[k][n] for n in range(3))
        sems = (lambda slot, k=k: send_sem.at[k, slot]), (lambda slot, k=k: recv_sem.at[k, slot])
        build = HalfParcel if k < 2 else Parcel
        parcels.append(
            build(keep, send, land, lambda step, k=k: levels[k][step], sems, ORDERS[k], place, "vyx" if k < 2 else "wvyx")
        )
    for k in range(2):
        parcels[k].goes, parcels[k].mine = zw != k, zw == k
    free_slot = {FC2_A: 0, FC1_A: 1}
    needs = {FC2_B: 0, VAL_PROJ: 1}

    def release(k):
        pl.semaphore_signal(free_sem.at[free_slot[k]], inc=1, device_id=sibling, device_id_type=MESH)

    def start(k):
        if k in needs:
            pl.semaphore_wait(free_sem.at[needs[k]], 1)
        parcels[k].start()

    r, c = keep_b.shape[-2], keep_b.shape[-1]
    unit, side_cols = r // 2, c // 2

    def put_block_rows(k, zz):
        for ref, who in ((send_a, 1 - core), (keep_a.at[k], core)):
            for b in range(2):
                for e in range(2):
                    at = pl.multiple_of((2 * b + who) * 4 * r + e * 2 * r, 8)
                    ref[zz, b, e] = tile[pl.ds(at, 2 * r), :].astype(BF16)

    def put_folds(send, kept, t):
        spot = pl.ds(pl.multiple_of(t * side_cols, 128), side_cols)
        for k in range(8):
            for ref, who in ((send, 1 - core), (kept, core)):
                for e in range(2):
                    at = pl.multiple_of((4 * k + 2 * who + e) * unit, 8)
                    piece = tile[pl.ds(at, unit), :]
                    ref[k // 4, (k // 2) % 2, k % 2, e, :, spot] = jnp.concatenate(
                        [piece[:, :side_cols], piece[:, side_cols:]], axis=0
                    ).astype(BF16)

    def step_one(k):
        parcels[k].gather(0)
        if k in free_slot:
            release(k)
        parcels[k].launch(0)

    flat = lambda ref: ref[...].reshape(images * rows, ref.shape[-1])
    column = lambda k: djoin[:, :, k * width : k * width + width].reshape(images * rows, width)

    vec[...] = jnp.zeros_like(vec)
    acc[...] = jnp.zeros_like(acc)
    dn2[...] = jnp.zeros_like(dn2)
    for copy in first:
        copy.wait()
    for i in range(images):
        gate = scal_ref[i, 5].astype(F32) * KEEP_SCALE
        live = row_valid(scal_ref, i, rows, half, 0)
        d_mlp = (jnp.where(live, cot[i].astype(F32), 0.0) * gate).astype(BF16)
        right[i] = d_mlp
        vec[11:12, :] += jnp.sum(d_mlp.astype(F32), axis=0, keepdims=True)
    pl.semaphore_wait(barrier, len(peers))

    wp_copy = pltpu.make_async_copy(wp_hbm, wbuf.at[2], w_sem.at[2])

    def wqkv_copy(k, slot):
        return pltpu.make_async_copy(wqkv_hbm.at[:, pl.ds(k * width, width)], wbuf.at[slot], w_sem.at[slot])

    @pl.loop(0, steps)
    def _(t):
        slot = t % 2
        w1_copy(t, slot).wait()
        w2_copy(t, slot).wait()

        @pl.when(t + 1 < steps)
        def _():
            w1_copy(t + 1, 1 - slot).start()
            w2_copy(t + 1, 1 - slot).start()

        @pl.when(t + 1 == steps)
        def _():
            wqkv_copy(0, 0).start()
            wp_copy.start()

        @pl.when(t == 2)
        def _():
            start(FC2_A)
            start(FC1_A)

        for i in range(images):
            pre = dot_nn(left[i], wbuf[slot]) + c1_ref[pl.ds(t, 1), :]
            hidden, slope = gelu_both(pre)
            hidden = hidden.astype(BF16)
            d_pre = (slope * dot_nt(right[i], wbuf[2 + slot])).astype(BF16)
            djoin[i, :, :width] = hidden
            djoin[i, :, width : 2 * width] = d_pre
            vec[pl.ds(7 + t, 1), :] += jnp.sum(d_pre.astype(F32), axis=0, keepdims=True)
            acc[i] += dot_nn(hidden, wbuf[2 + slot])
            dn2[i] += dot_nt(d_pre, wbuf[slot])

        tile[...] = dot_tn(column(0), flat(right))

        @pl.when(t == 2)
        def _():
            for k in (FC2_A, FC1_A):
                step_one(k)

        for k in range(2):

            @pl.when(t // 2 == k)
            def _():
                put_block_rows(k, t % 2)

        tile[...] = dot_tn(flat(left), column(1))
        for k in range(2):

            @pl.when(t // 2 == k)
            def _():
                put_folds(send_b.at[k], keep_b.at[k], t % 2)

    wqkv_copy(1, 1).start()
    wqkv_copy(2, 3).start()
    n1_in, att_in = fetch(n1_hbm, left), fetch(att_hbm, right)
    start(FC2_B)
    start(FC1_B)
    mid_in.wait()
    for i in range(images):
        gate = scal_ref[i, 5].astype(F32) * KEEP_SCALE
        final = mid[i] + gate * (acc[i] + c2_ref[...])
        out = jnp.where(row_valid(scal_ref, i, rows, half, 0), final, 0.0).astype(BF16)
        ost[i] = out[:half]
        gsend[i] = out[half:]
    out_own = pltpu.make_async_copy(ost, out_ref.at[pl.ds(x * images, images)], out_sem.at[0])
    out_own.start()
    out_far = Far(
        lambda: (gsend, out_ref.at[pl.ds(x * images, images)]), lambda: side_send.at[images], lambda: side_recv.at[images], across
    )

    wp_copy.wait()
    for i in range(images):
        live = row_valid(scal_ref, i, rows, half, 0)
        d_final = jnp.where(live, cot[i].astype(F32), 0.0)
        unit_two, rstd = norm_parts(mid[i])
        d_normed = dn2[i]
        vec[5:6, :] += jnp.sum(d_normed * unit_two, axis=0, keepdims=True)
        vec[6:7, :] += jnp.sum(d_normed, axis=0, keepdims=True)
        d_middle = d_final + norm_back(d_normed, g2_ref[...], unit_two, rstd)
        dn2[i] = d_middle
        gate = scal_ref[i, 4].astype(F32) * KEEP_SCALE
        d_branch = (d_middle * gate).astype(BF16)
        datt[i] = d_branch
        vec[4:5, :] += jnp.sum(d_branch.astype(F32), axis=0, keepdims=True)
    step_one(FC2_B)
    step_one(FC1_B)
    parcels[FC2_A].move(1)
    parcels[FC1_A].move(1)
    n1_in.wait()
    att_in.wait()
    tile[...] = dot_tn(flat(right), flat(datt))
    put_folds(send_b.at[0], keep_b.at[2], 1)
    x_in = [fetch(x_own, right.at[:, pl.ds(0, half)]), fetch(x_oth, right.at[:, pl.ds(half, half)])]
    for i in range(images):
        datt[i] = dot_nt(datt[i], wbuf[2]).astype(BF16)

    low_lane = lax.broadcasted_iota(jnp.int32, (rows, 128), 1) < HEAD_DIM
    sides = (low_lane, jnp.logical_not(low_lane))
    cuts = lambda pair: [slice(k * width + 128 * pair, k * width + 128 * pair + 128) for k in range(3)]
    total_pairs = images * pairs

    def next_probs(index, slot):
        @pl.when(index + SLOTS < 2 * total_pairs)
        def _():
            probs_copy((index + SLOTS) % total_pairs, slot).start()

    @pl.loop(0, images)
    def _(i):
        for pair in range(pairs):
            index = i * pairs + pair
            slot = index % SLOTS
            probs_copy(index, slot).wait()
            q_cut, _, v_cut = cuts(pair)
            a2 = datt[i, :, q_cut]
            dv = dot_nn(probs[slot, 0], jnp.where(sides[0], a2, 0)) + dot_nn(probs[slot, 1], jnp.where(sides[1], a2, 0))
            djoin[i, :, v_cut] = dv.astype(BF16)
            next_probs(index, slot)
        vec[3:4, :] += jnp.sum(djoin[i, :, 2 * width :].astype(F32), axis=0, keepdims=True)

    tile[...] = dot_tn(flat(left), column(2))
    put_folds(send_b.at[0], keep_b.at[2], 0)
    start(VAL_PROJ)

    plan = {
        (0, 2): lambda: step_one(VAL_PROJ),
        (0, 4): lambda: parcels[FC1_A].move(2),
        (0, 5): lambda: parcels[FC2_B].move(1),
        (1, 2): lambda: parcels[FC2_A].move(2),
        (1, 4): lambda: parcels[FC1_B].move(1),
        (2, 0): lambda: parcels[FC1_A].move(3),
        (2, 2): lambda: parcels[FC2_A].move(3),
        (2, 4): lambda: parcels[FC2_B].move(2),
    }

    @pl.loop(0, images)
    def _(i):
        q_slot = i % 2
        qkv_copy(i, q_slot).wait()
        for pair in range(pairs):
            index = total_pairs + i * pairs + pair
            slot = index % SLOTS
            probs_copy(index - total_pairs, slot).wait()
            q_cut, k_cut, v_cut = cuts(pair)
            q2, k2, v2, a2 = qkv[q_slot, :, q_cut], qkv[q_slot, :, k_cut], qkv[q_slot, :, v_cut], datt[i, :, q_cut]
            dq = dk = None
            for side in range(2):
                high = probs[slot, side].astype(F32)
                d_probs = dot_nt(v2, jnp.where(sides[side], a2, 0))
                inner = jnp.sum(high * d_probs, axis=0, keepdims=True)
                d_scores = (high * (d_probs - inner)).astype(BF16)
                parts = dot_tn(d_scores, jnp.where(sides[side], k2, 0)), dot_nn(d_scores, jnp.where(sides[side], q2, 0))
                dq, dk = parts if dq is None else (dq + parts[0], dk + parts[1])
            djoin[i, :, q_cut] = (dq * HEAD_DIM**-0.5).astype(BF16)
            djoin[i, :, k_cut] = dk.astype(BF16)
            next_probs(index, slot)
            for (image, at), job in plan.items():
                if at == pair:

                    @pl.when(i == image)
                    def _():
                        job()

        @pl.when(i + 2 < images)
        def _():
            qkv_copy(i + 2, q_slot).start()

        vec[2:3, :] += jnp.sum(djoin[i, :, :width].astype(F32), axis=0, keepdims=True)

    for t, k in ((0, QUERY), (1, KEY)):
        tile[...] = dot_tn(flat(left), column(t))
        put_folds(send_c.at[t], keep_c.at[t], 0)
        start(k)
    parcels[FC1_B].move(2)
    for copy in x_in:
        copy.wait()
    wqkv_copy(0, 0).wait()
    wqkv_copy(1, 1).wait()
    wqkv_copy(2, 3).wait()
    out_far.wait()

    def input_grad(i):
        unit_one, rstd = norm_parts(right[i].astype(F32))
        d_normed = dot_nt(djoin[i, :, :width], wbuf[0])
        d_normed += dot_nt(djoin[i, :, width : 2 * width], wbuf[1])
        d_normed += dot_nt(djoin[i, :, 2 * width :], wbuf[3])
        vec[0:1, :] += jnp.sum(d_normed * unit_one, axis=0, keepdims=True)
        vec[1:2, :] += jnp.sum(d_normed, axis=0, keepdims=True)
        out = dn2[i] + norm_back(d_normed, g1_ref[...], unit_one, rstd)
        acc[i, :half] = out[:half]
        gsend[i] = out[half:].astype(BF16)

    swaps = []
    for i in range(images):
        input_grad(i)
        swaps.append(
            Far(lambda i=i: (gsend.at[i], grecv.at[i]), lambda i=i: side_send.at[i], lambda i=i: side_recv.at[i], across)
        )
        if i == 0:
            step_one(QUERY)
            step_one(KEY)
        if i == 1:
            parcels[VAL_PROJ].move(1)
            parcels[FC2_B].move(3)
    grad_own = pltpu.make_async_copy(acc.at[:, pl.ds(0, half)], grad_ref.at[pl.ds(x * images, images)], out_sem.at[1])
    grad_own.start()

    def exchange(k):
        return Far(lambda: (vec, vget.at[k]), lambda: vec_send.at[k], lambda: vec_recv.at[k], peers[k])

    def write_folds(total, ref, tile_at):
        for t in range(total.shape[1] // side_cols):
            for h in range(2):
                at = (tile_at + t) * width + h * side_cols
                ref[:, at : at + side_cols] = total[h * unit : h * unit + unit, t * side_cols : t * side_cols + side_cols]

    def write_fc2(total):
        fc2_ref[...] = total

    between = [
        [lambda: parcels[FC1_B].move(3)],
        [lambda: parcels[QUERY].move(1), lambda: parcels[KEY].move(1)],
        [lambda: parcels[VAL_PROJ].move(2)],
        [lambda: parcels[QUERY].move(2), lambda: parcels[KEY].move(2)],
        [lambda: parcels[VAL_PROJ].move(3)],
    ]
    for k in range(len(peers)):
        trade = exchange(k)
        for job in between[k]:
            job()
        trade.wait()
        vec[...] += vget[k]
    vec_ref[...] = vec[...]
    parcels[FC2_A].finish(write_fc2)
    parcels[FC2_B].finish(write_fc2)
    parcels[QUERY].move(3)
    parcels[KEY].move(3)
    write_folds(parcels[FC1_A].gather(4), fc1_ref, 0)
    write_folds(parcels[FC1_B].gather(4), fc1_ref, 2)
    for i, copy in enumerate(swaps):
        copy.wait()
        acc[i, half:] = grecv[i].astype(F32)
    grad_oth = pltpu.make_async_copy(
        acc.at[:, pl.ds(half, half)], grad_ref.at[pl.ds((1 - x) * images, images)], out_sem.at[2]
    )
    grad_oth.start()
    total = parcels[VAL_PROJ].gather(4)
    write_folds(total[:, :side_cols], qkvg_ref, 2)
    write_folds(total[:, side_cols:], projg_ref, 0)
    write_folds(parcels[QUERY].gather(4), qkvg_ref, 0)
    write_folds(parcels[KEY].gather(4), qkvg_ref, 1)
    out_own.wait()
    grad_own.wait()
    grad_oth.wait()


def rest(scal, cot_own, cot_oth, n2, middle, qkv, probs, n1, attended, x_own, x_oth, w):
    images, half, width = cot_own.shape
    rows = 2 * half
    hidden_width = w["fc1_weight"].shape[1]
    r, c = 2 * (width // GROUP), width
    fc2_rows = hidden_width // GROUP
    hbm = pl.BlockSpec(memory_space=pl.ANY)
    vmem = pl.BlockSpec(memory_space=pltpu.VMEM)
    smem = pl.BlockSpec(memory_space=pltpu.SMEM)
    dma = pltpu.SemaphoreType.DMA
    whole = lambda dtype: pltpu.VMEM((images, rows, width), dtype)
    half_block = lambda dtype: pltpu.VMEM((images, half, width), dtype)
    level_bufs = []
    for k, order in enumerate(ORDERS):
        names = "vyx" if k < 2 else "wvyx"
        block = (fc2_rows, width) if k < 2 else (r, c) if k < 5 else (r, c // 2)
        level_bufs += [pltpu.VMEM(shape, BF16) for shape in level_shapes(names, order, *block)]
    rows_of = lambda *lead: pltpu.VMEM(lead + (2, 2, 2, fc2_rows, width), BF16)
    folds_of = lambda count, cols: pltpu.VMEM((count, 2, 2, 2, 2, r, cols), BF16)
    return pl.pallas_call(
        rest_kernel,
        in_specs=[smem] + [hbm] * 14 + [vmem] * 4,
        out_specs=[vmem] * 5 + [hbm] * 2,
        out_shape=[
            jax.ShapeDtypeStruct((fc2_rows, width), F32),
            jax.ShapeDtypeStruct((r // 2, hidden_width), F32),
            jax.ShapeDtypeStruct((r // 2, 3 * width), F32),
            jax.ShapeDtypeStruct((r // 2, width), F32),
            jax.ShapeDtypeStruct((16, width), F32),
            jax.ShapeDtypeStruct((2 * images, half, width), BF16),
            jax.ShapeDtypeStruct((2 * images, half, width), F32),
        ],
        scratch_shapes=[
            whole(BF16), whole(F32), whole(F32), whole(F32), whole(BF16), whole(BF16),
            pltpu.VMEM((4, width, width), BF16),
            pltpu.VMEM((2, rows, 3 * width), BF16),
            pltpu.VMEM((SLOTS, 2, rows, rows), BF16),
            pltpu.VMEM((images, rows, 3 * width), BF16),
            whole(BF16),
            pltpu.VMEM((width, width), F32),
            half_block(BF16), half_block(BF16), half_block(BF16),
            pltpu.VMEM((16, width), F32),
            pltpu.VMEM((5, 16, width), F32),
            rows_of(2), rows_of(), rows_of(),
            folds_of(3, c), folds_of(2, c), folds_of(2, c),
            folds_of(2, c // 2), folds_of(2, c // 2), folds_of(2, c // 2),
            *level_bufs,
            dma((8,)), dma((SLOTS,)), dma((2,)), dma((4,)), dma((PARTS, 5)), dma((PARTS, 5)), dma((images + 1,)),
            dma((images + 1,)), dma((5,)), dma((5,)), dma((3,)), pltpu.SemaphoreType.REGULAR((2,)),
        ],
        compiler_params=pltpu.CompilerParams(collective_id=0, has_side_effects=True, vmem_limit_bytes=64 * MIB),
        name="rest",
    )(scal, cot_own, cot_oth, n2, middle, qkv, probs, w["fc1_weight"], w["fc2_weight"], w["proj_weight"], w["qkv_weight"],
      n1, attended, x_own, x_oth, w["ln1_gain"], w["ln2_gain"], w["fc1_bias"].reshape(-1, width), w["fc2_bias"])


def spread(value):
    return lax.psum_scatter(value, ("img", "seq"), scatter_dimension=0, tiled=True)


def unfold(send, keep, core, folds):
    rows, cols = send.shape[-2], send.shape[-1]
    send, keep = (v.reshape(GROUP // 4, 2, rows, cols) for v in (send, keep))
    both = jnp.stack([jnp.where(core == 0, keep, send), jnp.where(core == 0, send, keep)], axis=1).astype(F32)
    if folds == 1:
        return both.reshape(GROUP * rows, cols)
    tiles = 4
    both = both.reshape(GROUP, 2, rows // 2, tiles, cols // tiles)
    return both.transpose(0, 2, 3, 1, 4).reshape(GROUP * rows // 2, 2 * cols)


def swap(value, axis, bit, size):
    return lax.ppermute(value, axis, [(i, i ^ bit) for i in range(size)])


def shards(img_size, args):
    (patches, grid_shape, split_rows, owner_shard, drop_masks, ln1_gain, ln1_bias, qkv_weight, qv_bias, proj_weight,
     proj_bias, ln2_gain, ln2_bias, fc1_weight, fc1_bias, fc2_weight, fc2_bias, cotangent) = args
    all_images, _, half, width = patches.shape
    images = all_images // 2
    rows = 2 * half
    tokens = images * rows
    side = lax.axis_index("seq")
    line = lax.axis_index("img")
    owners = 2 * img_size
    row = lambda v: v.reshape(1, -1)
    w = dict(
        ln1_gain=row(ln1_gain), ln1_bias=row(ln1_bias), qkv_weight=qkv_weight, q_bias=row(qv_bias[:width]),
        v_bias=row(qv_bias[width:]), proj_weight=proj_weight, proj_bias=row(proj_bias), ln2_gain=row(ln2_gain),
        ln2_bias=row(ln2_bias), fc1_weight=fc1_weight, fc1_bias=row(fc1_bias), fc2_weight=fc2_weight, fc2_bias=row(fc2_bias),
    )

    def exchange(value):
        value = value.reshape(all_images, half, width)
        own = lax.dynamic_slice_in_dim(value, side * images, images, axis=0)
        away = lax.dynamic_slice_in_dim(value, (1 - side) * images, images, axis=0)
        return own, swap(away, "seq", 1, 2)

    x_own, x_oth = exchange(patches)
    c_own, c_oth = exchange(cotangent)

    def place(own, back):
        back = back.astype(own.dtype)
        first = jnp.where(side == 0, own, back)
        second = jnp.where(side == 0, back, own)
        return jnp.concatenate([first, second], axis=0).reshape(all_images, 1, half, width)

    def restore(own, oth):
        return place(own, swap(oth, "seq", 1, 2))

    across = grid_shape[:, 1]
    counts = jnp.stack([split_rows * across, (grid_shape[:, 0] - split_rows) * across], axis=0)
    count_own = jnp.where(side == 0, counts[0], counts[1])
    count_oth = jnp.where(side == 0, counts[1], counts[0])
    special = (owner_shard == side).astype(jnp.int32)
    table = jnp.stack([count_own, special, count_oth, 1 - special, drop_masks[:, 0], drop_masks[:, 1]], axis=1)
    scal = lax.dynamic_slice_in_dim(table, side * images, images, axis=0)

    n1, qkv, probs, attended, middle, n2 = front(scal, x_own, x_oth, w)
    flat = lambda v: v.reshape(tokens, v.shape[-1])
    unit1 = width // GROUP
    unit2 = fc2_weight.shape[0] // GROUP
    if owners == GROUP:
        fc2_grad, fc1_grad, qkv_grad, proj_grad, sums, layer_out, patches_grad = rest(
            scal, c_own, c_oth, n2, middle, qkv, probs, n1, attended, x_own, x_oth, w
        )
        layer_out = layer_out.reshape(all_images, 1, half, width)
        patches_grad = patches_grad.reshape(all_images, 1, half, width)
        owner = 2 * line + side
        pieces = []
        for at, count in ((0, 1), (1, 1), (2, 2), (4, 1), (5, 1), (6, 1), (7, 4), (11, 1)):
            vector = sums[at : at + count].reshape(-1)
            pieces.append(lax.dynamic_slice_in_dim(vector, owner * count * unit1, count * unit1))
    else:
        mine = lax.rem(line, 2).reshape(1)
        hidden, slope, out_own, out_oth = mlp(scal, flat(n2), flat(middle), w, images, 512)
        layer_out = restore(out_own, out_oth)
        dn2, s2, k2, s1, k1, fc2_bias_grad, fc1_bias_grad = mlp_back(
            scal, mine, c_own, c_oth, flat(n2), hidden, slope, w, unit1, unit2
        )
        dn2 = dn2.reshape(images, rows, width)
        d_middle, d_branch, d_join, ln2_gain_grad, ln2_bias_grad, proj_bias_grad, q_grad, v_grad = attend_back(
            scal, c_own, c_oth, dn2, middle, qkv, probs, w
        )
        st, kt, grad_own, grad_oth, ln1_gain_grad, ln1_bias_grad = tail(
            mine, flat(n1), flat(d_join), flat(attended), flat(d_branch), x_own, x_oth, flat(d_middle), w, unit1
        )
        patches_grad = restore(grad_own, grad_oth)
        vectors = (
            ln1_gain_grad, ln1_bias_grad, jnp.concatenate([q_grad, v_grad], axis=1), proj_bias_grad, ln2_gain_grad,
            ln2_bias_grad, fc1_bias_grad, fc2_bias_grad,
        )
        fc2_grad = spread(unfold(s2, k2, line % 2, 1))
        fc1_grad = spread(unfold(s1, k1, line % 2, 2))
        tail_grad = spread(unfold(st, kt, line % 2, 2))
        qkv_grad, proj_grad = tail_grad[:, : 3 * width], tail_grad[:, 3 * width :]
        pieces = [spread(v.reshape(-1)) for v in vectors]
    l1g, l1b, qvb, pjb, l2g, l2b, f1b, f2b = pieces
    return (
        layer_out, patches_grad, l1g, l1b, qkv_grad, qvb, proj_grad, pjb, l2g, l2b, fc1_grad, f1b, fc2_grad, f2b,
    )


def solution(mesh):
    rep = [P()] * 12
    vec = P(("img", "seq"))
    mat = P(("img", "seq"), None)
    rows = P("img", "seq", None, None)

    def run(*args):
        return shards(mesh.shape["img"], args)

    return jax.shard_map(
        run,
        mesh=mesh,
        in_specs=(rows, P("img", None), P("img"), P("img"), P("img", None), *rep, rows),
        out_specs=(rows, rows, vec, vec, mat, vec, mat, vec, vec, vec, mat, vec, mat, vec),
        check_vma=False,
    )
```

```python
import functools

import jax
import jax.numpy as jnp
from jax import lax
from jax.experimental import pallas as pl
from jax.experimental.pallas import tpu as pltpu
from jax.sharding import PartitionSpec as P

HEAD_DIM = 64
LN_EPS = 1e-06
KEEP_SCALE = 1.0 / 0.9
MASK_FILL = -1e30
BF16 = jnp.bfloat16
F32 = jnp.float32
MIB = 1024 * 1024


def dot_nn(a, b):
    return lax.dot_general(a, b, (((1,), (0,)), ((), ())), preferred_element_type=F32)


def dot_nt(a, b):
    return lax.dot_general(a, b, (((1,), (1,)), ((), ())), preferred_element_type=F32)


def dot_tn(a, b):
    return lax.dot_general(a, b, (((0,), (0,)), ((), ())), preferred_element_type=F32)


def norm_parts(values):
    row_mean = jnp.mean(values, axis=-1, keepdims=True)
    centred = values - row_mean
    variance = jnp.mean(centred * centred, axis=-1, keepdims=True)
    rstd = lax.rsqrt(variance + LN_EPS)
    return centred * rstd, rstd


def norm_back(d_normed, gain, unit, rstd):
    d_unit = d_normed * gain
    mean_one = jnp.mean(d_unit, axis=-1, keepdims=True)
    mean_two = jnp.mean(d_unit * unit, axis=-1, keepdims=True)
    return rstd * (d_unit - mean_one - unit * mean_two)


def gelu_both(values):
    cdf = 0.5 + 0.5 * lax.erf(values * 0.7071067811865476)
    return values * cdf, cdf + values * (0.3989422804014327 * jnp.exp(-0.5 * values * values))


class Facts:
    def __init__(self, refs, images, x):
        self.grid, self.split, self.owner, self.drop = refs
        self.images, self.x = images, x

    def __getitem__(self, key):
        image, k = key
        at = self.x * self.images + image
        if k >= 4:
            return self.drop[at, k - 4]
        if k % 2 == 1:
            own = (self.owner[at] == self.x).astype(jnp.int32)
            return own if k == 1 else 1 - own
        across = self.grid[at, 1]
        first = self.split[at] * across
        second = (self.grid[at, 0] - self.split[at]) * across
        return jnp.where(self.x == k // 2, first, second)


def row_valid(scal_ref, image, rows, half, axis):
    shape = (rows, 1) if axis == 0 else (1, rows)
    slot = lax.broadcasted_iota(jnp.int32, shape, axis)
    other = slot >= half
    place = jnp.where(other, slot - half, slot)
    count = jnp.where(other, scal_ref[image, 2], scal_ref[image, 0])
    special = jnp.where(other, scal_ref[image, 3], scal_ref[image, 1])
    return jnp.where(place < 2, special, (place - 2 < count).astype(jnp.int32)) > 0


def front_kernel(
    scal_ref, own_ref, oth_ref, g1_ref, b1_ref, wqkv_ref, qb_ref, vb_ref, wp_ref, pb_ref, g2_ref, b2_ref,
    n1_ref, qkv_ref, probs_ref, att_ref, mid_ref, n2_ref,
):
    image = pl.program_id(0)
    half, width = own_ref.shape[1], own_ref.shape[2]
    rows = 2 * half
    x = jnp.concatenate([own_ref[0].astype(F32), oth_ref[0].astype(F32)], axis=0)
    unit, _ = norm_parts(x)
    n1 = (unit * g1_ref[...] + b1_ref[...]).astype(BF16)
    n1_ref[0] = n1
    qkv_ref[0, :, :width] = ((dot_nn(n1, wqkv_ref[:, :width]) + qb_ref[...]).astype(BF16) * BF16(HEAD_DIM**-0.5))
    qkv_ref[0, :, width : 2 * width] = dot_nn(n1, wqkv_ref[:, width : 2 * width]).astype(BF16)
    qkv_ref[0, :, 2 * width :] = (dot_nn(n1, wqkv_ref[:, 2 * width :]) + vb_ref[...]).astype(BF16)
    fill = jnp.where(row_valid(scal_ref, image, rows, half, 0), 0.0, MASK_FILL)
    low_lane = lax.broadcasted_iota(jnp.int32, (rows, 128), 1) < HEAD_DIM
    for pair in range(width // 128):
        cut = slice(128 * pair, 128 * pair + 128)
        q2 = qkv_ref[0, :, cut]
        k2 = qkv_ref[0, :, width + 128 * pair : width + 128 * pair + 128]
        v2 = qkv_ref[0, :, 2 * width + 128 * pair : 2 * width + 128 * pair + 128]
        total = None
        for side in range(2):
            mine = low_lane if side == 0 else jnp.logical_not(low_lane)
            scores = dot_nt(k2, jnp.where(mine, q2, 0)) + fill
            top = jnp.max(scores, axis=0, keepdims=True)
            weight = jnp.exp(scores - top)
            probs = (weight * (1.0 / jnp.sum(weight, axis=0, keepdims=True))).astype(BF16)
            probs_ref[0, 2 * pair + side] = probs
            part = dot_tn(probs, jnp.where(mine, v2, 0))
            total = part if total is None else total + part
        att_ref[0, :, cut] = total.astype(BF16)
    keep = scal_ref[image, 4].astype(F32) * KEEP_SCALE
    branch = dot_nn(att_ref[0], wp_ref[...]) + pb_ref[...]
    middle = jnp.concatenate([own_ref[0].astype(F32), oth_ref[0].astype(F32)], axis=0) + keep * branch
    mid_ref[0] = middle
    unit, _ = norm_parts(middle)
    n2_ref[0] = (unit * g2_ref[...] + b2_ref[...]).astype(BF16)


def full(shape):
    zeros = (0,) * len(shape)
    return pl.BlockSpec(shape, lambda *_: zeros, pipeline_mode=pl.Buffered(1))


def front(scal, own, oth, w):
    images, half, width = own.shape
    rows = 2 * half
    heads = width // HEAD_DIM
    per = lambda *tail: pl.BlockSpec((1,) + tail, lambda i, s: (i,) + (0,) * len(tail))
    flops = 2 * images * rows * width * (4 * width + 4 * rows)
    return pl.pallas_call(
        front_kernel,
        grid_spec=pltpu.PrefetchScalarGridSpec(
            num_scalar_prefetch=1,
            grid=(images,),
            in_specs=[
                per(half, width), per(half, width), full((1, width)), full((1, width)),
                full((width, 3 * width)), full((1, width)), full((1, width)),
                full((width, width)), full((1, width)), full((1, width)), full((1, width)),
            ],
            out_specs=[
                per(rows, width), per(rows, 3 * width), per(heads, rows, rows),
                per(rows, width), per(rows, width), per(rows, width),
            ],
        ),
        out_shape=[
            jax.ShapeDtypeStruct((images, rows, width), BF16),
            jax.ShapeDtypeStruct((images, rows, 3 * width), BF16),
            jax.ShapeDtypeStruct((images, heads, rows, rows), BF16),
            jax.ShapeDtypeStruct((images, rows, width), BF16),
            jax.ShapeDtypeStruct((images, rows, width), F32),
            jax.ShapeDtypeStruct((images, rows, width), BF16),
        ],
        compiler_params=pltpu.CompilerParams(vmem_limit_bytes=56 * MIB),
        cost_estimate=pl.CostEstimate(flops=flops, transcendentals=images * heads * rows * rows, bytes_accessed=30_000_000),
        name="front",
    )(scal, own, oth, w["ln1_gain"], w["ln1_bias"], w["qkv_weight"], w["q_bias"], w["v_bias"],
      w["proj_weight"], w["proj_bias"], w["ln2_gain"], w["ln2_bias"])


def mlp_kernel(
    scal_ref, n2_ref, mid_ref, w1_ref, c1_ref, w2_ref, c2_ref,
    hid_ref, slope_ref, own_ref, oth_ref, acc_ref,
):
    step = pl.program_id(0)
    images, half, width = own_ref.shape
    rows = 2 * half
    hidden, slope = gelu_both(dot_nn(n2_ref[...], w1_ref[...]) + c1_ref[...])
    hidden = hidden.astype(BF16)
    hid_ref[...] = hidden
    slope_ref[...] = slope.astype(BF16)
    part = dot_nn(hidden, w2_ref[...])

    @pl.when(step == 0)
    def _():
        acc_ref[...] = part

    @pl.when(step > 0)
    def _():
        acc_ref[...] += part

    @pl.when(step == pl.num_programs(0) - 1)
    def _():
        for image in range(images):
            keep = scal_ref[image, 5].astype(F32) * KEEP_SCALE
            cut = slice(rows * image, rows * image + rows)
            final = mid_ref[cut, :] + keep * (acc_ref[cut, :] + c2_ref[...])
            out = jnp.where(row_valid(scal_ref, image, rows, half, 0), final, 0.0).astype(BF16)
            own_ref[image] = out[:half]
            oth_ref[image] = out[half:]


def mlp(scal, n2, middle, w, images, tile):
    tokens, width = n2.shape
    hidden_width = w["fc1_weight"].shape[1]
    half = tokens // images // 2
    return pl.pallas_call(
        mlp_kernel,
        grid_spec=pltpu.PrefetchScalarGridSpec(
            num_scalar_prefetch=1,
            grid=(hidden_width // tile,),
            in_specs=[
                full((tokens, width)), full((tokens, width)),
                pl.BlockSpec((width, tile), lambda j, s: (0, j)), pl.BlockSpec((1, tile), lambda j, s: (0, j)),
                pl.BlockSpec((tile, width), lambda j, s: (j, 0)), full((1, width)),
            ],
            out_specs=[
                pl.BlockSpec((tokens, tile), lambda j, s: (0, j)), pl.BlockSpec((tokens, tile), lambda j, s: (0, j)),
                full((images, half, width)), full((images, half, width)),
            ],
            scratch_shapes=[pltpu.VMEM((tokens, width), F32)],
        ),
        out_shape=[
            jax.ShapeDtypeStruct((tokens, hidden_width), BF16),
            jax.ShapeDtypeStruct((tokens, hidden_width), BF16),
            jax.ShapeDtypeStruct((images, half, width), BF16),
            jax.ShapeDtypeStruct((images, half, width), BF16),
        ],
        compiler_params=pltpu.CompilerParams(vmem_limit_bytes=56 * MIB),
        cost_estimate=pl.CostEstimate(flops=4 * tokens * width * hidden_width, transcendentals=2 * tokens * hidden_width, bytes_accessed=30_000_000),
        name="mlp",
    )(scal, n2, middle, w["fc1_weight"], w["fc1_bias"], w["fc2_weight"], w["fc2_bias"])


def put_rows(grad_ref, value, send_ref, keep_ref, mine, lead):
    grad_ref[...] = value
    run = 2 * send_ref.shape[-2]
    for k in range(grad_ref.shape[0] // (2 * run)):
        for ref, core in ((send_ref, 1 - mine), (keep_ref, mine)):
            for x in range(2):
                at = pl.multiple_of((2 * k + core) * run + x * (run // 2), 8)
                ref[lead + (k, x)] = grad_ref[pl.ds(at, run // 2), :].astype(BF16)


def put_folded(grad_ref, value, send_ref, keep_ref, mine):
    grad_ref[...] = value
    unit = send_ref.shape[-2] // 2
    side = grad_ref.shape[1] // 2
    for k in range(grad_ref.shape[0] // (4 * unit)):
        for ref, core in ((send_ref, 1 - mine), (keep_ref, mine)):
            for x in range(2):
                at = pl.multiple_of((4 * k + 2 * core + x) * unit, 8)
                piece = grad_ref[pl.ds(at, unit), :]
                ref[k, x] = jnp.concatenate([piece[:, :side], piece[:, side:]], axis=0).astype(BF16)


def mlp_back_kernel(
    scal_ref, mine_ref, own_ref, oth_ref, n2_ref, hid_ref, slope_ref, w1_ref, w2_ref,
    dn2_ref, s2_ref, k2_ref, s1_ref, k1_ref, c2_ref, c1_ref, dmlp_ref, grad_ref, acc_ref,
):
    step = pl.program_id(0)
    images, half, width = own_ref.shape
    rows = 2 * half
    mine = mine_ref[0]

    @pl.when(step == 0)
    def _():
        total = jnp.zeros((1, width), F32)
        for image in range(images):
            keep = scal_ref[image, 5].astype(F32) * KEEP_SCALE
            cot = jnp.concatenate([own_ref[image].astype(F32), oth_ref[image].astype(F32)], axis=0)
            live = row_valid(scal_ref, image, rows, half, 0)
            d_mlp = (jnp.where(live, cot, 0.0) * keep).astype(BF16)
            dmlp_ref[rows * image : rows * image + rows, :] = d_mlp
            total += jnp.sum(d_mlp.astype(F32), axis=0, keepdims=True)
        c2_ref[...] = total

    d_pre = slope_ref[...].astype(F32) * dot_nt(dmlp_ref[...], w2_ref[...])
    d_pre = d_pre.astype(BF16)
    c1_ref[...] = jnp.sum(d_pre.astype(F32), axis=0, keepdims=True)
    part = dot_nt(d_pre, w1_ref[...])
    put_folded(grad_ref, dot_tn(n2_ref[...], d_pre), s1_ref, k1_ref, mine)
    put_rows(grad_ref, dot_tn(hid_ref[...], dmlp_ref[...]), s2_ref, k2_ref, mine, (0,))

    @pl.when(step == 0)
    def _():
        acc_ref[...] = part

    @pl.when(step > 0)
    def _():
        acc_ref[...] += part

    @pl.when(step == pl.num_programs(0) - 1)
    def _():
        dn2_ref[...] = acc_ref[...]


def mlp_back(scal, mine, own, oth, n2, hidden, slope, w, unit1, unit2):
    tokens, width = n2.shape
    images, half, _ = own.shape
    hidden_width = hidden.shape[1]
    tile = width
    steps = hidden_width // tile
    runs1, runs2 = width // (4 * unit1), tile // (4 * unit2)
    col = pl.BlockSpec((tokens, tile), lambda j, s, m: (0, j))
    half1 = pl.BlockSpec((runs1, 2, 2 * unit1, tile // 2), lambda j, s, m: (0, 0, 0, j))
    half2 = pl.BlockSpec((1, runs2, 2, unit2, width), lambda j, s, m: (j, 0, 0, 0, 0))
    return pl.pallas_call(
        mlp_back_kernel,
        grid_spec=pltpu.PrefetchScalarGridSpec(
            num_scalar_prefetch=2,
            grid=(steps,),
            in_specs=[
                full((images, half, width)), full((images, half, width)), full((tokens, width)), col, col,
                pl.BlockSpec((width, tile), lambda j, s, m: (0, j)), pl.BlockSpec((tile, width), lambda j, s, m: (j, 0)),
            ],
            out_specs=[
                full((tokens, width)), half2, half2, half1, half1,
                full((1, width)), pl.BlockSpec((1, tile), lambda j, s, m: (0, j)),
            ],
            scratch_shapes=[
                pltpu.VMEM((tokens, width), BF16), pltpu.VMEM((width, width), F32), pltpu.VMEM((tokens, width), F32),
            ],
        ),
        out_shape=[
            jax.ShapeDtypeStruct((tokens, width), F32),
            jax.ShapeDtypeStruct((steps, runs2, 2, unit2, width), BF16),
            jax.ShapeDtypeStruct((steps, runs2, 2, unit2, width), BF16),
            jax.ShapeDtypeStruct((runs1, 2, 2 * unit1, hidden_width // 2), BF16),
            jax.ShapeDtypeStruct((runs1, 2, 2 * unit1, hidden_width // 2), BF16),
            jax.ShapeDtypeStruct((1, width), F32),
            jax.ShapeDtypeStruct((1, hidden_width), F32),
        ],
        compiler_params=pltpu.CompilerParams(vmem_limit_bytes=58 * MIB),
        cost_estimate=pl.CostEstimate(flops=8 * tokens * width * hidden_width, transcendentals=0, bytes_accessed=35_000_000),
        name="mlp_back",
    )(scal, mine, own, oth, n2, hidden, slope, w["fc1_weight"], w["fc2_weight"])


def attend_back_kernel(
    scal_ref, own_ref, oth_ref, dn2_ref, mid_ref, qkv_ref, probs_ref, wp_ref, g2_ref,
    dmid_ref, dbr_ref, djoin_ref, g2g_ref, g2b_ref, pbg_ref, qbg_ref, vbg_ref, datt_ref,
):
    image = pl.program_id(0)
    half, width = own_ref.shape[1], own_ref.shape[2]
    rows = 2 * half
    live = row_valid(scal_ref, image, rows, half, 0)
    d_final = jnp.where(live, jnp.concatenate([own_ref[0].astype(F32), oth_ref[0].astype(F32)], axis=0), 0.0)
    unit, rstd = norm_parts(mid_ref[0])
    dn2 = dn2_ref[0]
    gain_part = jnp.sum(dn2 * unit, axis=0, keepdims=True)
    bias_part = jnp.sum(dn2, axis=0, keepdims=True)
    d_middle = d_final + norm_back(dn2, g2_ref[...], unit, rstd)
    dmid_ref[0] = d_middle
    keep = scal_ref[image, 4].astype(F32) * KEEP_SCALE
    d_branch = (d_middle * keep).astype(BF16)
    dbr_ref[0] = d_branch
    proj_part = jnp.sum(d_branch.astype(F32), axis=0, keepdims=True)
    datt_ref[...] = dot_nt(d_branch, wp_ref[...]).astype(BF16)
    low_lane = lax.broadcasted_iota(jnp.int32, (rows, 128), 1) < HEAD_DIM
    for pair in range(width // 128):
        cut = slice(128 * pair, 128 * pair + 128)
        q2 = qkv_ref[0, :, cut]
        k2 = qkv_ref[0, :, width + 128 * pair : width + 128 * pair + 128]
        v2 = qkv_ref[0, :, 2 * width + 128 * pair : 2 * width + 128 * pair + 128]
        a2 = datt_ref[:, cut]
        dq = dk = dv = None
        for side in range(2):
            mine = low_lane if side == 0 else jnp.logical_not(low_lane)
            probs_low = probs_ref[0, 2 * pair + side]
            probs = probs_low.astype(F32)
            a_side = jnp.where(mine, a2, 0)
            d_probs = dot_nt(v2, a_side)
            inner = jnp.sum(probs * d_probs, axis=0, keepdims=True)
            d_scores = (probs * (d_probs - inner)).astype(BF16)
            dq_part = dot_tn(d_scores, jnp.where(mine, k2, 0))
            dk_part = dot_nn(d_scores, jnp.where(mine, q2, 0))
            dv_part = dot_nn(probs_low, a_side)
            dq = dq_part if dq is None else dq + dq_part
            dk = dk_part if dk is None else dk + dk_part
            dv = dv_part if dv is None else dv + dv_part
        djoin_ref[0, :, cut] = (dq * HEAD_DIM**-0.5).astype(BF16)
        djoin_ref[0, :, width + 128 * pair : width + 128 * pair + 128] = dk.astype(BF16)
        djoin_ref[0, :, 2 * width + 128 * pair : 2 * width + 128 * pair + 128] = dv.astype(BF16)
    q_part = jnp.sum(djoin_ref[0, :, :width].astype(F32), axis=0, keepdims=True)
    v_part = jnp.sum(djoin_ref[0, :, 2 * width :].astype(F32), axis=0, keepdims=True)
    sums = ((g2g_ref, gain_part), (g2b_ref, bias_part), (pbg_ref, proj_part), (qbg_ref, q_part), (vbg_ref, v_part))

    @pl.when(image == 0)
    def _():
        for ref, part in sums:
            ref[...] = part

    @pl.when(image > 0)
    def _():
        for ref, part in sums:
            ref[...] += part


def attend_back(scal, own, oth, dn2, middle, qkv, probs, w):
    images, half, width = own.shape
    rows = 2 * half
    heads = width // HEAD_DIM
    per = lambda *tail: pl.BlockSpec((1,) + tail, lambda i, s: (i,) + (0,) * len(tail))
    vec = jax.ShapeDtypeStruct((1, width), F32)
    return pl.pallas_call(
        attend_back_kernel,
        grid_spec=pltpu.PrefetchScalarGridSpec(
            num_scalar_prefetch=1,
            grid=(images,),
            in_specs=[
                per(half, width), per(half, width), per(rows, width), per(rows, width), per(rows, 3 * width),
                per(heads, rows, rows), full((width, width)), full((1, width)),
            ],
            out_specs=[per(rows, width), per(rows, width), per(rows, 3 * width)] + [full((1, width))] * 5,
            scratch_shapes=[pltpu.VMEM((rows, width), BF16)],
        ),
        out_shape=[
            jax.ShapeDtypeStruct((images, rows, width), F32),
            jax.ShapeDtypeStruct((images, rows, width), BF16),
            jax.ShapeDtypeStruct((images, rows, 3 * width), BF16),
            vec, vec, vec, vec, vec,
        ],
        compiler_params=pltpu.CompilerParams(vmem_limit_bytes=56 * MIB),
        cost_estimate=pl.CostEstimate(flops=2 * images * rows * width * (width + 8 * rows), transcendentals=0, bytes_accessed=35_000_000),
        name="attend_back",
    )(scal, own, oth, dn2, middle, qkv, probs, w["proj_weight"], w["ln2_gain"])


def tail_kernel(
    mine_ref, n1_ref, djoin_ref, att_ref, dbr_ref, wqkv_ref, xo_ref, xt_ref, dmid_ref, g1_ref,
    send_ref, keep_ref, go_ref, gt_ref, g1g_ref, g1b_ref, grad_ref, acc_ref,
):
    step = pl.program_id(0)
    last = pl.num_programs(0) - 1
    images, half, width = xo_ref.shape
    rows = 2 * half
    mine = mine_ref[0]

    @pl.when(step < last)
    def _():
        put_folded(grad_ref, dot_tn(n1_ref[...], djoin_ref[...]), send_ref, keep_ref, mine)
        part = dot_nt(djoin_ref[...], wqkv_ref[...])

        @pl.when(step == 0)
        def _():
            acc_ref[...] = part

        @pl.when(step > 0)
        def _():
            acc_ref[...] += part

    @pl.when(step == last)
    def _():
        put_folded(grad_ref, dot_tn(att_ref[...], dbr_ref[...]), send_ref, keep_ref, mine)
        gain_sum = jnp.zeros((1, width), F32)
        bias_sum = jnp.zeros((1, width), F32)
        for image in range(images):
            x = jnp.concatenate([xo_ref[image].astype(F32), xt_ref[image].astype(F32)], axis=0)
            unit, rstd = norm_parts(x)
            dn1 = acc_ref[rows * image : rows * image + rows, :]
            gain_sum += jnp.sum(dn1 * unit, axis=0, keepdims=True)
            bias_sum += jnp.sum(dn1, axis=0, keepdims=True)
            out = dmid_ref[rows * image : rows * image + rows, :] + norm_back(dn1, g1_ref[...], unit, rstd)
            go_ref[image] = out[:half]
            gt_ref[image] = out[half:].astype(BF16)
        g1g_ref[...] = gain_sum
        g1b_ref[...] = bias_sum


def tail(mine, n1, d_join, attended, d_branch, own, oth, d_middle, w, unit):
    tokens, width = n1.shape
    images, half, _ = own.shape
    runs = width // (4 * unit)
    halves = pl.BlockSpec((runs, 2, 2 * unit, width // 2), lambda j, m: (0, 0, 0, j))
    clip = lambda j: jnp.minimum(j, 2)
    return pl.pallas_call(
        tail_kernel,
        grid_spec=pltpu.PrefetchScalarGridSpec(
            num_scalar_prefetch=1,
            grid=(4,),
            in_specs=[
                full((tokens, width)), pl.BlockSpec((tokens, width), lambda j, m: (0, clip(j))), full((tokens, width)),
                full((tokens, width)), pl.BlockSpec((width, width), lambda j, m: (0, clip(j))),
                full((images, half, width)), full((images, half, width)), full((tokens, width)), full((1, width)),
            ],
            out_specs=[
                halves, halves, full((images, half, width)), full((images, half, width)),
                full((1, width)), full((1, width)),
            ],
            scratch_shapes=[pltpu.VMEM((width, width), F32), pltpu.VMEM((tokens, width), F32)],
        ),
        out_shape=[
            jax.ShapeDtypeStruct((runs, 2, 2 * unit, 2 * width), BF16),
            jax.ShapeDtypeStruct((runs, 2, 2 * unit, 2 * width), BF16),
            jax.ShapeDtypeStruct((images, half, width), F32),
            jax.ShapeDtypeStruct((images, half, width), BF16),
            jax.ShapeDtypeStruct((1, width), F32),
            jax.ShapeDtypeStruct((1, width), F32),
        ],
        compiler_params=pltpu.CompilerParams(vmem_limit_bytes=56 * MIB),
        cost_estimate=pl.CostEstimate(flops=14 * tokens * width * width, transcendentals=0, bytes_accessed=35_000_000),
        name="tail",
    )(mine, n1, d_join, attended, d_branch, w["qkv_weight"], own, oth, d_middle, w["ln1_gain"])


def open_kernel(
    grid_ref, split_ref, owner_ref, drop_ref, patches_ref, cot_ref, g1_ref, b1_ref, qv_ref, pb_ref, g2_ref, b2_ref, c1_ref, c2_ref, wqkv_hbm, wp_hbm,
    unit_ref, rstd_ref, qkv_ref, probs_ref, att_ref, mid_ref, n2_ref, rows_ref, cot_oth,
    xbuf, wqkv_ref, wp_ref, load_sem, send_sem, recv_sem,
):
    image = pl.program_id(0)
    images, rows, width = xbuf.shape
    half = rows // 2
    line = lax.axis_index("img")
    x_at = lax.axis_index("seq")
    across = (line, 1 - x_at)
    scal_ref = Facts((grid_ref, split_ref, owner_ref, drop_ref), images, x_at)
    loads = [
        pltpu.make_async_copy(wqkv_hbm, wqkv_ref, load_sem.at[0]),
        pltpu.make_async_copy(wp_hbm, wp_ref, load_sem.at[1]),
    ]

    def own_copy(i):
        return pltpu.make_async_copy(patches_ref.at[x_at * images + i], xbuf.at[i, pl.ds(0, half)], load_sem.at[2 + i])

    def far_copy(i):
        return pltpu.make_async_remote_copy(
            src_ref=patches_ref.at[(1 - x_at) * images + i], dst_ref=xbuf.at[i, pl.ds(half, half)],
            send_sem=send_sem.at[i], recv_sem=recv_sem.at[i], device_id=across, device_id_type=MESH,
        )

    def cot_copy():
        return pltpu.make_async_remote_copy(
            src_ref=cot_ref.at[pl.ds((1 - x_at) * images, images)], dst_ref=cot_oth,
            send_sem=send_sem.at[images], recv_sem=recv_sem.at[images], device_id=across, device_id_type=MESH,
        )

    @pl.when(image == 0)
    def _():
        barrier = pltpu.get_barrier_semaphore()
        pl.semaphore_signal(barrier, inc=1, device_id=across, device_id_type=MESH)
        own_copy(0).start()
        loads[0].start()
        pl.semaphore_wait(barrier, 1)
        for i in range(images):
            far_copy(i).start()
        for i in range(1, images):
            own_copy(i).start()
        loads[1].start()
        row = lambda ref: ref[...].reshape(1, -1)
        rows_ref[...] = jnp.zeros_like(rows_ref)
        for k in range(c1_ref.shape[0] // width):
            rows_ref[k : k + 1, :] = row(c1_ref)[:, k * width : k * width + width]
        for k, ref in enumerate((c2_ref, g1_ref, b1_ref, g2_ref, b2_ref, pb_ref)):
            rows_ref[4 + k : 5 + k, :] = row(ref)
        rows_ref[10:11, :] = row(qv_ref)[:, :width]
        rows_ref[11:12, :] = row(qv_ref)[:, width:]
        loads[0].wait()
        loads[1].wait()

    for i in range(images):

        @pl.when(image == i)
        def _():
            own_copy(i).wait()
            far_copy(i).wait()

    @pl.when(image == 1)
    def _():
        cot_copy().start()

    vector = lambda k: rows_ref[k : k + 1, :]
    unit, rstd = norm_parts(xbuf[image].astype(F32))
    unit_ref[0] = unit.astype(BF16)
    rstd_ref[0] = rstd
    n1 = (unit * vector(5) + vector(6)).astype(BF16)
    qkv_ref[0, :, :width] = ((dot_nn(n1, wqkv_ref[:, :width]) + vector(10)).astype(BF16) * BF16(HEAD_DIM**-0.5))
    qkv_ref[0, :, width : 2 * width] = dot_nn(n1, wqkv_ref[:, width : 2 * width]).astype(BF16)
    qkv_ref[0, :, 2 * width :] = (dot_nn(n1, wqkv_ref[:, 2 * width :]) + vector(11)).astype(BF16)
    fill = jnp.where(row_valid(scal_ref, image, rows, half, 0), 0.0, MASK_FILL)
    low_lane = lax.broadcasted_iota(jnp.int32, (rows, 128), 1) < HEAD_DIM
    for pair in range(width // 128):
        cut, k_cut, v_cut = (slice(k * width + 128 * pair, k * width + 128 * pair + 128) for k in range(3))
        q2, k2, v2 = qkv_ref[0, :, cut], qkv_ref[0, :, k_cut], qkv_ref[0, :, v_cut]
        total = None
        for side in range(2):
            mine = low_lane if side == 0 else jnp.logical_not(low_lane)
            scores = dot_nt(k2, jnp.where(mine, q2, 0)) + fill
            top = jnp.max(scores, axis=0, keepdims=True)
            weight = jnp.exp(scores - top)
            probs = (weight * (1.0 / jnp.sum(weight, axis=0, keepdims=True))).astype(BF16)
            probs_ref[0, 2 * pair + side] = probs
            part = dot_tn(probs, jnp.where(mine, v2, 0))
            total = part if total is None else total + part
        att_ref[0, :, cut] = total.astype(BF16)
    keep = scal_ref[image, 4].astype(F32) * KEEP_SCALE
    middle = xbuf[image].astype(F32) + keep * (dot_nn(att_ref[0], wp_ref[...]) + vector(9))
    mid_ref[0] = middle
    unit, _ = norm_parts(middle)
    n2_ref[0] = (unit * vector(7) + vector(8)).astype(BF16)

    @pl.when(image == images - 1)
    def _():
        cot_copy().wait()


def opening(facts, patches, cotangent, args):
    all_images, half, width = patches.shape
    images = all_images // 2
    rows = 2 * half
    heads = width // HEAD_DIM
    per = lambda *tail: pl.BlockSpec((1,) + tail, lambda i: (i,) + (0,) * len(tail))
    hbm = pl.BlockSpec(memory_space=pl.ANY)
    vmem = pl.BlockSpec(memory_space=pltpu.VMEM)
    dma = pltpu.SemaphoreType.DMA
    shape = jax.ShapeDtypeStruct
    return pl.pallas_call(
        open_kernel,
        grid=(images,),
        in_specs=[pl.BlockSpec(memory_space=pltpu.SMEM)] * 4 + [hbm, hbm] + [vmem] * 8 + [hbm, hbm],
        out_specs=[
            per(rows, width), per(rows, 1), per(rows, 3 * width), per(heads, rows, rows), per(rows, width),
            per(rows, width), per(rows, width), vmem, hbm,
        ],
        out_shape=[
            shape((images, rows, width), BF16), shape((images, rows, 1), F32), shape((images, rows, 3 * width), BF16),
            shape((images, heads, rows, rows), BF16), shape((images, rows, width), BF16), shape((images, rows, width), F32),
            shape((images, rows, width), BF16), shape((16, width), F32), shape((images, half, width), BF16),
        ],
        scratch_shapes=[
            pltpu.VMEM((images, rows, width), BF16), pltpu.VMEM((width, 3 * width), BF16), pltpu.VMEM((width, width), BF16),
            dma((2 + images,)), dma((images + 1,)), dma((images + 1,)),
        ],
        compiler_params=pltpu.CompilerParams(collective_id=1, has_side_effects=True, vmem_limit_bytes=63 * MIB),
        name="opening",
    )(*facts, patches, cotangent, *args)


def emit_kernel(
    fc2_ref, fc1_ref, u_ref, proj_ref, sums_ref, rows_ref, w_ref, own_ref, back_ref, lo_ref,
    out_ref, grad_ref, l1g, l1b, qkvg, qvb, projg, pjb, l2g, l2b, fc1g, f1b, fc2g, f2b, buf, own_buf, back_buf, lo_buf, sems,
):
    side = lax.axis_index("seq")
    owner = 2 * lax.axis_index("img") + side
    images, half, width = own_ref.shape
    unit = u_ref.shape[0]
    arrivals = [
        pltpu.make_async_copy(back_ref, back_buf, sems.at[0]), pltpu.make_async_copy(own_ref, own_buf, sems.at[1]),
        pltpu.make_async_copy(lo_ref, lo_buf, sems.at[2]),
    ]
    for copy in arrivals:
        copy.start()
    arrivals[0].wait()
    buf[...] = back_buf[...].astype(F32)
    other = pltpu.make_async_copy(buf, grad_ref.at[pl.ds((1 - side) * images, images)], sems.at[0])
    other.start()
    arrivals[1].wait()
    mine = pltpu.make_async_copy(own_buf, grad_ref.at[pl.ds(side * images, images)], sems.at[1])
    mine.start()
    arrivals[2].wait()
    keep = pltpu.make_async_copy(lo_buf, out_ref, sems.at[2])
    keep.start()
    fc2g[...] = fc2_ref[...]
    fc1g[...] = fc1_ref[...]
    projg[...] = proj_ref[...]
    lane = lax.broadcasted_iota(jnp.int32, (unit, width), 1)
    slot = lax.broadcasted_iota(jnp.int32, (unit, width), 0)
    here = lane == owner * unit + slot
    column = lambda k: jnp.sum(jnp.where(here, rows_ref[k : k + 1, :], 0.0), axis=1, keepdims=True)
    gain, bias = column(5), column(6)
    gain_sum = bias_sum = 0.0
    for k, at in enumerate((2, 0, 3)):
        cut = slice(k * width, k * width + width)
        total, weight, sums = u_ref[:, cut], w_ref[:, cut].astype(F32), sums_ref[at : at + 1, :]
        qkvg[:, cut] = gain * total + bias * sums
        gain_sum += jnp.sum(weight * total, axis=1, keepdims=True)
        bias_sum += jnp.sum(weight * sums, axis=1, keepdims=True)
    diag = lax.broadcasted_iota(jnp.int32, (unit, 128), 1) == lax.broadcasted_iota(jnp.int32, (unit, 128), 0)
    for ref, value in ((l1g, gain_sum), (l1b, bias_sum)):
        ref[...] = jnp.sum(jnp.where(diag, value, 0.0), axis=0, keepdims=True)[0, :unit]
    for ref, at, count in ((pjb, 4, 1), (l2g, 5, 1), (l2b, 6, 1), (f2b, 11, 1), (f1b, 7, 4), (qvb, 2, 2)):
        size = unit * count
        place = owner * size
        which, start = place // width, place % width
        row = sums_ref[at : at + 1, :]
        for k in range(1, count):
            row = jnp.where(which == k, sums_ref[at + k : at + k + 1, :], row)
        sel = lax.broadcasted_iota(jnp.int32, (size, width), 1) == start + lax.broadcasted_iota(jnp.int32, (size, width), 0)
        tall = jnp.sum(jnp.where(sel, row, 0.0), axis=1, keepdims=True)
        eye = lax.broadcasted_iota(jnp.int32, (size, 128), 1) == lax.broadcasted_iota(jnp.int32, (size, 128), 0)
        ref[...] = jnp.sum(jnp.where(eye, tall, 0.0), axis=0, keepdims=True)[0, :size]
    keep.wait()
    mine.wait()
    other.wait()


def emit(fc2, fc1, u, proj, sums, rows, qkv_weight, own, back, layer_out):
    images, half, width = own.shape
    unit = u.shape[0]
    hbm = pl.BlockSpec(memory_space=pl.ANY)
    whole = lambda v: pl.BlockSpec(v.shape, lambda i: (0,) * len(v.shape))
    shape = lambda *dims: jax.ShapeDtypeStruct(dims, F32)
    outs = [
        shape(unit), shape(unit), shape(unit, 3 * width), shape(2 * unit), shape(unit, width), shape(unit), shape(unit),
        shape(unit), shape(*fc1.shape), shape(fc1.shape[1] // GROUP), shape(*fc2.shape), shape(unit),
    ]
    return pl.pallas_call(
        emit_kernel,
        grid=(1,),
        in_specs=[whole(v) for v in (fc2, fc1, u, proj, sums, rows)]
        + [pl.BlockSpec((unit, 3 * width), lambda i: (2 * lax.axis_index("img") + lax.axis_index("seq"), 0)), hbm, hbm, hbm],
        out_specs=[hbm, hbm] + [whole(v) for v in outs],
        scratch_shapes=[
            pltpu.VMEM(own.shape, F32), pltpu.VMEM(own.shape, F32), pltpu.VMEM(back.shape, BF16),
            pltpu.VMEM(layer_out.shape, BF16), pltpu.SemaphoreType.DMA((3,)),
        ],
        out_shape=[jax.ShapeDtypeStruct(layer_out.shape, BF16), shape(2 * images, half, width)] + outs,
        compiler_params=pltpu.CompilerParams(vmem_limit_bytes=63 * MIB),
        name="emit",
    )(fc2, fc1, u, proj, sums, rows, qkv_weight, own, back, layer_out)


MESH = pl.DeviceIdType.MESH
PARTS = 7
SLOTS = 3
GROUP = 32


class Far:
    def __init__(self, ends, send_sem, recv_sem, peer):
        self.parts = (ends, send_sem, recv_sem, peer)
        self.build().start()

    def build(self):
        ends, send_sem, recv_sem, peer = self.parts
        src, dst = ends()
        return pltpu.make_async_remote_copy(
            src_ref=src, dst_ref=dst, send_sem=send_sem(), recv_sem=recv_sem(), device_id=peer, device_id_type=MESH
        )

    def wait(self):
        self.build().wait()


class Parcel:
    def __init__(self, keep, send, landing, levels, sems, order, place, names="wvyx"):
        self.keep, self.send, self.landing, self.levels, self.sems = keep, send, landing, levels, sems
        self.order, self.place, self.names = order, place, names

    def copy(self, src, dst, slot, peer):
        send_sem, recv_sem = self.sems
        return pltpu.make_async_remote_copy(
            src_ref=src, dst_ref=dst, send_sem=send_sem(slot), recv_sem=recv_sem(slot), device_id=peer, device_id_type=MESH
        )

    def bring(self, step):
        if step == 0:
            return self.copy(self.send(), self.landing(), 0, self.place["core"][1])
        name, used = self.order[step - 1], self.order[:step]
        spot = tuple(
            self.place[n][2] if n == name else self.place[n][0] if n in used else slice(None) for n in self.names
        )
        return self.copy(self.keep().at[spot], self.levels(step - 1), step, self.place[name][1])

    def start(self):
        self.bring(0).start()

    def gather(self, step):
        self.bring(step).wait()
        return self.add(step)

    def add(self, step):
        used = self.order[:step]
        left = [n for n in self.names if n not in used]
        arrived = self.levels(step - 1) if step else self.landing()

        def one(i):
            at = {}
            for n in reversed(left):
                at[n] = i % 2
                i = i // 2
            inner = tuple(at[n] for n in left)
            spot = tuple(at[n] if n in at else self.place[n][0] for n in self.names)
            total = self.keep()[spot].astype(F32) + arrived[inner].astype(F32)
            if step == len(self.order):
                return total
            self.keep()[spot] = total.astype(BF16)

        if not left:
            return one(0)
        pl.loop(0, 2 ** len(left))(lambda i: one(i) and None)

    def launch(self, step):
        self.bring(step + 1).start()

    def move(self, step):
        self.gather(step)
        self.launch(step)


class HalfParcel(Parcel):
    def launch(self, step):
        if step < 3:
            return super().launch(step)

        @pl.when(self.goes)
        def _():
            self.bring(4).start()

    def finish(self, write):
        @pl.when(self.goes)
        def _():
            self.bring(4).wait_send()

        @pl.when(self.mine)
        def _():
            self.bring(4).wait_recv()
            write(self.add(4))


def level_shapes(names, order, rows, cols):
    return [
        (2,) * len([n for n in names if n not in order[: step + 1]]) + (rows, cols) for step in range(len(order))
    ]


ORDERS = ("yvxw", "vxyw", "xwyv", "yxwv", "vwyx", "yvxw", "vywx")
FC2_A, FC2_B, FC1_A, FC1_B, VAL_PROJ, QUERY, KEY = range(7)


def rest_kernel(
    grid_ref, split_ref, owner_ref, drop_ref, cot_hbm, cot_oth, n2_hbm, mid_hbm, qkv_hbm, probs_hbm, w1_hbm, w2_hbm, wp_hbm, wqkv_hbm, unit_hbm, rstd_hbm,
    att_hbm, rows_ref,
    fc2_ref, fc1_ref, qkvg_ref, projg_ref, vec_ref, out_ref, grad_ref, back_ref,
    cot, rstd_one, dn2, mid, acc, left, right, wbuf, qkv, probs, djoin, datt, tile, ost, gsend, grecv, vec, vget,
    keep_a, send_a, land_a, keep_b, send_b, land_b, keep_c, send_c, land_c, *others,
):
    levels = [others[4 * k : 4 * k + 4] for k in range(PARTS)]
    (load_sem, probs_sem, qkv_sem, w_sem, send_sem, recv_sem, side_send, side_recv, vec_send, vec_recv, out_sem,
     free_sem) = others[4 * PARTS :]
    images, rows, width = dn2.shape
    half = rows // 2
    pairs = width // 128
    steps = w1_hbm.shape[1] // width
    line = lax.axis_index("img")
    x = lax.axis_index("seq")
    core = line % 2
    y = (line // 2) % 2
    z = line // 4
    sibling = (line + 1 - 2 * core, x)
    level = (line + 2 - 4 * y, x)
    across = (line, 1 - x)
    scal_ref = Facts((grid_ref, split_ref, owner_ref, drop_ref), images, x)
    zv, zw = z % 2, z // 2
    near_z = (line + 4 - 8 * zv, x)
    far_z = (line + 8 - 16 * zw, x)
    peers = [sibling, level, across, near_z, far_z]
    barrier = pltpu.get_barrier_semaphore()
    for peer in peers:
        pl.semaphore_signal(barrier, inc=1, device_id=peer, device_id_type=MESH)

    loads = []

    def fetch(src, dst):
        copy = pltpu.make_async_copy(src, dst, load_sem.at[len(loads)])
        copy.start()
        loads.append(copy)
        return copy

    def probs_copy(index, slot):
        return pltpu.make_async_copy(
            probs_hbm.at[index // pairs, pl.ds(2 * (index % pairs), 2)], probs.at[slot], probs_sem.at[slot]
        )

    def qkv_copy(i, slot):
        return pltpu.make_async_copy(qkv_hbm.at[i], qkv.at[slot], qkv_sem.at[slot])

    def w1_copy(t, slot):
        at = pl.multiple_of(t * width, 128)
        return pltpu.make_async_copy(w1_hbm.at[:, pl.ds(at, width)], wbuf.at[slot], w_sem.at[slot])

    def w2_copy(t, slot):
        at = pl.multiple_of(t * width, 128)
        return pltpu.make_async_copy(w2_hbm.at[pl.ds(at, width), :], wbuf.at[2 + slot], w_sem.at[2 + slot])

    first = [fetch(cot_hbm.at[pl.ds(x * images, images)], cot.at[:, pl.ds(0, half)]), fetch(cot_oth, cot.at[:, pl.ds(half, half)]), fetch(n2_hbm, left)]
    w1_copy(0, 0).start()
    w2_copy(0, 0).start()
    mid_in = fetch(mid_hbm, mid)
    for slot in range(SLOTS):
        probs_copy(slot, slot).start()
    for slot in range(2):
        qkv_copy(slot, slot).start()

    place = {
        "core": (core, sibling), "y": (y, level, 1 - y), "x": (x, across, 1 - x),
        "v": (zv, near_z, 1 - zv), "w": (zw, far_z, 1 - zw),
    }
    homes = [
        (keep_a.at[0], send_a, land_a), (keep_a.at[1], send_a, land_a),
        (keep_b.at[0], send_b.at[0], land_b.at[0]), (keep_b.at[1], send_b.at[1], land_b.at[1]),
        (keep_b.at[2], send_b.at[0], land_b.at[0]),
        (keep_c.at[0], send_c.at[0], land_c.at[0]), (keep_c.at[1], send_c.at[1], land_c.at[1]),
    ]
    parcels = []
    for k in range(PARTS):
        keep, send, land = (lambda k=k, n=n: homes[k][n] for n in range(3))
        sems = (lambda slot, k=k: send_sem.at[k, slot]), (lambda slot, k=k: recv_sem.at[k, slot])
        build = HalfParcel if k < 2 else Parcel
        parcels.append(
            build(keep, send, land, lambda step, k=k: levels[k][step], sems, ORDERS[k], place, "vyx" if k < 2 else "wvyx")
        )
    for k in range(2):
        parcels[k].goes, parcels[k].mine = zw != k, zw == k
    free_slot = {FC2_A: 0, FC1_A: 1}
    needs = {FC2_B: 0, VAL_PROJ: 1}

    def release(k):
        pl.semaphore_signal(free_sem.at[free_slot[k]], inc=1, device_id=sibling, device_id_type=MESH)

    def start(k):
        if k in needs:
            pl.semaphore_wait(free_sem.at[needs[k]], 1)
        parcels[k].start()

    r, c = keep_b.shape[-2], keep_b.shape[-1]
    unit, side_cols = r // 2, c // 2

    def put_block_rows(k, zz):
        for ref, who in ((send_a, 1 - core), (keep_a.at[k], core)):
            for b in range(2):
                for e in range(2):
                    at = pl.multiple_of((2 * b + who) * 4 * r + e * 2 * r, 8)
                    ref[zz, b, e] = tile[pl.ds(at, 2 * r), :].astype(BF16)

    def put_folds(send, kept, t):
        spot = pl.ds(pl.multiple_of(t * side_cols, 128), side_cols)

        @pl.loop(0, 8)
        def _(k):
            for ref, who in ((send, 1 - core), (kept, core)):
                for e in range(2):
                    at = pl.multiple_of((4 * k + 2 * who + e) * unit, 8)
                    piece = tile[pl.ds(at, unit), :]
                    ref[k // 4, (k // 2) % 2, k % 2, e, :, spot] = jnp.concatenate(
                        [piece[:, :side_cols], piece[:, side_cols:]], axis=0
                    ).astype(BF16)

    def step_one(k):
        parcels[k].gather(0)
        if k in free_slot:
            release(k)
        parcels[k].launch(0)

    flat = lambda ref: ref[...].reshape(images * rows, ref.shape[-1])
    column = lambda k: djoin[:, :, k * width : k * width + width].reshape(images * rows, width)

    vec[...] = jnp.zeros_like(vec)
    acc[...] = jnp.zeros_like(acc)
    dn2[...] = jnp.zeros_like(dn2)
    for copy in first:
        copy.wait()
    for i in range(images):
        gate = scal_ref[i, 5].astype(F32) * KEEP_SCALE
        live = row_valid(scal_ref, i, rows, half, 0)
        d_mlp = (jnp.where(live, cot[i].astype(F32), 0.0) * gate).astype(BF16)
        right[i] = d_mlp
        vec[11:12, :] += jnp.sum(d_mlp.astype(F32), axis=0, keepdims=True)
    pl.semaphore_wait(barrier, len(peers))

    wp_copy = pltpu.make_async_copy(wp_hbm, wbuf.at[2], w_sem.at[2])

    def wqkv_copy(k, slot):
        return pltpu.make_async_copy(wqkv_hbm.at[:, pl.ds(k * width, width)], wbuf.at[slot], w_sem.at[slot])

    @pl.loop(0, steps)
    def _(t):
        slot = t % 2
        w1_copy(t, slot).wait()
        w2_copy(t, slot).wait()

        @pl.when(t + 1 < steps)
        def _():
            w1_copy(t + 1, 1 - slot).start()
            w2_copy(t + 1, 1 - slot).start()

        @pl.when(t + 1 == steps)
        def _():
            wqkv_copy(0, 0).start()
            wp_copy.start()

        @pl.when(t == 2)
        def _():
            start(FC2_A)
            start(FC1_A)

        for i in range(images):
            pre = dot_nn(left[i], wbuf[slot]) + rows_ref[pl.ds(t, 1), :]
            hidden, slope = gelu_both(pre)
            hidden = hidden.astype(BF16)
            d_pre = (slope * dot_nt(right[i], wbuf[2 + slot])).astype(BF16)
            djoin[i, :, :width] = hidden
            djoin[i, :, width : 2 * width] = d_pre
            vec[pl.ds(7 + t, 1), :] += jnp.sum(d_pre.astype(F32), axis=0, keepdims=True)
            acc[i] += dot_nn(hidden, wbuf[2 + slot])
            dn2[i] += dot_nt(d_pre, wbuf[slot])

        tile[...] = dot_tn(column(0), flat(right))

        @pl.when(t == 2)
        def _():
            for k in (FC2_A, FC1_A):
                step_one(k)

        for k in range(2):

            @pl.when(t // 2 == k)
            def _():
                put_block_rows(k, t % 2)

        tile[...] = dot_tn(flat(left), column(1))
        for k in range(2):

            @pl.when(t // 2 == k)
            def _():
                put_folds(send_b.at[k], keep_b.at[k], t % 2)

    wqkv_copy(1, 1).start()
    wqkv_copy(2, 3).start()
    unit_in, att_in, rstd_in = fetch(unit_hbm, left), fetch(att_hbm, right), fetch(rstd_hbm, rstd_one)
    start(FC2_B)
    start(FC1_B)
    mid_in.wait()
    for i in range(images):
        gate = scal_ref[i, 5].astype(F32) * KEEP_SCALE
        final = mid[i] + gate * (acc[i] + rows_ref[4:5, :])
        out = jnp.where(row_valid(scal_ref, i, rows, half, 0), final, 0.0).astype(BF16)
        ost[i] = out[:half]
        gsend[i] = out[half:]
    out_own = pltpu.make_async_copy(ost, out_ref.at[pl.ds(x * images, images)], out_sem.at[0])
    out_own.start()
    out_far = Far(
        lambda: (gsend, out_ref.at[pl.ds(x * images, images)]), lambda: side_send.at[images], lambda: side_recv.at[images], across
    )

    wp_copy.wait()
    for i in range(images):
        live = row_valid(scal_ref, i, rows, half, 0)
        d_final = jnp.where(live, cot[i].astype(F32), 0.0)
        unit_two, rstd = norm_parts(mid[i])
        d_normed = dn2[i]
        vec[5:6, :] += jnp.sum(d_normed * unit_two, axis=0, keepdims=True)
        vec[6:7, :] += jnp.sum(d_normed, axis=0, keepdims=True)
        d_middle = d_final + norm_back(d_normed, rows_ref[7:8, :], unit_two, rstd)
        dn2[i] = d_middle
        gate = scal_ref[i, 4].astype(F32) * KEEP_SCALE
        d_branch = (d_middle * gate).astype(BF16)
        datt[i] = d_branch
        vec[4:5, :] += jnp.sum(d_branch.astype(F32), axis=0, keepdims=True)
    parcels[FC2_A].move(1)
    unit_in.wait()
    att_in.wait()
    rstd_in.wait()
    tile[...] = dot_tn(flat(right), flat(datt))
    put_folds(send_b.at[0], keep_b.at[2], 1)
    step_one(FC1_B)
    for i in range(images):
        datt[i] = dot_nt(datt[i], wbuf[2]).astype(BF16)
    step_one(FC2_B)

    low_lane = lax.broadcasted_iota(jnp.int32, (rows, 128), 1) < HEAD_DIM
    sides = (low_lane, jnp.logical_not(low_lane))
    cuts = lambda pair: [slice(k * width + 128 * pair, k * width + 128 * pair + 128) for k in range(3)]
    total_pairs = images * pairs

    def next_probs(index, slot):
        @pl.when(index + SLOTS < 2 * total_pairs)
        def _():
            probs_copy((index + SLOTS) % total_pairs, slot).start()

    def pump(plan, i, pair):
        for (image, at), job in plan.items():
            if at == pair:

                @pl.when(i == image)
                def _():
                    job()

    early_plan = {
        (0, 4): lambda: parcels[FC1_A].move(1),
        (2, 3): lambda: parcels[FC2_A].move(2),
    }

    @pl.loop(0, images)
    def _(i):
        for pair in range(pairs):
            index = i * pairs + pair
            slot = index % SLOTS
            probs_copy(index, slot).wait()
            q_cut, _, v_cut = cuts(pair)
            a2 = datt[i, :, q_cut]
            dv = dot_nn(probs[slot, 0], jnp.where(sides[0], a2, 0)) + dot_nn(probs[slot, 1], jnp.where(sides[1], a2, 0))
            djoin[i, :, v_cut] = dv.astype(BF16)
            next_probs(index, slot)
            pump(early_plan, i, pair)
        vec[3:4, :] += jnp.sum(djoin[i, :, 2 * width :].astype(F32), axis=0, keepdims=True)

    tile[...] = dot_tn(flat(left), column(2))
    put_folds(send_b.at[0], keep_b.at[2], 0)
    start(VAL_PROJ)

    plan = {
        (0, 5): lambda: parcels[FC1_B].move(1),
        (1, 0): lambda: step_one(VAL_PROJ),
        (1, 3): lambda: parcels[FC2_A].move(3),
        (1, 4): lambda: parcels[FC1_A].move(2),
        (2, 2): lambda: parcels[FC2_B].move(1),
        (2, 3): lambda: parcels[FC1_B].move(2),
    }

    @pl.loop(0, images)
    def _(i):
        q_slot = i % 2
        qkv_copy(i, q_slot).wait()
        for pair in range(pairs):
            index = total_pairs + i * pairs + pair
            slot = index % SLOTS
            probs_copy(index - total_pairs, slot).wait()
            q_cut, k_cut, v_cut = cuts(pair)
            q2, k2, v2, a2 = qkv[q_slot, :, q_cut], qkv[q_slot, :, k_cut], qkv[q_slot, :, v_cut], datt[i, :, q_cut]
            dq = dk = None
            for side in range(2):
                high = probs[slot, side].astype(F32)
                d_probs = dot_nt(v2, jnp.where(sides[side], a2, 0))
                inner = jnp.sum(high * d_probs, axis=0, keepdims=True)
                d_scores = (high * (d_probs - inner)).astype(BF16)
                parts = dot_tn(d_scores, jnp.where(sides[side], k2, 0)), dot_nn(d_scores, jnp.where(sides[side], q2, 0))
                dq, dk = parts if dq is None else (dq + parts[0], dk + parts[1])
            djoin[i, :, q_cut] = (dq * HEAD_DIM**-0.5).astype(BF16)
            djoin[i, :, k_cut] = dk.astype(BF16)
            next_probs(index, slot)
            pump(plan, i, pair)

        @pl.when(i + 2 < images)
        def _():
            qkv_copy(i + 2, q_slot).start()

        vec[2:3, :] += jnp.sum(djoin[i, :, :width].astype(F32), axis=0, keepdims=True)
        vec[0:1, :] += jnp.sum(djoin[i, :, width : 2 * width].astype(F32), axis=0, keepdims=True)

    for t, k in ((0, QUERY), (1, KEY)):
        tile[...] = dot_tn(flat(left), column(t))
        put_folds(send_c.at[t], keep_c.at[t], 0)
        start(k)
    wqkv_copy(0, 0).wait()
    wqkv_copy(1, 1).wait()
    wqkv_copy(2, 3).wait()
    out_far.wait()

    def input_grad(i):
        d_normed = dot_nt(djoin[i, :, :width], wbuf[0])
        d_normed += dot_nt(djoin[i, :, width : 2 * width], wbuf[1])
        d_normed += dot_nt(djoin[i, :, 2 * width :], wbuf[3])
        out = dn2[i] + norm_back(d_normed, rows_ref[5:6, :], left[i].astype(F32), rstd_one[i])
        acc[i, :half] = out[:half]
        gsend[i] = out[half:].astype(BF16)

    def exchange(k):
        return Far(lambda: (vec, vget.at[k]), lambda: vec_send.at[k], lambda: vec_recv.at[k], peers[k])

    def settle(k, trade):
        trade.wait()
        vec[...] += vget[k]

    def write_folds(total, ref, tile_at):
        for t in range(total.shape[1] // side_cols):
            for h in range(2):
                at = (tile_at + t) * width + h * side_cols
                ref[:, at : at + side_cols] = total[h * unit : h * unit + unit, t * side_cols : t * side_cols + side_cols]

    def write_fc2(total):
        fc2_ref[...] = total

    swaps = []

    def swap_out(i):
        swaps.append(
            Far(lambda: (gsend.at[i], grecv.at[i]), lambda: side_send.at[i], lambda: side_recv.at[i], across)
        )

    trade = exchange(0)
    input_grad(0)
    swap_out(0)
    settle(0, trade)
    trade = exchange(1)
    parcels[VAL_PROJ].move(1)
    step_one(QUERY)
    step_one(KEY)
    input_grad(1)
    swap_out(1)
    settle(1, trade)
    trade = exchange(2)
    parcels[QUERY].move(1)
    parcels[KEY].move(1)
    input_grad(2)
    swap_out(2)
    settle(2, trade)
    trade = exchange(3)
    grad_own = pltpu.make_async_copy(acc.at[:, pl.ds(0, half)], grad_ref, out_sem.at[1])
    grad_own.start()
    parcels[KEY].move(2)
    parcels[FC1_B].move(3)
    parcels[FC2_B].move(2)
    settle(3, trade)
    trade = exchange(4)
    parcels[FC2_A].finish(write_fc2)
    parcels[FC1_A].move(3)
    parcels[QUERY].move(2)
    parcels[VAL_PROJ].move(2)
    settle(4, trade)
    vec_ref[...] = vec[...]
    parcels[FC2_B].move(3)
    write_folds(parcels[FC1_B].gather(4), fc1_ref, 2)
    parcels[KEY].move(3)
    write_folds(parcels[FC1_A].gather(4), fc1_ref, 0)
    parcels[QUERY].move(3)
    parcels[VAL_PROJ].move(3)
    write_folds(parcels[KEY].gather(4), qkvg_ref, 1)
    parcels[FC2_B].finish(write_fc2)
    write_folds(parcels[QUERY].gather(4), qkvg_ref, 0)
    for copy in swaps:
        copy.wait()
    grad_oth = pltpu.make_async_copy(grecv, back_ref, out_sem.at[2])
    grad_oth.start()
    total = parcels[VAL_PROJ].gather(4)
    write_folds(total[:, :side_cols], qkvg_ref, 2)
    write_folds(total[:, side_cols:], projg_ref, 0)
    out_own.wait()
    grad_own.wait()
    grad_oth.wait()


def rest(facts, cotangent, cot_oth, n2, middle, qkv, probs, unit_one, rstd_one, attended, rows_in, w):
    images, half, width = cot_oth.shape
    rows = 2 * half
    hidden_width = w["fc1_weight"].shape[1]
    r, c = 2 * (width // GROUP), width
    fc2_rows = hidden_width // GROUP
    hbm = pl.BlockSpec(memory_space=pl.ANY)
    vmem = pl.BlockSpec(memory_space=pltpu.VMEM)
    smem = pl.BlockSpec(memory_space=pltpu.SMEM)
    dma = pltpu.SemaphoreType.DMA
    whole = lambda dtype: pltpu.VMEM((images, rows, width), dtype)
    half_block = lambda dtype: pltpu.VMEM((images, half, width), dtype)
    level_bufs = []
    for k, order in enumerate(ORDERS):
        names = "vyx" if k < 2 else "wvyx"
        block = (fc2_rows, width) if k < 2 else (r, c) if k < 5 else (r, c // 2)
        level_bufs += [pltpu.VMEM(shape, BF16) for shape in level_shapes(names, order, *block)]
    rows_of = lambda *lead: pltpu.VMEM(lead + (2, 2, 2, fc2_rows, width), BF16)
    folds_of = lambda count, cols: pltpu.VMEM((count, 2, 2, 2, 2, r, cols), BF16)
    return pl.pallas_call(
        rest_kernel,
        in_specs=[smem] * 4 + [hbm] * 13 + [vmem],
        out_specs=[vmem] * 5 + [hbm] * 3,
        out_shape=[
            jax.ShapeDtypeStruct((fc2_rows, width), F32),
            jax.ShapeDtypeStruct((r // 2, hidden_width), F32),
            jax.ShapeDtypeStruct((r // 2, 3 * width), F32),
            jax.ShapeDtypeStruct((r // 2, width), F32),
            jax.ShapeDtypeStruct((16, width), F32),
            jax.ShapeDtypeStruct((2 * images, half, width), BF16),
            jax.ShapeDtypeStruct((images, half, width), F32),
            jax.ShapeDtypeStruct((images, half, width), BF16),
        ],
        scratch_shapes=[
            whole(BF16), pltpu.VMEM((images, rows, 1), F32), whole(F32), whole(F32), whole(F32), whole(BF16), whole(BF16),
            pltpu.VMEM((4, width, width), BF16),
            pltpu.VMEM((2, rows, 3 * width), BF16),
            pltpu.VMEM((SLOTS, 2, rows, rows), BF16),
            pltpu.VMEM((images, rows, 3 * width), BF16),
            whole(BF16),
            pltpu.VMEM((width, width), F32),
            half_block(BF16), half_block(BF16), half_block(BF16),
            pltpu.VMEM((16, width), F32),
            pltpu.VMEM((5, 16, width), F32),
            rows_of(2), rows_of(), rows_of(),
            folds_of(3, c), folds_of(2, c), folds_of(2, c),
            folds_of(2, c // 2), folds_of(2, c // 2), folds_of(2, c // 2),
            *level_bufs,
            dma((8,)), dma((SLOTS,)), dma((2,)), dma((4,)), dma((PARTS, 5)), dma((PARTS, 5)), dma((images + 1,)),
            dma((images + 1,)), dma((5,)), dma((5,)), dma((3,)), pltpu.SemaphoreType.REGULAR((2,)),
        ],
        compiler_params=pltpu.CompilerParams(collective_id=0, has_side_effects=True, vmem_limit_bytes=64 * MIB),
        name="rest",
    )(*facts, cotangent, cot_oth, n2, middle, qkv, probs, w["fc1_weight"], w["fc2_weight"], w["proj_weight"],
      w["qkv_weight"], unit_one, rstd_one, attended, rows_in)


def spread(value):
    return lax.psum_scatter(value, ("img", "seq"), scatter_dimension=0, tiled=True)


def unfold(send, keep, core, folds):
    rows, cols = send.shape[-2], send.shape[-1]
    send, keep = (v.reshape(GROUP // 4, 2, rows, cols) for v in (send, keep))
    both = jnp.stack([jnp.where(core == 0, keep, send), jnp.where(core == 0, send, keep)], axis=1).astype(F32)
    if folds == 1:
        return both.reshape(GROUP * rows, cols)
    tiles = 4
    both = both.reshape(GROUP, 2, rows // 2, tiles, cols // tiles)
    return both.transpose(0, 2, 3, 1, 4).reshape(GROUP * rows // 2, 2 * cols)


def swap(value, axis, bit, size):
    return lax.ppermute(value, axis, [(i, i ^ bit) for i in range(size)])


def shards(img_size, args):
    (patches, grid_shape, split_rows, owner_shard, drop_masks, ln1_gain, ln1_bias, qkv_weight, qv_bias, proj_weight,
     proj_bias, ln2_gain, ln2_bias, fc1_weight, fc1_bias, fc2_weight, fc2_bias, cotangent) = args
    all_images, _, half, width = patches.shape
    images = all_images // 2
    rows = 2 * half
    tokens = images * rows
    side = lax.axis_index("seq")
    line = lax.axis_index("img")
    owners = 2 * img_size
    row = lambda v: v.reshape(1, -1)
    w = dict(
        ln1_gain=row(ln1_gain), ln1_bias=row(ln1_bias), qkv_weight=qkv_weight, q_bias=row(qv_bias[:width]),
        v_bias=row(qv_bias[width:]), proj_weight=proj_weight, proj_bias=row(proj_bias), ln2_gain=row(ln2_gain),
        ln2_bias=row(ln2_bias), fc1_weight=fc1_weight, fc1_bias=row(fc1_bias), fc2_weight=fc2_weight, fc2_bias=row(fc2_bias),
    )

    def exchange(value):
        value = value.reshape(all_images, half, width)
        own = lax.dynamic_slice_in_dim(value, side * images, images, axis=0)
        away = lax.dynamic_slice_in_dim(value, (1 - side) * images, images, axis=0)
        return own, swap(away, "seq", 1, 2)

    def place(own, back):
        back = back.astype(own.dtype)
        first = jnp.where(side == 0, own, back)
        second = jnp.where(side == 0, back, own)
        return jnp.concatenate([first, second], axis=0).reshape(all_images, 1, half, width)

    def restore(own, oth):
        return place(own, swap(oth, "seq", 1, 2))

    across = grid_shape[:, 1]
    counts = jnp.stack([split_rows * across, (grid_shape[:, 0] - split_rows) * across], axis=0)
    count_own = jnp.where(side == 0, counts[0], counts[1])
    count_oth = jnp.where(side == 0, counts[1], counts[0])
    special = (owner_shard == side).astype(jnp.int32)
    table = jnp.stack([count_own, special, count_oth, 1 - special, drop_masks[:, 0], drop_masks[:, 1]], axis=1)
    scal = lax.dynamic_slice_in_dim(table, side * images, images, axis=0)

    flat = lambda v: v.reshape(tokens, v.shape[-1])
    unit1 = width // GROUP
    unit2 = fc2_weight.shape[0] // GROUP
    if owners == GROUP:
        merge = lambda v: v.reshape(all_images, half, width)
        facts = (grid_shape, split_rows, owner_shard, drop_masks)
        unit_one, rstd_one, qkv, probs, attended, middle, n2, rows_in, c_oth = opening(
            facts, merge(patches), merge(cotangent),
            (ln1_gain, ln1_bias, qv_bias, proj_bias, ln2_gain, ln2_bias, fc1_bias, fc2_bias, qkv_weight, proj_weight),
        )
        fc2_part, fc1_part, u_part, proj_part, sums, out_part, grad_own, grad_back = rest(
            facts, merge(cotangent), c_oth, n2, middle, qkv, probs, unit_one, rstd_one, attended, rows_in, w
        )
        outs = emit(
            fc2_part, fc1_part, u_part, proj_part, sums, rows_in, qkv_weight,
            grad_own, grad_back, out_part,
        )
        layer_out, patches_grad = (v.reshape(all_images, 1, half, width) for v in outs[:2])
        return (layer_out, patches_grad, *outs[2:])
    else:
        x_own, x_oth = exchange(patches)
        c_own, c_oth = exchange(cotangent)
        n1, qkv, probs, attended, middle, n2 = front(scal, x_own, x_oth, w)
        mine = lax.rem(line, 2).reshape(1)
        hidden, slope, out_own, out_oth = mlp(scal, flat(n2), flat(middle), w, images, 512)
        layer_out = restore(out_own, out_oth)
        dn2, s2, k2, s1, k1, fc2_bias_grad, fc1_bias_grad = mlp_back(
            scal, mine, c_own, c_oth, flat(n2), hidden, slope, w, unit1, unit2
        )
        dn2 = dn2.reshape(images, rows, width)
        d_middle, d_branch, d_join, ln2_gain_grad, ln2_bias_grad, proj_bias_grad, q_grad, v_grad = attend_back(
            scal, c_own, c_oth, dn2, middle, qkv, probs, w
        )
        st, kt, grad_own, grad_oth, ln1_gain_grad, ln1_bias_grad = tail(
            mine, flat(n1), flat(d_join), flat(attended), flat(d_branch), x_own, x_oth, flat(d_middle), w, unit1
        )
        patches_grad = restore(grad_own, grad_oth)
        vectors = (
            ln1_gain_grad, ln1_bias_grad, jnp.concatenate([q_grad, v_grad], axis=1), proj_bias_grad, ln2_gain_grad,
            ln2_bias_grad, fc1_bias_grad, fc2_bias_grad,
        )
        fc2_grad = spread(unfold(s2, k2, line % 2, 1))
        fc1_grad = spread(unfold(s1, k1, line % 2, 2))
        tail_grad = spread(unfold(st, kt, line % 2, 2))
        qkv_grad, proj_grad = tail_grad[:, : 3 * width], tail_grad[:, 3 * width :]
        pieces = [spread(v.reshape(-1)) for v in vectors]
    l1g, l1b, qvb, pjb, l2g, l2b, f1b, f2b = pieces
    return (
        layer_out, patches_grad, l1g, l1b, qkv_grad, qvb, proj_grad, pjb, l2g, l2b, fc1_grad, f1b, fc2_grad, f2b,
    )


def solution(mesh):
    rep = [P()] * 12
    vec = P(("img", "seq"))
    mat = P(("img", "seq"), None)
    rows = P("img", "seq", None, None)

    def run(*args):
        return shards(mesh.shape["img"], args)

    return jax.shard_map(
        run,
        mesh=mesh,
        in_specs=(rows, P("img", None), P("img"), P("img"), P("img", None), *rep, rows),
        out_specs=(rows, rows, vec, vec, mat, vec, mat, vec, vec, vec, mat, vec, mat, vec),
        check_vma=False,
    )
```

```python
import functools

import jax
import jax.numpy as jnp
from jax import lax
from jax.experimental import pallas as pl
from jax.experimental.pallas import tpu as pltpu
from jax.sharding import PartitionSpec as P

HEAD_DIM = 64
LN_EPS = 1e-06
KEEP_SCALE = 1.0 / 0.9
MASK_FILL = -1e30
BF16 = jnp.bfloat16
F32 = jnp.float32
MIB = 1024 * 1024


def dot_nn(a, b):
    return lax.dot_general(a, b, (((1,), (0,)), ((), ())), preferred_element_type=F32)


def dot_nt(a, b):
    return lax.dot_general(a, b, (((1,), (1,)), ((), ())), preferred_element_type=F32)


def dot_tn(a, b):
    return lax.dot_general(a, b, (((0,), (0,)), ((), ())), preferred_element_type=F32)


def norm_parts(values):
    row_mean = jnp.mean(values, axis=-1, keepdims=True)
    centred = values - row_mean
    variance = jnp.mean(centred * centred, axis=-1, keepdims=True)
    rstd = lax.rsqrt(variance + LN_EPS)
    return centred * rstd, rstd


def norm_back(d_normed, gain, unit, rstd):
    d_unit = d_normed * gain
    mean_one = jnp.mean(d_unit, axis=-1, keepdims=True)
    mean_two = jnp.mean(d_unit * unit, axis=-1, keepdims=True)
    return rstd * (d_unit - mean_one - unit * mean_two)


def gelu_both(values):
    cdf = 0.5 + 0.5 * lax.erf(values * 0.7071067811865476)
    return values * cdf, cdf + values * (0.3989422804014327 * jnp.exp(-0.5 * values * values))


class Facts:
    def __init__(self, refs, images, x):
        self.grid, self.split, self.owner, self.drop = refs
        self.images, self.x = images, x

    def __getitem__(self, key):
        image, k = key
        at = self.x * self.images + image
        if k >= 4:
            return self.drop[k - 4, at]
        if k % 2 == 1:
            own = (self.owner[at] == self.x).astype(jnp.int32)
            return own if k == 1 else 1 - own
        across = self.grid[1, at]
        first = self.split[at] * across
        second = (self.grid[0, at] - self.split[at]) * across
        return jnp.where(self.x == k // 2, first, second)


def row_valid(scal_ref, image, rows, half, axis):
    shape = (rows, 1) if axis == 0 else (1, rows)
    slot = lax.broadcasted_iota(jnp.int32, shape, axis)
    other = slot >= half
    place = jnp.where(other, slot - half, slot)
    count = jnp.where(other, scal_ref[image, 2], scal_ref[image, 0])
    special = jnp.where(other, scal_ref[image, 3], scal_ref[image, 1])
    return jnp.where(place < 2, special, (place - 2 < count).astype(jnp.int32)) > 0


def front_kernel(
    scal_ref, own_ref, oth_ref, g1_ref, b1_ref, wqkv_ref, qb_ref, vb_ref, wp_ref, pb_ref, g2_ref, b2_ref,
    n1_ref, qkv_ref, probs_ref, att_ref, mid_ref, n2_ref,
):
    image = pl.program_id(0)
    half, width = own_ref.shape[1], own_ref.shape[2]
    rows = 2 * half
    x = jnp.concatenate([own_ref[0].astype(F32), oth_ref[0].astype(F32)], axis=0)
    unit, _ = norm_parts(x)
    n1 = (unit * g1_ref[...] + b1_ref[...]).astype(BF16)
    n1_ref[0] = n1
    qkv_ref[0, :, :width] = ((dot_nn(n1, wqkv_ref[:, :width]) + qb_ref[...]).astype(BF16) * BF16(HEAD_DIM**-0.5))
    qkv_ref[0, :, width : 2 * width] = dot_nn(n1, wqkv_ref[:, width : 2 * width]).astype(BF16)
    qkv_ref[0, :, 2 * width :] = (dot_nn(n1, wqkv_ref[:, 2 * width :]) + vb_ref[...]).astype(BF16)
    fill = jnp.where(row_valid(scal_ref, image, rows, half, 0), 0.0, MASK_FILL)
    low_lane = lax.broadcasted_iota(jnp.int32, (rows, 128), 1) < HEAD_DIM
    for pair in range(width // 128):
        cut = slice(128 * pair, 128 * pair + 128)
        q2 = qkv_ref[0, :, cut]
        k2 = qkv_ref[0, :, width + 128 * pair : width + 128 * pair + 128]
        v2 = qkv_ref[0, :, 2 * width + 128 * pair : 2 * width + 128 * pair + 128]
        total = None
        for side in range(2):
            mine = low_lane if side == 0 else jnp.logical_not(low_lane)
            scores = dot_nt(k2, jnp.where(mine, q2, 0)) + fill
            top = jnp.max(scores, axis=0, keepdims=True)
            weight = jnp.exp(scores - top)
            probs = (weight * (1.0 / jnp.sum(weight, axis=0, keepdims=True))).astype(BF16)
            probs_ref[0, 2 * pair + side] = probs
            part = dot_tn(probs, jnp.where(mine, v2, 0))
            total = part if total is None else total + part
        att_ref[0, :, cut] = total.astype(BF16)
    keep = scal_ref[image, 4].astype(F32) * KEEP_SCALE
    branch = dot_nn(att_ref[0], wp_ref[...]) + pb_ref[...]
    middle = jnp.concatenate([own_ref[0].astype(F32), oth_ref[0].astype(F32)], axis=0) + keep * branch
    mid_ref[0] = middle
    unit, _ = norm_parts(middle)
    n2_ref[0] = (unit * g2_ref[...] + b2_ref[...]).astype(BF16)


def full(shape):
    zeros = (0,) * len(shape)
    return pl.BlockSpec(shape, lambda *_: zeros, pipeline_mode=pl.Buffered(1))


def front(scal, own, oth, w):
    images, half, width = own.shape
    rows = 2 * half
    heads = width // HEAD_DIM
    per = lambda *tail: pl.BlockSpec((1,) + tail, lambda i, s: (i,) + (0,) * len(tail))
    flops = 2 * images * rows * width * (4 * width + 4 * rows)
    return pl.pallas_call(
        front_kernel,
        grid_spec=pltpu.PrefetchScalarGridSpec(
            num_scalar_prefetch=1,
            grid=(images,),
            in_specs=[
                per(half, width), per(half, width), full((1, width)), full((1, width)),
                full((width, 3 * width)), full((1, width)), full((1, width)),
                full((width, width)), full((1, width)), full((1, width)), full((1, width)),
            ],
            out_specs=[
                per(rows, width), per(rows, 3 * width), per(heads, rows, rows),
                per(rows, width), per(rows, width), per(rows, width),
            ],
        ),
        out_shape=[
            jax.ShapeDtypeStruct((images, rows, width), BF16),
            jax.ShapeDtypeStruct((images, rows, 3 * width), BF16),
            jax.ShapeDtypeStruct((images, heads, rows, rows), BF16),
            jax.ShapeDtypeStruct((images, rows, width), BF16),
            jax.ShapeDtypeStruct((images, rows, width), F32),
            jax.ShapeDtypeStruct((images, rows, width), BF16),
        ],
        compiler_params=pltpu.CompilerParams(vmem_limit_bytes=56 * MIB),
        cost_estimate=pl.CostEstimate(flops=flops, transcendentals=images * heads * rows * rows, bytes_accessed=30_000_000),
        name="front",
    )(scal, own, oth, w["ln1_gain"], w["ln1_bias"], w["qkv_weight"], w["q_bias"], w["v_bias"],
      w["proj_weight"], w["proj_bias"], w["ln2_gain"], w["ln2_bias"])


def mlp_kernel(
    scal_ref, n2_ref, mid_ref, w1_ref, c1_ref, w2_ref, c2_ref,
    hid_ref, slope_ref, own_ref, oth_ref, acc_ref,
):
    step = pl.program_id(0)
    images, half, width = own_ref.shape
    rows = 2 * half
    hidden, slope = gelu_both(dot_nn(n2_ref[...], w1_ref[...]) + c1_ref[...])
    hidden = hidden.astype(BF16)
    hid_ref[...] = hidden
    slope_ref[...] = slope.astype(BF16)
    part = dot_nn(hidden, w2_ref[...])

    @pl.when(step == 0)
    def _():
        acc_ref[...] = part

    @pl.when(step > 0)
    def _():
        acc_ref[...] += part

    @pl.when(step == pl.num_programs(0) - 1)
    def _():
        for image in range(images):
            keep = scal_ref[image, 5].astype(F32) * KEEP_SCALE
            cut = slice(rows * image, rows * image + rows)
            final = mid_ref[cut, :] + keep * (acc_ref[cut, :] + c2_ref[...])
            out = jnp.where(row_valid(scal_ref, image, rows, half, 0), final, 0.0).astype(BF16)
            own_ref[image] = out[:half]
            oth_ref[image] = out[half:]


def mlp(scal, n2, middle, w, images, tile):
    tokens, width = n2.shape
    hidden_width = w["fc1_weight"].shape[1]
    half = tokens // images // 2
    return pl.pallas_call(
        mlp_kernel,
        grid_spec=pltpu.PrefetchScalarGridSpec(
            num_scalar_prefetch=1,
            grid=(hidden_width // tile,),
            in_specs=[
                full((tokens, width)), full((tokens, width)),
                pl.BlockSpec((width, tile), lambda j, s: (0, j)), pl.BlockSpec((1, tile), lambda j, s: (0, j)),
                pl.BlockSpec((tile, width), lambda j, s: (j, 0)), full((1, width)),
            ],
            out_specs=[
                pl.BlockSpec((tokens, tile), lambda j, s: (0, j)), pl.BlockSpec((tokens, tile), lambda j, s: (0, j)),
                full((images, half, width)), full((images, half, width)),
            ],
            scratch_shapes=[pltpu.VMEM((tokens, width), F32)],
        ),
        out_shape=[
            jax.ShapeDtypeStruct((tokens, hidden_width), BF16),
            jax.ShapeDtypeStruct((tokens, hidden_width), BF16),
            jax.ShapeDtypeStruct((images, half, width), BF16),
            jax.ShapeDtypeStruct((images, half, width), BF16),
        ],
        compiler_params=pltpu.CompilerParams(vmem_limit_bytes=56 * MIB),
        cost_estimate=pl.CostEstimate(flops=4 * tokens * width * hidden_width, transcendentals=2 * tokens * hidden_width, bytes_accessed=30_000_000),
        name="mlp",
    )(scal, n2, middle, w["fc1_weight"], w["fc1_bias"], w["fc2_weight"], w["fc2_bias"])


def put_rows(grad_ref, value, send_ref, keep_ref, mine, lead):
    grad_ref[...] = value
    run = 2 * send_ref.shape[-2]
    for k in range(grad_ref.shape[0] // (2 * run)):
        for ref, core in ((send_ref, 1 - mine), (keep_ref, mine)):
            for x in range(2):
                at = pl.multiple_of((2 * k + core) * run + x * (run // 2), 8)
                ref[lead + (k, x)] = grad_ref[pl.ds(at, run // 2), :].astype(BF16)


def put_folded(grad_ref, value, send_ref, keep_ref, mine):
    grad_ref[...] = value
    unit = send_ref.shape[-2] // 2
    side = grad_ref.shape[1] // 2
    for k in range(grad_ref.shape[0] // (4 * unit)):
        for ref, core in ((send_ref, 1 - mine), (keep_ref, mine)):
            for x in range(2):
                at = pl.multiple_of((4 * k + 2 * core + x) * unit, 8)
                piece = grad_ref[pl.ds(at, unit), :]
                ref[k, x] = jnp.concatenate([piece[:, :side], piece[:, side:]], axis=0).astype(BF16)


def mlp_back_kernel(
    scal_ref, mine_ref, own_ref, oth_ref, n2_ref, hid_ref, slope_ref, w1_ref, w2_ref,
    dn2_ref, s2_ref, k2_ref, s1_ref, k1_ref, c2_ref, c1_ref, dmlp_ref, grad_ref, acc_ref,
):
    step = pl.program_id(0)
    images, half, width = own_ref.shape
    rows = 2 * half
    mine = mine_ref[0]

    @pl.when(step == 0)
    def _():
        total = jnp.zeros((1, width), F32)
        for image in range(images):
            keep = scal_ref[image, 5].astype(F32) * KEEP_SCALE
            cot = jnp.concatenate([own_ref[image].astype(F32), oth_ref[image].astype(F32)], axis=0)
            live = row_valid(scal_ref, image, rows, half, 0)
            d_mlp = (jnp.where(live, cot, 0.0) * keep).astype(BF16)
            dmlp_ref[rows * image : rows * image + rows, :] = d_mlp
            total += jnp.sum(d_mlp.astype(F32), axis=0, keepdims=True)
        c2_ref[...] = total

    d_pre = slope_ref[...].astype(F32) * dot_nt(dmlp_ref[...], w2_ref[...])
    d_pre = d_pre.astype(BF16)
    c1_ref[...] = jnp.sum(d_pre.astype(F32), axis=0, keepdims=True)
    part = dot_nt(d_pre, w1_ref[...])
    put_folded(grad_ref, dot_tn(n2_ref[...], d_pre), s1_ref, k1_ref, mine)
    put_rows(grad_ref, dot_tn(hid_ref[...], dmlp_ref[...]), s2_ref, k2_ref, mine, (0,))

    @pl.when(step == 0)
    def _():
        acc_ref[...] = part

    @pl.when(step > 0)
    def _():
        acc_ref[...] += part

    @pl.when(step == pl.num_programs(0) - 1)
    def _():
        dn2_ref[...] = acc_ref[...]


def mlp_back(scal, mine, own, oth, n2, hidden, slope, w, unit1, unit2):
    tokens, width = n2.shape
    images, half, _ = own.shape
    hidden_width = hidden.shape[1]
    tile = width
    steps = hidden_width // tile
    runs1, runs2 = width // (4 * unit1), tile // (4 * unit2)
    col = pl.BlockSpec((tokens, tile), lambda j, s, m: (0, j))
    half1 = pl.BlockSpec((runs1, 2, 2 * unit1, tile // 2), lambda j, s, m: (0, 0, 0, j))
    half2 = pl.BlockSpec((1, runs2, 2, unit2, width), lambda j, s, m: (j, 0, 0, 0, 0))
    return pl.pallas_call(
        mlp_back_kernel,
        grid_spec=pltpu.PrefetchScalarGridSpec(
            num_scalar_prefetch=2,
            grid=(steps,),
            in_specs=[
                full((images, half, width)), full((images, half, width)), full((tokens, width)), col, col,
                pl.BlockSpec((width, tile), lambda j, s, m: (0, j)), pl.BlockSpec((tile, width), lambda j, s, m: (j, 0)),
            ],
            out_specs=[
                full((tokens, width)), half2, half2, half1, half1,
                full((1, width)), pl.BlockSpec((1, tile), lambda j, s, m: (0, j)),
            ],
            scratch_shapes=[
                pltpu.VMEM((tokens, width), BF16), pltpu.VMEM((width, width), F32), pltpu.VMEM((tokens, width), F32),
            ],
        ),
        out_shape=[
            jax.ShapeDtypeStruct((tokens, width), F32),
            jax.ShapeDtypeStruct((steps, runs2, 2, unit2, width), BF16),
            jax.ShapeDtypeStruct((steps, runs2, 2, unit2, width), BF16),
            jax.ShapeDtypeStruct((runs1, 2, 2 * unit1, hidden_width // 2), BF16),
            jax.ShapeDtypeStruct((runs1, 2, 2 * unit1, hidden_width // 2), BF16),
            jax.ShapeDtypeStruct((1, width), F32),
            jax.ShapeDtypeStruct((1, hidden_width), F32),
        ],
        compiler_params=pltpu.CompilerParams(vmem_limit_bytes=58 * MIB),
        cost_estimate=pl.CostEstimate(flops=8 * tokens * width * hidden_width, transcendentals=0, bytes_accessed=35_000_000),
        name="mlp_back",
    )(scal, mine, own, oth, n2, hidden, slope, w["fc1_weight"], w["fc2_weight"])


def attend_back_kernel(
    scal_ref, own_ref, oth_ref, dn2_ref, mid_ref, qkv_ref, probs_ref, wp_ref, g2_ref,
    dmid_ref, dbr_ref, djoin_ref, g2g_ref, g2b_ref, pbg_ref, qbg_ref, vbg_ref, datt_ref,
):
    image = pl.program_id(0)
    half, width = own_ref.shape[1], own_ref.shape[2]
    rows = 2 * half
    live = row_valid(scal_ref, image, rows, half, 0)
    d_final = jnp.where(live, jnp.concatenate([own_ref[0].astype(F32), oth_ref[0].astype(F32)], axis=0), 0.0)
    unit, rstd = norm_parts(mid_ref[0])
    dn2 = dn2_ref[0]
    gain_part = jnp.sum(dn2 * unit, axis=0, keepdims=True)
    bias_part = jnp.sum(dn2, axis=0, keepdims=True)
    d_middle = d_final + norm_back(dn2, g2_ref[...], unit, rstd)
    dmid_ref[0] = d_middle
    keep = scal_ref[image, 4].astype(F32) * KEEP_SCALE
    d_branch = (d_middle * keep).astype(BF16)
    dbr_ref[0] = d_branch
    proj_part = jnp.sum(d_branch.astype(F32), axis=0, keepdims=True)
    datt_ref[...] = dot_nt(d_branch, wp_ref[...]).astype(BF16)
    low_lane = lax.broadcasted_iota(jnp.int32, (rows, 128), 1) < HEAD_DIM
    for pair in range(width // 128):
        cut = slice(128 * pair, 128 * pair + 128)
        q2 = qkv_ref[0, :, cut]
        k2 = qkv_ref[0, :, width + 128 * pair : width + 128 * pair + 128]
        v2 = qkv_ref[0, :, 2 * width + 128 * pair : 2 * width + 128 * pair + 128]
        a2 = datt_ref[:, cut]
        dq = dk = dv = None
        for side in range(2):
            mine = low_lane if side == 0 else jnp.logical_not(low_lane)
            probs_low = probs_ref[0, 2 * pair + side]
            probs = probs_low.astype(F32)
            a_side = jnp.where(mine, a2, 0)
            d_probs = dot_nt(v2, a_side)
            inner = jnp.sum(probs * d_probs, axis=0, keepdims=True)
            d_scores = (probs * (d_probs - inner)).astype(BF16)
            dq_part = dot_tn(d_scores, jnp.where(mine, k2, 0))
            dk_part = dot_nn(d_scores, jnp.where(mine, q2, 0))
            dv_part = dot_nn(probs_low, a_side)
            dq = dq_part if dq is None else dq + dq_part
            dk = dk_part if dk is None else dk + dk_part
            dv = dv_part if dv is None else dv + dv_part
        djoin_ref[0, :, cut] = (dq * HEAD_DIM**-0.5).astype(BF16)
        djoin_ref[0, :, width + 128 * pair : width + 128 * pair + 128] = dk.astype(BF16)
        djoin_ref[0, :, 2 * width + 128 * pair : 2 * width + 128 * pair + 128] = dv.astype(BF16)
    q_part = jnp.sum(djoin_ref[0, :, :width].astype(F32), axis=0, keepdims=True)
    v_part = jnp.sum(djoin_ref[0, :, 2 * width :].astype(F32), axis=0, keepdims=True)
    sums = ((g2g_ref, gain_part), (g2b_ref, bias_part), (pbg_ref, proj_part), (qbg_ref, q_part), (vbg_ref, v_part))

    @pl.when(image == 0)
    def _():
        for ref, part in sums:
            ref[...] = part

    @pl.when(image > 0)
    def _():
        for ref, part in sums:
            ref[...] += part


def attend_back(scal, own, oth, dn2, middle, qkv, probs, w):
    images, half, width = own.shape
    rows = 2 * half
    heads = width // HEAD_DIM
    per = lambda *tail: pl.BlockSpec((1,) + tail, lambda i, s: (i,) + (0,) * len(tail))
    vec = jax.ShapeDtypeStruct((1, width), F32)
    return pl.pallas_call(
        attend_back_kernel,
        grid_spec=pltpu.PrefetchScalarGridSpec(
            num_scalar_prefetch=1,
            grid=(images,),
            in_specs=[
                per(half, width), per(half, width), per(rows, width), per(rows, width), per(rows, 3 * width),
                per(heads, rows, rows), full((width, width)), full((1, width)),
            ],
            out_specs=[per(rows, width), per(rows, width), per(rows, 3 * width)] + [full((1, width))] * 5,
            scratch_shapes=[pltpu.VMEM((rows, width), BF16)],
        ),
        out_shape=[
            jax.ShapeDtypeStruct((images, rows, width), F32),
            jax.ShapeDtypeStruct((images, rows, width), BF16),
            jax.ShapeDtypeStruct((images, rows, 3 * width), BF16),
            vec, vec, vec, vec, vec,
        ],
        compiler_params=pltpu.CompilerParams(vmem_limit_bytes=56 * MIB),
        cost_estimate=pl.CostEstimate(flops=2 * images * rows * width * (width + 8 * rows), transcendentals=0, bytes_accessed=35_000_000),
        name="attend_back",
    )(scal, own, oth, dn2, middle, qkv, probs, w["proj_weight"], w["ln2_gain"])


def tail_kernel(
    mine_ref, n1_ref, djoin_ref, att_ref, dbr_ref, wqkv_ref, xo_ref, xt_ref, dmid_ref, g1_ref,
    send_ref, keep_ref, go_ref, gt_ref, g1g_ref, g1b_ref, grad_ref, acc_ref,
):
    step = pl.program_id(0)
    last = pl.num_programs(0) - 1
    images, half, width = xo_ref.shape
    rows = 2 * half
    mine = mine_ref[0]

    @pl.when(step < last)
    def _():
        put_folded(grad_ref, dot_tn(n1_ref[...], djoin_ref[...]), send_ref, keep_ref, mine)
        part = dot_nt(djoin_ref[...], wqkv_ref[...])

        @pl.when(step == 0)
        def _():
            acc_ref[...] = part

        @pl.when(step > 0)
        def _():
            acc_ref[...] += part

    @pl.when(step == last)
    def _():
        put_folded(grad_ref, dot_tn(att_ref[...], dbr_ref[...]), send_ref, keep_ref, mine)
        gain_sum = jnp.zeros((1, width), F32)
        bias_sum = jnp.zeros((1, width), F32)
        for image in range(images):
            x = jnp.concatenate([xo_ref[image].astype(F32), xt_ref[image].astype(F32)], axis=0)
            unit, rstd = norm_parts(x)
            dn1 = acc_ref[rows * image : rows * image + rows, :]
            gain_sum += jnp.sum(dn1 * unit, axis=0, keepdims=True)
            bias_sum += jnp.sum(dn1, axis=0, keepdims=True)
            out = dmid_ref[rows * image : rows * image + rows, :] + norm_back(dn1, g1_ref[...], unit, rstd)
            go_ref[image] = out[:half]
            gt_ref[image] = out[half:].astype(BF16)
        g1g_ref[...] = gain_sum
        g1b_ref[...] = bias_sum


def tail(mine, n1, d_join, attended, d_branch, own, oth, d_middle, w, unit):
    tokens, width = n1.shape
    images, half, _ = own.shape
    runs = width // (4 * unit)
    halves = pl.BlockSpec((runs, 2, 2 * unit, width // 2), lambda j, m: (0, 0, 0, j))
    clip = lambda j: jnp.minimum(j, 2)
    return pl.pallas_call(
        tail_kernel,
        grid_spec=pltpu.PrefetchScalarGridSpec(
            num_scalar_prefetch=1,
            grid=(4,),
            in_specs=[
                full((tokens, width)), pl.BlockSpec((tokens, width), lambda j, m: (0, clip(j))), full((tokens, width)),
                full((tokens, width)), pl.BlockSpec((width, width), lambda j, m: (0, clip(j))),
                full((images, half, width)), full((images, half, width)), full((tokens, width)), full((1, width)),
            ],
            out_specs=[
                halves, halves, full((images, half, width)), full((images, half, width)),
                full((1, width)), full((1, width)),
            ],
            scratch_shapes=[pltpu.VMEM((width, width), F32), pltpu.VMEM((tokens, width), F32)],
        ),
        out_shape=[
            jax.ShapeDtypeStruct((runs, 2, 2 * unit, 2 * width), BF16),
            jax.ShapeDtypeStruct((runs, 2, 2 * unit, 2 * width), BF16),
            jax.ShapeDtypeStruct((images, half, width), F32),
            jax.ShapeDtypeStruct((images, half, width), BF16),
            jax.ShapeDtypeStruct((1, width), F32),
            jax.ShapeDtypeStruct((1, width), F32),
        ],
        compiler_params=pltpu.CompilerParams(vmem_limit_bytes=56 * MIB),
        cost_estimate=pl.CostEstimate(flops=14 * tokens * width * width, transcendentals=0, bytes_accessed=35_000_000),
        name="tail",
    )(mine, n1, d_join, attended, d_branch, w["qkv_weight"], own, oth, d_middle, w["ln1_gain"])


def emit_kernel(
    fc2_ref, fc1_ref, u_ref, proj_ref, sums_ref, gain_ref, bias_ref, w_ref, own_ref, back_ref, lo_ref,
    out_ref, grad_ref, l1g, l1b, qkvg, qvb, projg, pjb, l2g, l2b, fc1g, f1b, fc2g, f2b, buf, own_buf, back_buf, lo_buf, sems,
):
    side = lax.axis_index("seq")
    owner = 2 * lax.axis_index("img") + side
    images, half, width = own_ref.shape
    unit = u_ref.shape[0]
    arrivals = [
        pltpu.make_async_copy(back_ref, back_buf, sems.at[0]), pltpu.make_async_copy(own_ref, own_buf, sems.at[1]),
        pltpu.make_async_copy(lo_ref, lo_buf, sems.at[2]),
    ]
    for copy in arrivals:
        copy.start()
    arrivals[0].wait()
    buf[...] = back_buf[...].astype(F32)
    other = pltpu.make_async_copy(buf, grad_ref.at[pl.ds((1 - side) * images, images)], sems.at[0])
    other.start()
    arrivals[1].wait()
    mine = pltpu.make_async_copy(own_buf, grad_ref.at[pl.ds(side * images, images)], sems.at[1])
    mine.start()
    arrivals[2].wait()
    keep = pltpu.make_async_copy(lo_buf, out_ref, sems.at[2])
    keep.start()
    fc2g[...] = fc2_ref[...]
    fc1g[...] = fc1_ref[...]
    projg[...] = proj_ref[...]
    lane = lax.broadcasted_iota(jnp.int32, (unit, width), 1)
    slot = lax.broadcasted_iota(jnp.int32, (unit, width), 0)
    here = lane == owner * unit + slot
    column = lambda ref: jnp.sum(jnp.where(here, ref[...].reshape(1, width), 0.0), axis=1, keepdims=True)
    gain, bias = column(gain_ref), column(bias_ref)
    gain_sum = bias_sum = 0.0
    for k, at in enumerate((2, 0, 3)):
        cut = slice(k * width, k * width + width)
        total, weight, sums = u_ref[:, cut], w_ref[:, cut].astype(F32), sums_ref[at : at + 1, :]
        qkvg[:, cut] = gain * total + bias * sums
        gain_sum += jnp.sum(weight * total, axis=1, keepdims=True)
        bias_sum += jnp.sum(weight * sums, axis=1, keepdims=True)
    diag = lax.broadcasted_iota(jnp.int32, (unit, 128), 1) == lax.broadcasted_iota(jnp.int32, (unit, 128), 0)
    for ref, value in ((l1g, gain_sum), (l1b, bias_sum)):
        ref[...] = jnp.sum(jnp.where(diag, value, 0.0), axis=0, keepdims=True)[0, :unit]
    for ref, at, count in ((pjb, 4, 1), (l2g, 5, 1), (l2b, 6, 1), (f2b, 11, 1), (f1b, 7, 4), (qvb, 2, 2)):
        size = unit * count
        place = owner * size
        which, start = place // width, place % width
        row = sums_ref[at : at + 1, :]
        for k in range(1, count):
            row = jnp.where(which == k, sums_ref[at + k : at + k + 1, :], row)
        sel = lax.broadcasted_iota(jnp.int32, (size, width), 1) == start + lax.broadcasted_iota(jnp.int32, (size, width), 0)
        tall = jnp.sum(jnp.where(sel, row, 0.0), axis=1, keepdims=True)
        eye = lax.broadcasted_iota(jnp.int32, (size, 128), 1) == lax.broadcasted_iota(jnp.int32, (size, 128), 0)
        ref[...] = jnp.sum(jnp.where(eye, tall, 0.0), axis=0, keepdims=True)[0, :size]
    keep.wait()
    mine.wait()
    other.wait()


def emit(fc2, fc1, u, proj, sums, gain, bias, qkv_weight, own, back, layer_out):
    images, half, width = own.shape
    unit = u.shape[0]
    hbm = pl.BlockSpec(memory_space=pl.ANY)
    whole = lambda v: pl.BlockSpec(v.shape, lambda i: (0,) * len(v.shape))
    shape = lambda *dims: jax.ShapeDtypeStruct(dims, F32)
    outs = [
        shape(unit), shape(unit), shape(unit, 3 * width), shape(2 * unit), shape(unit, width), shape(unit), shape(unit),
        shape(unit), shape(*fc1.shape), shape(fc1.shape[1] // GROUP), shape(*fc2.shape), shape(unit),
    ]
    return pl.pallas_call(
        emit_kernel,
        grid=(1,),
        in_specs=[whole(v) for v in (fc2, fc1, u, proj, sums, gain, bias)]
        + [pl.BlockSpec((unit, 3 * width), lambda i: (2 * lax.axis_index("img") + lax.axis_index("seq"), 0)), hbm, hbm, hbm],
        out_specs=[hbm, hbm] + [whole(v) for v in outs],
        scratch_shapes=[
            pltpu.VMEM(own.shape, F32), pltpu.VMEM(own.shape, F32), pltpu.VMEM(back.shape, BF16),
            pltpu.VMEM(layer_out.shape, BF16), pltpu.SemaphoreType.DMA((3,)),
        ],
        out_shape=[jax.ShapeDtypeStruct(layer_out.shape, BF16), shape(2 * images, half, width)] + outs,
        compiler_params=pltpu.CompilerParams(vmem_limit_bytes=63 * MIB),
        name="emit",
    )(fc2, fc1, u, proj, sums, gain, bias, qkv_weight, own, back, layer_out)


MESH = pl.DeviceIdType.MESH
PARTS = 7
SLOTS = 3
GROUP = 32


class Far:
    def __init__(self, ends, send_sem, recv_sem, peer):
        self.parts = (ends, send_sem, recv_sem, peer)
        self.build().start()

    def build(self):
        ends, send_sem, recv_sem, peer = self.parts
        src, dst = ends()
        return pltpu.make_async_remote_copy(
            src_ref=src, dst_ref=dst, send_sem=send_sem(), recv_sem=recv_sem(), device_id=peer, device_id_type=MESH
        )

    def wait(self):
        self.build().wait()


class Parcel:
    def __init__(self, keep, send, landing, levels, sems, order, place, names="wvyx"):
        self.keep, self.send, self.landing, self.levels, self.sems = keep, send, landing, levels, sems
        self.order, self.place, self.names = order, place, names

    def copy(self, src, dst, slot, peer):
        send_sem, recv_sem = self.sems
        return pltpu.make_async_remote_copy(
            src_ref=src, dst_ref=dst, send_sem=send_sem(slot), recv_sem=recv_sem(slot), device_id=peer, device_id_type=MESH
        )

    def bring(self, step):
        if step == 0:
            return self.copy(self.send(), self.landing(), 0, self.place["core"][1])
        name, used = self.order[step - 1], self.order[:step]
        spot = tuple(
            self.place[n][2] if n == name else self.place[n][0] if n in used else slice(None) for n in self.names
        )
        return self.copy(self.keep().at[spot], self.levels(step - 1), step, self.place[name][1])

    def start(self):
        self.bring(0).start()

    def gather(self, step):
        self.bring(step).wait()
        return self.add(step)

    def add(self, step):
        used = self.order[:step]
        left = [n for n in self.names if n not in used]
        arrived = self.levels(step - 1) if step else self.landing()

        def one(i):
            at = {}
            for n in reversed(left):
                at[n] = i % 2
                i = i // 2
            inner = tuple(at[n] for n in left)
            spot = tuple(at[n] if n in at else self.place[n][0] for n in self.names)
            total = self.keep()[spot].astype(F32) + arrived[inner].astype(F32)
            if step == len(self.order):
                return total
            self.keep()[spot] = total.astype(BF16)

        if not left:
            return one(0)
        pl.loop(0, 2 ** len(left))(lambda i: one(i) and None)

    def launch(self, step):
        self.bring(step + 1).start()

    def move(self, step):
        self.gather(step)
        self.launch(step)


class HalfParcel(Parcel):
    def launch(self, step):
        if step < 3:
            return super().launch(step)

        @pl.when(self.goes)
        def _():
            self.bring(4).start()

    def finish(self, write):
        @pl.when(self.goes)
        def _():
            self.bring(4).wait_send()

        @pl.when(self.mine)
        def _():
            self.bring(4).wait_recv()
            write(self.add(4))


def level_shapes(names, order, rows, cols):
    return [
        (2,) * len([n for n in names if n not in order[: step + 1]]) + (rows, cols) for step in range(len(order))
    ]


ORDERS = ("yvxw", "yvxw", "wxvy", "xwvy", "yvwx", "yvwx", "vyxw")
FC2_A, FC2_B, FC1_A, FC1_B, VAL_PROJ, QUERY, KEY = range(7)
PLAN = {
    "b02": ((FC2_B, 0),),
    "b24": ((FC1_B, 0),),
    "c01": ((FC2_A, 1),),
    "c04": ((VAL_PROJ, 0),),
    "c12": ((FC2_B, 1),),
    "c15": ((FC2_A, 2),),
    "c20": ((FC1_A, 1),),
    "c22": ((FC1_B, 1),),
    "c25": ((FC2_A, 3), (FC2_B, 2), (VAL_PROJ, 1)),
    "key": ((QUERY, 0),),
    "input0": ((KEY, 0), (FC2_B, 3)),
    "input1": ((VAL_PROJ, 2), (QUERY, 1)),
    "input2": ((FC1_A, 2), (FC2_A, 4), (KEY, 1)),
    "end0": ((FC2_B, 4), (FC1_B, 2), (QUERY, 2), (KEY, 2)),
    "end1": (
        (FC1_A, 3), (VAL_PROJ, 3), (FC1_B, 3), (KEY, 3), (QUERY, 3), (FC1_A, 4), (VAL_PROJ, 4), (FC1_B, 4), (QUERY, 4),
        (KEY, 4),
    ),
}


def rest_kernel(
    grid_ref, split_ref, owner_ref, drop_ref, patches_hbm, cot_hbm, w1_hbm, w2_hbm, wp_hbm, wqkv_hbm,
    g1_ref, b1_ref, qv_ref, pb_ref, g2_ref, b2_ref, c1_ref, c2_ref,
    fc2_ref, fc1_ref, qkvg_ref, projg_ref, vec_ref, out_ref, grad_ref, back_ref, unit_hbm, qkv_hbm, probs_hbm, att_hbm,
    cot, rstd_one, rows_ref, dn2, mid, acc, left, right, wbuf, qkv, probs, djoin, datt, tile, ost, gsend, grecv, vec, vget,
    keep_a, send_a, land_a, keep_b, send_b, land_b, keep_c, send_c, land_c, *others,
):
    levels = [others[4 * k : 4 * k + 4] for k in range(PARTS)]
    (load_sem, probs_sem, qkv_sem, w_sem, open_sem, open_send, open_recv, send_sem, recv_sem, side_send, side_recv, vec_send, vec_recv, out_sem,
     free_sem) = others[4 * PARTS :]
    images, rows, width = dn2.shape
    half = rows // 2
    pairs = width // 128
    steps = w1_hbm.shape[1] // width
    line = lax.axis_index("img")
    x = lax.axis_index("seq")
    core = line % 2
    y = (line // 2) % 2
    z = line // 4
    sibling = (line + 1 - 2 * core, x)
    level = (line + 2 - 4 * y, x)
    across = (line, 1 - x)
    scal_ref = Facts((grid_ref, split_ref, owner_ref, drop_ref), images, x)
    zv, zw = z % 2, z // 2
    near_z = (line + 4 - 8 * zv, x)
    far_z = (line + 8 - 16 * zw, x)
    peers = [sibling, level, across, near_z, far_z]
    barrier = pltpu.get_barrier_semaphore()
    for peer in peers:
        pl.semaphore_signal(barrier, inc=1, device_id=peer, device_id_type=MESH)

    loads = []

    def fetch(src, dst):
        copy = pltpu.make_async_copy(src, dst, load_sem.at[len(loads)])
        copy.start()
        loads.append(copy)
        return copy

    def probs_copy(index, slot):
        return pltpu.make_async_copy(
            probs_hbm.at[index // pairs, pl.ds(2 * (index % pairs), 2)], probs.at[slot], probs_sem.at[slot]
        )

    def qkv_copy(i, slot):
        return pltpu.make_async_copy(qkv_hbm.at[i], qkv.at[slot], qkv_sem.at[slot])

    def w1_copy(t, slot):
        at = pl.multiple_of(t * width, 128)
        return pltpu.make_async_copy(w1_hbm.at[:, pl.ds(at, width)], wbuf.at[slot], w_sem.at[slot])

    def w2_copy(t, slot):
        at = pl.multiple_of(t * width, 128)
        return pltpu.make_async_copy(w2_hbm.at[pl.ds(at, width), :], wbuf.at[2 + slot], w_sem.at[2 + slot])

    def x_copy(i):
        return pltpu.make_async_copy(patches_hbm.at[x * images + i], right.at[i, pl.ds(0, half)], open_sem.at[i])

    def x_far(i):
        return pltpu.make_async_remote_copy(
            src_ref=patches_hbm.at[(1 - x) * images + i], dst_ref=right.at[i, pl.ds(half, half)],
            send_sem=open_send.at[i], recv_sem=open_recv.at[i], device_id=across, device_id_type=MESH,
        )

    def cot_far(i):
        return pltpu.make_async_remote_copy(
            src_ref=cot_hbm.at[(1 - x) * images + i], dst_ref=cot.at[i, pl.ds(half, half)],
            send_sem=open_send.at[images + i], recv_sem=open_recv.at[images + i], device_id=across, device_id_type=MESH,
        )

    def probs_out(index, slot):
        return pltpu.make_async_copy(
            probs.at[slot], probs_hbm.at[index // pairs, pl.ds(2 * (index % pairs), 2)], probs_sem.at[slot]
        )

    def saves(i):
        return [
            pltpu.make_async_copy(datt.at[i], unit_hbm.at[i], open_sem.at[images + 4 * i]),
            pltpu.make_async_copy(djoin.at[i], qkv_hbm.at[i], open_sem.at[images + 4 * i + 1]),
            pltpu.make_async_copy(ost.at[i], att_hbm.at[i, pl.ds(0, half)], open_sem.at[images + 4 * i + 2]),
            pltpu.make_async_copy(gsend.at[i], att_hbm.at[i, pl.ds(half, half)], open_sem.at[images + 4 * i + 3]),
        ]

    def wqkv_copy(k, slot):
        return pltpu.make_async_copy(wqkv_hbm.at[:, pl.ds(k * width, width)], wbuf.at[slot], w_sem.at[slot])

    def wp_copy(slot):
        return pltpu.make_async_copy(wp_hbm, wbuf.at[slot], w_sem.at[slot])

    def write_folds(total, ref, tile_at):
        for t in range(total.shape[1] // side_cols):
            for h in range(2):
                at = (tile_at + t) * width + h * side_cols
                ref[:, at : at + side_cols] = total[h * unit : h * unit + unit, t * side_cols : t * side_cols + side_cols]

    def write_fc2(total):
        fc2_ref[...] = total

    def write_out(k):
        if k in (FC2_A, FC2_B):
            return parcels[k].finish(write_fc2)
        total = parcels[k].gather(4)
        if k == VAL_PROJ:
            write_folds(total[:, :side_cols], qkvg_ref, 2)
            write_folds(total[:, side_cols:], projg_ref, 0)
        else:
            ref, tile_at = {FC1_A: (fc1_ref, 0), FC1_B: (fc1_ref, 2), QUERY: (qkvg_ref, 0), KEY: (qkvg_ref, 1)}[k]
            write_folds(total, ref, tile_at)

    def at_point(name):
        for k, step in PLAN.get(name, ()):
            if step == 0:
                step_one(k)
            elif step < 4:
                parcels[k].move(step)
            else:
                write_out(k)

    def plan_of(tag):
        return {
            (int(name[1]), int(name[2])): (lambda name=name: at_point(name))
            for name in PLAN if len(name) == 3 and name[0] == tag and name[1:].isdigit()
        }

    def pump(plan, i, pair):
        for (image, at), job in plan.items():
            if at == pair:

                @pl.when(i == image)
                def _():
                    job()

    first_plan = {
        (0, 3): lambda: x_far(2).start(),
        (1, 1): lambda: cot_far(0).start(),
        (2, 3): lambda: cot_far(2).start(),
    }
    weights_in = [wqkv_copy(0, 0), wqkv_copy(1, 2), wqkv_copy(2, 3), wp_copy(1)]
    x_copy(0).start()
    pl.semaphore_wait(barrier, len(peers))
    x_far(0).start()
    for copy in weights_in:
        copy.start()
    for i in range(1, images):
        x_copy(i).start()
    cot_in = fetch(cot_hbm.at[pl.ds(x * images, images)], cot.at[:, pl.ds(0, half)])
    line_of = lambda ref: ref[...].reshape(1, -1)
    for k in range(steps):
        rows_ref[k : k + 1, :] = line_of(c1_ref)[:, k * width : k * width + width]
    for k, ref in enumerate((c2_ref, g1_ref, b1_ref, g2_ref, b2_ref, pb_ref)):
        rows_ref[4 + k : 5 + k, :] = line_of(ref)
    rows_ref[10:11, :] = line_of(qv_ref)[:, :width]
    rows_ref[11:12, :] = line_of(qv_ref)[:, width:]
    vector = lambda k: rows_ref[k : k + 1, :]
    low_lane = lax.broadcasted_iota(jnp.int32, (rows, 128), 1) < HEAD_DIM
    sides = (low_lane, jnp.logical_not(low_lane))
    cuts = lambda pair: [slice(k * width + 128 * pair, k * width + 128 * pair + 128) for k in range(3)]
    vec[...] = jnp.zeros_like(vec)
    acc[...] = jnp.zeros_like(acc)
    dn2[...] = jnp.zeros_like(dn2)
    for copy in weights_in:
        copy.wait()

    @pl.loop(0, images)
    def _(i):
        x_copy(i).wait()
        x_far(i).wait()

        @pl.when(i == 0)
        def _():
            x_far(1).start()

        @pl.when(i == images - 1)
        def _():
            cot_far(1).start()

        unit_one, rstd = norm_parts(right[i].astype(F32))
        datt[i] = unit_one.astype(BF16)
        rstd_one[i] = rstd
        n1 = (unit_one * vector(5) + vector(6)).astype(BF16)
        djoin[i, :, :width] = (dot_nn(n1, wbuf[0]) + vector(10)).astype(BF16) * BF16(HEAD_DIM**-0.5)
        djoin[i, :, width : 2 * width] = dot_nn(n1, wbuf[2]).astype(BF16)
        djoin[i, :, 2 * width :] = (dot_nn(n1, wbuf[3]) + vector(11)).astype(BF16)

        @pl.when(i == images - 1)
        def _():
            w1_copy(0, 0).start()
            w2_copy(0, 0).start()

        fill = jnp.where(row_valid(scal_ref, i, rows, half, 0), 0.0, MASK_FILL)
        for pair in range(pairs):
            index = i * pairs + pair
            slot = index % SLOTS

            @pl.when(index >= SLOTS)
            def _():
                probs_out(index - SLOTS, slot).wait()

            q_cut, k_cut, v_cut = cuts(pair)
            q2, k2, v2 = djoin[i, :, q_cut], djoin[i, :, k_cut], djoin[i, :, v_cut]
            total = None
            for side in range(2):
                scores = dot_nt(k2, jnp.where(sides[side], q2, 0)) + fill
                top = jnp.max(scores, axis=0, keepdims=True)
                weight = jnp.exp(scores - top)
                low = (weight * (1.0 / jnp.sum(weight, axis=0, keepdims=True))).astype(BF16)
                probs[slot, side] = low
                part = dot_tn(low, jnp.where(sides[side], v2, 0))
                total = part if total is None else total + part
            attended = total.astype(BF16)
            ost[i, :, q_cut] = attended[:half]
            gsend[i, :, q_cut] = attended[half:]
            probs_out(index, slot).start()
            pump(first_plan, i, pair)
        gate = scal_ref[i, 4].astype(F32) * KEEP_SCALE
        attended = jnp.concatenate([ost[i], gsend[i]], axis=0)
        middle = right[i].astype(F32) + gate * (dot_nn(attended, wbuf[1]) + vector(9))
        mid[i] = middle
        unit_two, _ = norm_parts(middle)
        left[i] = (unit_two * vector(7) + vector(8)).astype(BF16)
        for copy in saves(i):
            copy.start()

    for slot in range(SLOTS):
        probs_out(images * pairs - SLOTS + slot, slot).wait()
    for i in range(images):
        for copy in saves(i):
            copy.wait()
    for slot in range(SLOTS):
        probs_copy(slot, slot).start()
    for slot in range(2):
        qkv_copy(slot, slot).start()
    cot_in.wait()

    place = {
        "core": (core, sibling), "y": (y, level, 1 - y), "x": (x, across, 1 - x),
        "v": (zv, near_z, 1 - zv), "w": (zw, far_z, 1 - zw),
    }
    homes = [
        (keep_a.at[0], send_a, land_a), (keep_a.at[1], send_a, land_a),
        (keep_b.at[0], send_b.at[0], land_b.at[0]), (keep_b.at[1], send_b.at[1], land_b.at[1]),
        (keep_b.at[2], send_b.at[0], land_b.at[0]),
        (keep_c.at[0], send_c.at[0], land_c.at[0]), (keep_c.at[1], send_c.at[1], land_c.at[1]),
    ]
    parcels = []
    for k in range(PARTS):
        keep, send, land = (lambda k=k, n=n: homes[k][n] for n in range(3))
        sems = (lambda slot, k=k: send_sem.at[k, slot]), (lambda slot, k=k: recv_sem.at[k, slot])
        build = HalfParcel if k < 2 else Parcel
        parcels.append(
            build(keep, send, land, lambda step, k=k: levels[k][step], sems, ORDERS[k], place, "vyx" if k < 2 else "wvyx")
        )
    for k in range(2):
        parcels[k].goes, parcels[k].mine = zw != k, zw == k
    free_slot = {FC2_A: 0, FC1_A: 1}
    needs = {FC2_B: 0, VAL_PROJ: 1}

    def release(k):
        pl.semaphore_signal(free_sem.at[free_slot[k]], inc=1, device_id=sibling, device_id_type=MESH)

    def start(k):
        if k in needs:
            pl.semaphore_wait(free_sem.at[needs[k]], 1)
        parcels[k].start()

    r, c = keep_b.shape[-2], keep_b.shape[-1]
    unit, side_cols = r // 2, c // 2

    def put_block_rows(k, zz):
        for ref, who in ((send_a, 1 - core), (keep_a.at[k], core)):
            for b in range(2):
                for e in range(2):
                    at = pl.multiple_of((2 * b + who) * 4 * r + e * 2 * r, 8)
                    ref[zz, b, e] = tile[pl.ds(at, 2 * r), :].astype(BF16)

    def put_folds(send, kept, t):
        spot = pl.ds(pl.multiple_of(t * side_cols, 128), side_cols)

        @pl.loop(0, 8)
        def _(k):
            for ref, who in ((send, 1 - core), (kept, core)):
                for e in range(2):
                    at = pl.multiple_of((4 * k + 2 * who + e) * unit, 8)
                    piece = tile[pl.ds(at, unit), :]
                    ref[k // 4, (k // 2) % 2, k % 2, e, :, spot] = jnp.concatenate(
                        [piece[:, :side_cols], piece[:, side_cols:]], axis=0
                    ).astype(BF16)

    def step_one(k):
        parcels[k].gather(0)
        if k in free_slot:
            release(k)
        parcels[k].launch(0)

    flat = lambda ref: ref[...].reshape(images * rows, ref.shape[-1])
    column = lambda k: djoin[:, :, k * width : k * width + width].reshape(images * rows, width)

    @pl.loop(0, steps)
    def _(t):
        slot = t % 2
        w1_copy(t, slot).wait()
        w2_copy(t, slot).wait()

        @pl.when(t + 1 < steps)
        def _():
            w1_copy(t + 1, 1 - slot).start()
            w2_copy(t + 1, 1 - slot).start()

        @pl.when(t + 1 == steps)
        def _():
            wqkv_copy(0, 0).start()
            wp_copy(2).start()

        @pl.when(t == 2)
        def _():
            start(FC2_A)
            start(FC1_A)

        for i in range(images):
            hidden, slope = gelu_both(dot_nn(left[i], wbuf[slot]) + rows_ref[pl.ds(t, 1), :])
            hidden = hidden.astype(BF16)
            djoin[i, :, :width] = hidden
            djoin[i, :, 2 * width :] = slope.astype(BF16)
            acc[i] += dot_nn(hidden, wbuf[2 + slot])

        @pl.when(t == 0)
        def _():
            for i in range(images):
                cot_far(i).wait()
                gate = scal_ref[i, 5].astype(F32) * KEEP_SCALE
                live = row_valid(scal_ref, i, rows, half, 0)
                d_mlp = (jnp.where(live, cot[i].astype(F32), 0.0) * gate).astype(BF16)
                right[i] = d_mlp
                vec[11:12, :] += jnp.sum(d_mlp.astype(F32), axis=0, keepdims=True)

        for i in range(images):
            d_pre = (djoin[i, :, 2 * width :].astype(F32) * dot_nt(right[i], wbuf[2 + slot])).astype(BF16)
            djoin[i, :, width : 2 * width] = d_pre
            vec[pl.ds(7 + t, 1), :] += jnp.sum(d_pre.astype(F32), axis=0, keepdims=True)
            dn2[i] += dot_nt(d_pre, wbuf[slot])

        tile[...] = dot_tn(column(0), flat(right))

        @pl.when(t == 2)
        def _():
            for k in (FC2_A, FC1_A):
                step_one(k)

        for k in range(2):

            @pl.when(t // 2 == k)
            def _():
                put_block_rows(k, t % 2)

        tile[...] = dot_tn(flat(left), column(1))
        for k in range(2):

            @pl.when(t // 2 == k)
            def _():
                put_folds(send_b.at[k], keep_b.at[k], t % 2)

    wqkv_copy(1, 1).start()
    wqkv_copy(2, 3).start()
    unit_in, att_in = fetch(unit_hbm, left), fetch(att_hbm, right)
    start(FC2_B)
    start(FC1_B)
    for i in range(images):
        gate = scal_ref[i, 5].astype(F32) * KEEP_SCALE
        final = mid[i] + gate * (acc[i] + rows_ref[4:5, :])
        out = jnp.where(row_valid(scal_ref, i, rows, half, 0), final, 0.0).astype(BF16)
        ost[i] = out[:half]
        gsend[i] = out[half:]
    out_own = pltpu.make_async_copy(ost, out_ref.at[pl.ds(x * images, images)], out_sem.at[0])
    out_own.start()
    out_far = Far(
        lambda: (gsend, out_ref.at[pl.ds(x * images, images)]), lambda: side_send.at[images], lambda: side_recv.at[images], across
    )

    wp_copy(2).wait()
    for i in range(images):
        live = row_valid(scal_ref, i, rows, half, 0)
        d_final = jnp.where(live, cot[i].astype(F32), 0.0)
        unit_two, rstd = norm_parts(mid[i])
        d_normed = dn2[i]
        vec[5:6, :] += jnp.sum(d_normed * unit_two, axis=0, keepdims=True)
        vec[6:7, :] += jnp.sum(d_normed, axis=0, keepdims=True)
        d_middle = d_final + norm_back(d_normed, rows_ref[7:8, :], unit_two, rstd)
        dn2[i] = d_middle
        gate = scal_ref[i, 4].astype(F32) * KEEP_SCALE
        d_branch = (d_middle * gate).astype(BF16)
        datt[i] = d_branch
        vec[4:5, :] += jnp.sum(d_branch.astype(F32), axis=0, keepdims=True)
    at_point("norm")
    unit_in.wait()
    att_in.wait()
    tile[...] = dot_tn(flat(right), flat(datt))
    put_folds(send_b.at[0], keep_b.at[2], 1)
    at_point("proj")
    for i in range(images):
        datt[i] = dot_nt(datt[i], wbuf[2]).astype(BF16)
    at_point("back")

    total_pairs = images * pairs

    def next_probs(index, slot):
        @pl.when(index + SLOTS < 2 * total_pairs)
        def _():
            probs_copy((index + SLOTS) % total_pairs, slot).start()

    @pl.loop(0, images)
    def _(i):
        for pair in range(pairs):
            index = i * pairs + pair
            slot = index % SLOTS
            probs_copy(index, slot).wait()
            q_cut, _, v_cut = cuts(pair)
            a2 = datt[i, :, q_cut]
            dv = dot_nn(probs[slot, 0], jnp.where(sides[0], a2, 0)) + dot_nn(probs[slot, 1], jnp.where(sides[1], a2, 0))
            djoin[i, :, v_cut] = dv.astype(BF16)
            next_probs(index, slot)
            pump(plan_of("b"), i, pair)
        vec[3:4, :] += jnp.sum(djoin[i, :, 2 * width :].astype(F32), axis=0, keepdims=True)

    tile[...] = dot_tn(flat(left), column(2))
    put_folds(send_b.at[0], keep_b.at[2], 0)
    start(VAL_PROJ)

    @pl.loop(0, images)
    def _(i):
        q_slot = i % 2
        qkv_copy(i, q_slot).wait()
        for pair in range(pairs):
            index = total_pairs + i * pairs + pair
            slot = index % SLOTS
            probs_copy(index - total_pairs, slot).wait()
            q_cut, k_cut, v_cut = cuts(pair)
            q2, k2, v2, a2 = qkv[q_slot, :, q_cut], qkv[q_slot, :, k_cut], qkv[q_slot, :, v_cut], datt[i, :, q_cut]
            dq = dk = None
            for side in range(2):
                high = probs[slot, side].astype(F32)
                d_probs = dot_nt(v2, jnp.where(sides[side], a2, 0))
                inner = jnp.sum(high * d_probs, axis=0, keepdims=True)
                d_scores = (high * (d_probs - inner)).astype(BF16)
                parts = dot_tn(d_scores, jnp.where(sides[side], k2, 0)), dot_nn(d_scores, jnp.where(sides[side], q2, 0))
                dq, dk = parts if dq is None else (dq + parts[0], dk + parts[1])
            djoin[i, :, q_cut] = (dq * HEAD_DIM**-0.5).astype(BF16)
            djoin[i, :, k_cut] = dk.astype(BF16)
            next_probs(index, slot)
            pump(plan_of("c"), i, pair)

        @pl.when(i + 2 < images)
        def _():
            qkv_copy(i + 2, q_slot).start()

        vec[2:3, :] += jnp.sum(djoin[i, :, :width].astype(F32), axis=0, keepdims=True)
        vec[0:1, :] += jnp.sum(djoin[i, :, width : 2 * width].astype(F32), axis=0, keepdims=True)

    for t, k in ((0, QUERY), (1, KEY)):
        tile[...] = dot_tn(flat(left), column(t))
        put_folds(send_c.at[t], keep_c.at[t], 0)
        start(k)
    at_point("key")
    wqkv_copy(0, 0).wait()
    wqkv_copy(1, 1).wait()
    wqkv_copy(2, 3).wait()
    out_far.wait()

    def input_grad(i):
        d_normed = dot_nt(djoin[i, :, :width], wbuf[0])
        d_normed += dot_nt(djoin[i, :, width : 2 * width], wbuf[1])
        d_normed += dot_nt(djoin[i, :, 2 * width :], wbuf[3])
        out = dn2[i] + norm_back(d_normed, rows_ref[5:6, :], left[i].astype(F32), rstd_one[i])
        acc[i, :half] = out[:half]
        gsend[i] = out[half:].astype(BF16)

    def exchange(k):
        return Far(lambda: (vec, vget.at[k]), lambda: vec_send.at[k], lambda: vec_recv.at[k], peers[k])

    def settle(k, trade):
        trade.wait()
        vec[...] += vget[k]

    swaps = []

    def swap_out(i):
        swaps.append(
            Far(lambda: (gsend.at[i], grecv.at[i]), lambda: side_send.at[i], lambda: side_recv.at[i], across)
        )

    for i in range(images):
        trade = exchange(i)
        input_grad(i)
        swap_out(i)
        settle(i, trade)
        if i + 1 < images:
            at_point("input%d" % i)
    grad_own = pltpu.make_async_copy(acc.at[:, pl.ds(0, half)], grad_ref, out_sem.at[1])
    grad_own.start()
    trade = exchange(3)
    at_point("input2")
    settle(3, trade)
    trade = exchange(4)
    at_point("end0")
    settle(4, trade)
    vec_ref[...] = vec[...]
    at_point("end1")
    for copy in swaps:
        copy.wait()
    grad_oth = pltpu.make_async_copy(grecv, back_ref, out_sem.at[2])
    grad_oth.start()
    out_own.wait()
    grad_own.wait()
    grad_oth.wait()


def rest(facts, patches, cotangent, vectors, w):
    all_images, half, width = patches.shape
    images = all_images // 2
    rows = 2 * half
    heads = width // HEAD_DIM
    hidden_width = w["fc1_weight"].shape[1]
    r, c = 2 * (width // GROUP), width
    fc2_rows = hidden_width // GROUP
    hbm = pl.BlockSpec(memory_space=pl.ANY)
    vmem = pl.BlockSpec(memory_space=pltpu.VMEM)
    smem = pl.BlockSpec(memory_space=pltpu.SMEM)
    dma = pltpu.SemaphoreType.DMA
    whole = lambda dtype: pltpu.VMEM((images, rows, width), dtype)
    half_block = lambda dtype: pltpu.VMEM((images, half, width), dtype)
    level_bufs = []
    for k, order in enumerate(ORDERS):
        names = "vyx" if k < 2 else "wvyx"
        block = (fc2_rows, width) if k < 2 else (r, c) if k < 5 else (r, c // 2)
        level_bufs += [pltpu.VMEM(shape, BF16) for shape in level_shapes(names, order, *block)]
    rows_of = lambda *lead: pltpu.VMEM(lead + (2, 2, 2, fc2_rows, width), BF16)
    folds_of = lambda count, cols: pltpu.VMEM((count, 2, 2, 2, 2, r, cols), BF16)
    return pl.pallas_call(
        rest_kernel,
        in_specs=[smem] * 4 + [hbm] * 6 + [vmem] * 8,
        out_specs=[vmem] * 5 + [hbm] * 7,
        out_shape=[
            jax.ShapeDtypeStruct((fc2_rows, width), F32),
            jax.ShapeDtypeStruct((r // 2, hidden_width), F32),
            jax.ShapeDtypeStruct((r // 2, 3 * width), F32),
            jax.ShapeDtypeStruct((r // 2, width), F32),
            jax.ShapeDtypeStruct((16, width), F32),
            jax.ShapeDtypeStruct((2 * images, half, width), BF16),
            jax.ShapeDtypeStruct((images, half, width), F32),
            jax.ShapeDtypeStruct((images, half, width), BF16),
            jax.ShapeDtypeStruct((images, rows, width), BF16),
            jax.ShapeDtypeStruct((images, rows, 3 * width), BF16),
            jax.ShapeDtypeStruct((images, heads, rows, rows), BF16),
            jax.ShapeDtypeStruct((images, rows, width), BF16),
        ],
        scratch_shapes=[
            whole(BF16), pltpu.VMEM((images, rows, 1), F32), pltpu.VMEM((16, width), F32), whole(F32), whole(F32), whole(F32), whole(BF16), whole(BF16),
            pltpu.VMEM((4, width, width), BF16),
            pltpu.VMEM((2, rows, 3 * width), BF16),
            pltpu.VMEM((SLOTS, 2, rows, rows), BF16),
            pltpu.VMEM((images, rows, 3 * width), BF16),
            whole(BF16),
            pltpu.VMEM((width, width), F32),
            half_block(BF16), half_block(BF16), half_block(BF16),
            pltpu.VMEM((16, width), F32),
            pltpu.VMEM((5, 16, width), F32),
            rows_of(2), rows_of(), rows_of(),
            folds_of(3, c), folds_of(2, c), folds_of(2, c),
            folds_of(2, c // 2), folds_of(2, c // 2), folds_of(2, c // 2),
            *level_bufs,
            dma((4,)), dma((SLOTS,)), dma((2,)), dma((4,)), dma((5 * images,)), dma((2 * images,)), dma((2 * images,)),
            dma((PARTS, 5)), dma((PARTS, 5)), dma((images + 1,)),
            dma((images + 1,)), dma((5,)), dma((5,)), dma((3,)), pltpu.SemaphoreType.REGULAR((2,)),
        ],
        compiler_params=pltpu.CompilerParams(collective_id=0, has_side_effects=True, vmem_limit_bytes=64 * MIB),
        name="rest",
    )(*facts, patches, cotangent, w["fc1_weight"], w["fc2_weight"], w["proj_weight"], w["qkv_weight"], *vectors)


def spread(value):
    return lax.psum_scatter(value, ("img", "seq"), scatter_dimension=0, tiled=True)


def unfold(send, keep, core, folds):
    rows, cols = send.shape[-2], send.shape[-1]
    send, keep = (v.reshape(GROUP // 4, 2, rows, cols) for v in (send, keep))
    both = jnp.stack([jnp.where(core == 0, keep, send), jnp.where(core == 0, send, keep)], axis=1).astype(F32)
    if folds == 1:
        return both.reshape(GROUP * rows, cols)
    tiles = 4
    both = both.reshape(GROUP, 2, rows // 2, tiles, cols // tiles)
    return both.transpose(0, 2, 3, 1, 4).reshape(GROUP * rows // 2, 2 * cols)


def swap(value, axis, bit, size):
    return lax.ppermute(value, axis, [(i, i ^ bit) for i in range(size)])


def shards(img_size, args):
    (patches, grid_shape, split_rows, owner_shard, drop_masks, ln1_gain, ln1_bias, qkv_weight, qv_bias, proj_weight,
     proj_bias, ln2_gain, ln2_bias, fc1_weight, fc1_bias, fc2_weight, fc2_bias, cotangent) = args
    all_images, _, half, width = patches.shape
    images = all_images // 2
    rows = 2 * half
    tokens = images * rows
    side = lax.axis_index("seq")
    line = lax.axis_index("img")
    owners = 2 * img_size
    row = lambda v: v.reshape(1, -1)
    w = dict(
        ln1_gain=row(ln1_gain), ln1_bias=row(ln1_bias), qkv_weight=qkv_weight, q_bias=row(qv_bias[:width]),
        v_bias=row(qv_bias[width:]), proj_weight=proj_weight, proj_bias=row(proj_bias), ln2_gain=row(ln2_gain),
        ln2_bias=row(ln2_bias), fc1_weight=fc1_weight, fc1_bias=row(fc1_bias), fc2_weight=fc2_weight, fc2_bias=row(fc2_bias),
    )

    def exchange(value):
        value = value.reshape(all_images, half, width)
        own = lax.dynamic_slice_in_dim(value, side * images, images, axis=0)
        away = lax.dynamic_slice_in_dim(value, (1 - side) * images, images, axis=0)
        return own, swap(away, "seq", 1, 2)

    def place(own, back):
        back = back.astype(own.dtype)
        first = jnp.where(side == 0, own, back)
        second = jnp.where(side == 0, back, own)
        return jnp.concatenate([first, second], axis=0).reshape(all_images, 1, half, width)

    def restore(own, oth):
        return place(own, swap(oth, "seq", 1, 2))

    across = grid_shape[:, 1]
    counts = jnp.stack([split_rows * across, (grid_shape[:, 0] - split_rows) * across], axis=0)
    count_own = jnp.where(side == 0, counts[0], counts[1])
    count_oth = jnp.where(side == 0, counts[1], counts[0])
    special = (owner_shard == side).astype(jnp.int32)
    table = jnp.stack([count_own, special, count_oth, 1 - special, drop_masks[:, 0], drop_masks[:, 1]], axis=1)
    scal = lax.dynamic_slice_in_dim(table, side * images, images, axis=0)

    flat = lambda v: v.reshape(tokens, v.shape[-1])
    unit1 = width // GROUP
    unit2 = fc2_weight.shape[0] // GROUP
    if owners == GROUP:
        merge = lambda v: v.reshape(all_images, half, width)
        facts = (grid_shape.T, split_rows, owner_shard, drop_masks.T)
        fc2_part, fc1_part, u_part, proj_part, sums, out_part, grad_own, grad_back, *_ = rest(
            facts, merge(patches), merge(cotangent),
            (ln1_gain, ln1_bias, qv_bias, proj_bias, ln2_gain, ln2_bias, fc1_bias, fc2_bias), w,
        )
        outs = emit(
            fc2_part, fc1_part, u_part, proj_part, sums, ln1_gain, ln1_bias, qkv_weight, grad_own, grad_back, out_part
        )
        layer_out, patches_grad = (v.reshape(all_images, 1, half, width) for v in outs[:2])
        return (layer_out, patches_grad, *outs[2:])
    else:
        x_own, x_oth = exchange(patches)
        c_own, c_oth = exchange(cotangent)
        n1, qkv, probs, attended, middle, n2 = front(scal, x_own, x_oth, w)
        mine = lax.rem(line, 2).reshape(1)
        hidden, slope, out_own, out_oth = mlp(scal, flat(n2), flat(middle), w, images, 512)
        layer_out = restore(out_own, out_oth)
        dn2, s2, k2, s1, k1, fc2_bias_grad, fc1_bias_grad = mlp_back(
            scal, mine, c_own, c_oth, flat(n2), hidden, slope, w, unit1, unit2
        )
        dn2 = dn2.reshape(images, rows, width)
        d_middle, d_branch, d_join, ln2_gain_grad, ln2_bias_grad, proj_bias_grad, q_grad, v_grad = attend_back(
            scal, c_own, c_oth, dn2, middle, qkv, probs, w
        )
        st, kt, grad_own, grad_oth, ln1_gain_grad, ln1_bias_grad = tail(
            mine, flat(n1), flat(d_join), flat(attended), flat(d_branch), x_own, x_oth, flat(d_middle), w, unit1
        )
        patches_grad = restore(grad_own, grad_oth)
        vectors = (
            ln1_gain_grad, ln1_bias_grad, jnp.concatenate([q_grad, v_grad], axis=1), proj_bias_grad, ln2_gain_grad,
            ln2_bias_grad, fc1_bias_grad, fc2_bias_grad,
        )
        fc2_grad = spread(unfold(s2, k2, line % 2, 1))
        fc1_grad = spread(unfold(s1, k1, line % 2, 2))
        tail_grad = spread(unfold(st, kt, line % 2, 2))
        qkv_grad, proj_grad = tail_grad[:, : 3 * width], tail_grad[:, 3 * width :]
        pieces = [spread(v.reshape(-1)) for v in vectors]
    l1g, l1b, qvb, pjb, l2g, l2b, f1b, f2b = pieces
    return (
        layer_out, patches_grad, l1g, l1b, qkv_grad, qvb, proj_grad, pjb, l2g, l2b, fc1_grad, f1b, fc2_grad, f2b,
    )


def solution(mesh):
    rep = [P()] * 12
    vec = P(("img", "seq"))
    mat = P(("img", "seq"), None)
    rows = P("img", "seq", None, None)

    def run(*args):
        return shards(mesh.shape["img"], args)

    return jax.shard_map(
        run,
        mesh=mesh,
        in_specs=(rows, P("img", None), P("img"), P("img"), P("img", None), *rep, rows),
        out_specs=(rows, rows, vec, vec, mat, vec, mat, vec, vec, vec, mat, vec, mat, vec),
        check_vma=False,
    )
```

```python
import functools

import jax
import jax.numpy as jnp
from jax import lax
from jax.experimental import pallas as pl
from jax.experimental.pallas import tpu as pltpu
from jax.sharding import PartitionSpec as P

HEAD_DIM = 64
LN_EPS = 1e-06
KEEP_SCALE = 1.0 / 0.9
MASK_FILL = -1e30
BF16 = jnp.bfloat16
F32 = jnp.float32
MIB = 1024 * 1024


def dot_nn(a, b):
    return lax.dot_general(a, b, (((1,), (0,)), ((), ())), preferred_element_type=F32)


def dot_nt(a, b):
    return lax.dot_general(a, b, (((1,), (1,)), ((), ())), preferred_element_type=F32)


def dot_tn(a, b):
    return lax.dot_general(a, b, (((0,), (0,)), ((), ())), preferred_element_type=F32)


def norm_parts(values):
    row_mean = jnp.mean(values, axis=-1, keepdims=True)
    centred = values - row_mean
    variance = jnp.mean(centred * centred, axis=-1, keepdims=True)
    rstd = lax.rsqrt(variance + LN_EPS)
    return centred * rstd, rstd


def norm_back(d_normed, gain, unit, rstd):
    d_unit = d_normed * gain
    mean_one = jnp.mean(d_unit, axis=-1, keepdims=True)
    mean_two = jnp.mean(d_unit * unit, axis=-1, keepdims=True)
    return rstd * (d_unit - mean_one - unit * mean_two)


def gelu_both(values):
    cdf = 0.5 + 0.5 * lax.erf(values * 0.7071067811865476)
    return values * cdf, cdf + values * (0.3989422804014327 * jnp.exp(-0.5 * values * values))


class Facts:
    def __init__(self, refs, images, x):
        self.grid, self.split, self.owner, self.drop = refs
        self.images, self.x = images, x

    def __getitem__(self, key):
        image, k = key
        at = self.x * self.images + image
        if k >= 4:
            return self.drop[k - 4, at]
        if k % 2 == 1:
            own = (self.owner[at] == self.x).astype(jnp.int32)
            return own if k == 1 else 1 - own
        across = self.grid[1, at]
        first = self.split[at] * across
        second = (self.grid[0, at] - self.split[at]) * across
        return jnp.where(self.x == k // 2, first, second)


def row_valid(scal_ref, image, rows, half, axis):
    shape = (rows, 1) if axis == 0 else (1, rows)
    slot = lax.broadcasted_iota(jnp.int32, shape, axis)
    other = slot >= half
    place = jnp.where(other, slot - half, slot)
    count = jnp.where(other, scal_ref[image, 2], scal_ref[image, 0])
    special = jnp.where(other, scal_ref[image, 3], scal_ref[image, 1])
    return jnp.where(place < 2, special, (place - 2 < count).astype(jnp.int32)) > 0


def front_kernel(
    scal_ref, own_ref, oth_ref, g1_ref, b1_ref, wqkv_ref, qb_ref, vb_ref, wp_ref, pb_ref, g2_ref, b2_ref,
    n1_ref, qkv_ref, probs_ref, att_ref, mid_ref, n2_ref,
):
    image = pl.program_id(0)
    half, width = own_ref.shape[1], own_ref.shape[2]
    rows = 2 * half
    x = jnp.concatenate([own_ref[0].astype(F32), oth_ref[0].astype(F32)], axis=0)
    unit, _ = norm_parts(x)
    n1 = (unit * g1_ref[...] + b1_ref[...]).astype(BF16)
    n1_ref[0] = n1
    qkv_ref[0, :, :width] = ((dot_nn(n1, wqkv_ref[:, :width]) + qb_ref[...]).astype(BF16) * BF16(HEAD_DIM**-0.5))
    qkv_ref[0, :, width : 2 * width] = dot_nn(n1, wqkv_ref[:, width : 2 * width]).astype(BF16)
    qkv_ref[0, :, 2 * width :] = (dot_nn(n1, wqkv_ref[:, 2 * width :]) + vb_ref[...]).astype(BF16)
    fill = jnp.where(row_valid(scal_ref, image, rows, half, 0), 0.0, MASK_FILL)
    low_lane = lax.broadcasted_iota(jnp.int32, (rows, 128), 1) < HEAD_DIM
    for pair in range(width // 128):
        cut = slice(128 * pair, 128 * pair + 128)
        q2 = qkv_ref[0, :, cut]
        k2 = qkv_ref[0, :, width + 128 * pair : width + 128 * pair + 128]
        v2 = qkv_ref[0, :, 2 * width + 128 * pair : 2 * width + 128 * pair + 128]
        total = None
        for side in range(2):
            mine = low_lane if side == 0 else jnp.logical_not(low_lane)
            scores = dot_nt(k2, jnp.where(mine, q2, 0)) + fill
            top = jnp.max(scores, axis=0, keepdims=True)
            weight = jnp.exp(scores - top)
            probs = (weight * (1.0 / jnp.sum(weight, axis=0, keepdims=True))).astype(BF16)
            probs_ref[0, 2 * pair + side] = probs
            part = dot_tn(probs, jnp.where(mine, v2, 0))
            total = part if total is None else total + part
        att_ref[0, :, cut] = total.astype(BF16)
    keep = scal_ref[image, 4].astype(F32) * KEEP_SCALE
    branch = dot_nn(att_ref[0], wp_ref[...]) + pb_ref[...]
    middle = jnp.concatenate([own_ref[0].astype(F32), oth_ref[0].astype(F32)], axis=0) + keep * branch
    mid_ref[0] = middle
    unit, _ = norm_parts(middle)
    n2_ref[0] = (unit * g2_ref[...] + b2_ref[...]).astype(BF16)


def full(shape):
    zeros = (0,) * len(shape)
    return pl.BlockSpec(shape, lambda *_: zeros, pipeline_mode=pl.Buffered(1))


def front(scal, own, oth, w):
    images, half, width = own.shape
    rows = 2 * half
    heads = width // HEAD_DIM
    per = lambda *tail: pl.BlockSpec((1,) + tail, lambda i, s: (i,) + (0,) * len(tail))
    flops = 2 * images * rows * width * (4 * width + 4 * rows)
    return pl.pallas_call(
        front_kernel,
        grid_spec=pltpu.PrefetchScalarGridSpec(
            num_scalar_prefetch=1,
            grid=(images,),
            in_specs=[
                per(half, width), per(half, width), full((1, width)), full((1, width)),
                full((width, 3 * width)), full((1, width)), full((1, width)),
                full((width, width)), full((1, width)), full((1, width)), full((1, width)),
            ],
            out_specs=[
                per(rows, width), per(rows, 3 * width), per(heads, rows, rows),
                per(rows, width), per(rows, width), per(rows, width),
            ],
        ),
        out_shape=[
            jax.ShapeDtypeStruct((images, rows, width), BF16),
            jax.ShapeDtypeStruct((images, rows, 3 * width), BF16),
            jax.ShapeDtypeStruct((images, heads, rows, rows), BF16),
            jax.ShapeDtypeStruct((images, rows, width), BF16),
            jax.ShapeDtypeStruct((images, rows, width), F32),
            jax.ShapeDtypeStruct((images, rows, width), BF16),
        ],
        compiler_params=pltpu.CompilerParams(vmem_limit_bytes=56 * MIB),
        cost_estimate=pl.CostEstimate(flops=flops, transcendentals=images * heads * rows * rows, bytes_accessed=30_000_000),
        name="front",
    )(scal, own, oth, w["ln1_gain"], w["ln1_bias"], w["qkv_weight"], w["q_bias"], w["v_bias"],
      w["proj_weight"], w["proj_bias"], w["ln2_gain"], w["ln2_bias"])


def mlp_kernel(
    scal_ref, n2_ref, mid_ref, w1_ref, c1_ref, w2_ref, c2_ref,
    hid_ref, slope_ref, own_ref, oth_ref, acc_ref,
):
    step = pl.program_id(0)
    images, half, width = own_ref.shape
    rows = 2 * half
    hidden, slope = gelu_both(dot_nn(n2_ref[...], w1_ref[...]) + c1_ref[...])
    hidden = hidden.astype(BF16)
    hid_ref[...] = hidden
    slope_ref[...] = slope.astype(BF16)
    part = dot_nn(hidden, w2_ref[...])

    @pl.when(step == 0)
    def _():
        acc_ref[...] = part

    @pl.when(step > 0)
    def _():
        acc_ref[...] += part

    @pl.when(step == pl.num_programs(0) - 1)
    def _():
        for image in range(images):
            keep = scal_ref[image, 5].astype(F32) * KEEP_SCALE
            cut = slice(rows * image, rows * image + rows)
            final = mid_ref[cut, :] + keep * (acc_ref[cut, :] + c2_ref[...])
            out = jnp.where(row_valid(scal_ref, image, rows, half, 0), final, 0.0).astype(BF16)
            own_ref[image] = out[:half]
            oth_ref[image] = out[half:]


def mlp(scal, n2, middle, w, images, tile):
    tokens, width = n2.shape
    hidden_width = w["fc1_weight"].shape[1]
    half = tokens // images // 2
    return pl.pallas_call(
        mlp_kernel,
        grid_spec=pltpu.PrefetchScalarGridSpec(
            num_scalar_prefetch=1,
            grid=(hidden_width // tile,),
            in_specs=[
                full((tokens, width)), full((tokens, width)),
                pl.BlockSpec((width, tile), lambda j, s: (0, j)), pl.BlockSpec((1, tile), lambda j, s: (0, j)),
                pl.BlockSpec((tile, width), lambda j, s: (j, 0)), full((1, width)),
            ],
            out_specs=[
                pl.BlockSpec((tokens, tile), lambda j, s: (0, j)), pl.BlockSpec((tokens, tile), lambda j, s: (0, j)),
                full((images, half, width)), full((images, half, width)),
            ],
            scratch_shapes=[pltpu.VMEM((tokens, width), F32)],
        ),
        out_shape=[
            jax.ShapeDtypeStruct((tokens, hidden_width), BF16),
            jax.ShapeDtypeStruct((tokens, hidden_width), BF16),
            jax.ShapeDtypeStruct((images, half, width), BF16),
            jax.ShapeDtypeStruct((images, half, width), BF16),
        ],
        compiler_params=pltpu.CompilerParams(vmem_limit_bytes=56 * MIB),
        cost_estimate=pl.CostEstimate(flops=4 * tokens * width * hidden_width, transcendentals=2 * tokens * hidden_width, bytes_accessed=30_000_000),
        name="mlp",
    )(scal, n2, middle, w["fc1_weight"], w["fc1_bias"], w["fc2_weight"], w["fc2_bias"])


def put_rows(grad_ref, value, send_ref, keep_ref, mine, lead):
    grad_ref[...] = value
    run = 2 * send_ref.shape[-2]
    for k in range(grad_ref.shape[0] // (2 * run)):
        for ref, core in ((send_ref, 1 - mine), (keep_ref, mine)):
            for x in range(2):
                at = pl.multiple_of((2 * k + core) * run + x * (run // 2), 8)
                ref[lead + (k, x)] = grad_ref[pl.ds(at, run // 2), :].astype(BF16)


def put_folded(grad_ref, value, send_ref, keep_ref, mine):
    grad_ref[...] = value
    unit = send_ref.shape[-2] // 2
    side = grad_ref.shape[1] // 2
    for k in range(grad_ref.shape[0] // (4 * unit)):
        for ref, core in ((send_ref, 1 - mine), (keep_ref, mine)):
            for x in range(2):
                at = pl.multiple_of((4 * k + 2 * core + x) * unit, 8)
                piece = grad_ref[pl.ds(at, unit), :]
                ref[k, x] = jnp.concatenate([piece[:, :side], piece[:, side:]], axis=0).astype(BF16)


def mlp_back_kernel(
    scal_ref, mine_ref, own_ref, oth_ref, n2_ref, hid_ref, slope_ref, w1_ref, w2_ref,
    dn2_ref, s2_ref, k2_ref, s1_ref, k1_ref, c2_ref, c1_ref, dmlp_ref, grad_ref, acc_ref,
):
    step = pl.program_id(0)
    images, half, width = own_ref.shape
    rows = 2 * half
    mine = mine_ref[0]

    @pl.when(step == 0)
    def _():
        total = jnp.zeros((1, width), F32)
        for image in range(images):
            keep = scal_ref[image, 5].astype(F32) * KEEP_SCALE
            cot = jnp.concatenate([own_ref[image].astype(F32), oth_ref[image].astype(F32)], axis=0)
            live = row_valid(scal_ref, image, rows, half, 0)
            d_mlp = (jnp.where(live, cot, 0.0) * keep).astype(BF16)
            dmlp_ref[rows * image : rows * image + rows, :] = d_mlp
            total += jnp.sum(d_mlp.astype(F32), axis=0, keepdims=True)
        c2_ref[...] = total

    d_pre = slope_ref[...].astype(F32) * dot_nt(dmlp_ref[...], w2_ref[...])
    d_pre = d_pre.astype(BF16)
    c1_ref[...] = jnp.sum(d_pre.astype(F32), axis=0, keepdims=True)
    part = dot_nt(d_pre, w1_ref[...])
    put_folded(grad_ref, dot_tn(n2_ref[...], d_pre), s1_ref, k1_ref, mine)
    put_rows(grad_ref, dot_tn(hid_ref[...], dmlp_ref[...]), s2_ref, k2_ref, mine, (0,))

    @pl.when(step == 0)
    def _():
        acc_ref[...] = part

    @pl.when(step > 0)
    def _():
        acc_ref[...] += part

    @pl.when(step == pl.num_programs(0) - 1)
    def _():
        dn2_ref[...] = acc_ref[...]


def mlp_back(scal, mine, own, oth, n2, hidden, slope, w, unit1, unit2):
    tokens, width = n2.shape
    images, half, _ = own.shape
    hidden_width = hidden.shape[1]
    tile = width
    steps = hidden_width // tile
    runs1, runs2 = width // (4 * unit1), tile // (4 * unit2)
    col = pl.BlockSpec((tokens, tile), lambda j, s, m: (0, j))
    half1 = pl.BlockSpec((runs1, 2, 2 * unit1, tile // 2), lambda j, s, m: (0, 0, 0, j))
    half2 = pl.BlockSpec((1, runs2, 2, unit2, width), lambda j, s, m: (j, 0, 0, 0, 0))
    return pl.pallas_call(
        mlp_back_kernel,
        grid_spec=pltpu.PrefetchScalarGridSpec(
            num_scalar_prefetch=2,
            grid=(steps,),
            in_specs=[
                full((images, half, width)), full((images, half, width)), full((tokens, width)), col, col,
                pl.BlockSpec((width, tile), lambda j, s, m: (0, j)), pl.BlockSpec((tile, width), lambda j, s, m: (j, 0)),
            ],
            out_specs=[
                full((tokens, width)), half2, half2, half1, half1,
                full((1, width)), pl.BlockSpec((1, tile), lambda j, s, m: (0, j)),
            ],
            scratch_shapes=[
                pltpu.VMEM((tokens, width), BF16), pltpu.VMEM((width, width), F32), pltpu.VMEM((tokens, width), F32),
            ],
        ),
        out_shape=[
            jax.ShapeDtypeStruct((tokens, width), F32),
            jax.ShapeDtypeStruct((steps, runs2, 2, unit2, width), BF16),
            jax.ShapeDtypeStruct((steps, runs2, 2, unit2, width), BF16),
            jax.ShapeDtypeStruct((runs1, 2, 2 * unit1, hidden_width // 2), BF16),
            jax.ShapeDtypeStruct((runs1, 2, 2 * unit1, hidden_width // 2), BF16),
            jax.ShapeDtypeStruct((1, width), F32),
            jax.ShapeDtypeStruct((1, hidden_width), F32),
        ],
        compiler_params=pltpu.CompilerParams(vmem_limit_bytes=58 * MIB),
        cost_estimate=pl.CostEstimate(flops=8 * tokens * width * hidden_width, transcendentals=0, bytes_accessed=35_000_000),
        name="mlp_back",
    )(scal, mine, own, oth, n2, hidden, slope, w["fc1_weight"], w["fc2_weight"])


def attend_back_kernel(
    scal_ref, own_ref, oth_ref, dn2_ref, mid_ref, qkv_ref, probs_ref, wp_ref, g2_ref,
    dmid_ref, dbr_ref, djoin_ref, g2g_ref, g2b_ref, pbg_ref, qbg_ref, vbg_ref, datt_ref,
):
    image = pl.program_id(0)
    half, width = own_ref.shape[1], own_ref.shape[2]
    rows = 2 * half
    live = row_valid(scal_ref, image, rows, half, 0)
    d_final = jnp.where(live, jnp.concatenate([own_ref[0].astype(F32), oth_ref[0].astype(F32)], axis=0), 0.0)
    unit, rstd = norm_parts(mid_ref[0])
    dn2 = dn2_ref[0]
    gain_part = jnp.sum(dn2 * unit, axis=0, keepdims=True)
    bias_part = jnp.sum(dn2, axis=0, keepdims=True)
    d_middle = d_final + norm_back(dn2, g2_ref[...], unit, rstd)
    dmid_ref[0] = d_middle
    keep = scal_ref[image, 4].astype(F32) * KEEP_SCALE
    d_branch = (d_middle * keep).astype(BF16)
    dbr_ref[0] = d_branch
    proj_part = jnp.sum(d_branch.astype(F32), axis=0, keepdims=True)
    datt_ref[...] = dot_nt(d_branch, wp_ref[...]).astype(BF16)
    low_lane = lax.broadcasted_iota(jnp.int32, (rows, 128), 1) < HEAD_DIM
    for pair in range(width // 128):
        cut = slice(128 * pair, 128 * pair + 128)
        q2 = qkv_ref[0, :, cut]
        k2 = qkv_ref[0, :, width + 128 * pair : width + 128 * pair + 128]
        v2 = qkv_ref[0, :, 2 * width + 128 * pair : 2 * width + 128 * pair + 128]
        a2 = datt_ref[:, cut]
        dq = dk = dv = None
        for side in range(2):
            mine = low_lane if side == 0 else jnp.logical_not(low_lane)
            probs_low = probs_ref[0, 2 * pair + side]
            probs = probs_low.astype(F32)
            a_side = jnp.where(mine, a2, 0)
            d_probs = dot_nt(v2, a_side)
            inner = jnp.sum(probs * d_probs, axis=0, keepdims=True)
            d_scores = (probs * (d_probs - inner)).astype(BF16)
            dq_part = dot_tn(d_scores, jnp.where(mine, k2, 0))
            dk_part = dot_nn(d_scores, jnp.where(mine, q2, 0))
            dv_part = dot_nn(probs_low, a_side)
            dq = dq_part if dq is None else dq + dq_part
            dk = dk_part if dk is None else dk + dk_part
            dv = dv_part if dv is None else dv + dv_part
        djoin_ref[0, :, cut] = (dq * HEAD_DIM**-0.5).astype(BF16)
        djoin_ref[0, :, width + 128 * pair : width + 128 * pair + 128] = dk.astype(BF16)
        djoin_ref[0, :, 2 * width + 128 * pair : 2 * width + 128 * pair + 128] = dv.astype(BF16)
    q_part = jnp.sum(djoin_ref[0, :, :width].astype(F32), axis=0, keepdims=True)
    v_part = jnp.sum(djoin_ref[0, :, 2 * width :].astype(F32), axis=0, keepdims=True)
    sums = ((g2g_ref, gain_part), (g2b_ref, bias_part), (pbg_ref, proj_part), (qbg_ref, q_part), (vbg_ref, v_part))

    @pl.when(image == 0)
    def _():
        for ref, part in sums:
            ref[...] = part

    @pl.when(image > 0)
    def _():
        for ref, part in sums:
            ref[...] += part


def attend_back(scal, own, oth, dn2, middle, qkv, probs, w):
    images, half, width = own.shape
    rows = 2 * half
    heads = width // HEAD_DIM
    per = lambda *tail: pl.BlockSpec((1,) + tail, lambda i, s: (i,) + (0,) * len(tail))
    vec = jax.ShapeDtypeStruct((1, width), F32)
    return pl.pallas_call(
        attend_back_kernel,
        grid_spec=pltpu.PrefetchScalarGridSpec(
            num_scalar_prefetch=1,
            grid=(images,),
            in_specs=[
                per(half, width), per(half, width), per(rows, width), per(rows, width), per(rows, 3 * width),
                per(heads, rows, rows), full((width, width)), full((1, width)),
            ],
            out_specs=[per(rows, width), per(rows, width), per(rows, 3 * width)] + [full((1, width))] * 5,
            scratch_shapes=[pltpu.VMEM((rows, width), BF16)],
        ),
        out_shape=[
            jax.ShapeDtypeStruct((images, rows, width), F32),
            jax.ShapeDtypeStruct((images, rows, width), BF16),
            jax.ShapeDtypeStruct((images, rows, 3 * width), BF16),
            vec, vec, vec, vec, vec,
        ],
        compiler_params=pltpu.CompilerParams(vmem_limit_bytes=56 * MIB),
        cost_estimate=pl.CostEstimate(flops=2 * images * rows * width * (width + 8 * rows), transcendentals=0, bytes_accessed=35_000_000),
        name="attend_back",
    )(scal, own, oth, dn2, middle, qkv, probs, w["proj_weight"], w["ln2_gain"])


def tail_kernel(
    mine_ref, n1_ref, djoin_ref, att_ref, dbr_ref, wqkv_ref, xo_ref, xt_ref, dmid_ref, g1_ref,
    send_ref, keep_ref, go_ref, gt_ref, g1g_ref, g1b_ref, grad_ref, acc_ref,
):
    step = pl.program_id(0)
    last = pl.num_programs(0) - 1
    images, half, width = xo_ref.shape
    rows = 2 * half
    mine = mine_ref[0]

    @pl.when(step < last)
    def _():
        put_folded(grad_ref, dot_tn(n1_ref[...], djoin_ref[...]), send_ref, keep_ref, mine)
        part = dot_nt(djoin_ref[...], wqkv_ref[...])

        @pl.when(step == 0)
        def _():
            acc_ref[...] = part

        @pl.when(step > 0)
        def _():
            acc_ref[...] += part

    @pl.when(step == last)
    def _():
        put_folded(grad_ref, dot_tn(att_ref[...], dbr_ref[...]), send_ref, keep_ref, mine)
        gain_sum = jnp.zeros((1, width), F32)
        bias_sum = jnp.zeros((1, width), F32)
        for image in range(images):
            x = jnp.concatenate([xo_ref[image].astype(F32), xt_ref[image].astype(F32)], axis=0)
            unit, rstd = norm_parts(x)
            dn1 = acc_ref[rows * image : rows * image + rows, :]
            gain_sum += jnp.sum(dn1 * unit, axis=0, keepdims=True)
            bias_sum += jnp.sum(dn1, axis=0, keepdims=True)
            out = dmid_ref[rows * image : rows * image + rows, :] + norm_back(dn1, g1_ref[...], unit, rstd)
            go_ref[image] = out[:half]
            gt_ref[image] = out[half:].astype(BF16)
        g1g_ref[...] = gain_sum
        g1b_ref[...] = bias_sum


def tail(mine, n1, d_join, attended, d_branch, own, oth, d_middle, w, unit):
    tokens, width = n1.shape
    images, half, _ = own.shape
    runs = width // (4 * unit)
    halves = pl.BlockSpec((runs, 2, 2 * unit, width // 2), lambda j, m: (0, 0, 0, j))
    clip = lambda j: jnp.minimum(j, 2)
    return pl.pallas_call(
        tail_kernel,
        grid_spec=pltpu.PrefetchScalarGridSpec(
            num_scalar_prefetch=1,
            grid=(4,),
            in_specs=[
                full((tokens, width)), pl.BlockSpec((tokens, width), lambda j, m: (0, clip(j))), full((tokens, width)),
                full((tokens, width)), pl.BlockSpec((width, width), lambda j, m: (0, clip(j))),
                full((images, half, width)), full((images, half, width)), full((tokens, width)), full((1, width)),
            ],
            out_specs=[
                halves, halves, full((images, half, width)), full((images, half, width)),
                full((1, width)), full((1, width)),
            ],
            scratch_shapes=[pltpu.VMEM((width, width), F32), pltpu.VMEM((tokens, width), F32)],
        ),
        out_shape=[
            jax.ShapeDtypeStruct((runs, 2, 2 * unit, 2 * width), BF16),
            jax.ShapeDtypeStruct((runs, 2, 2 * unit, 2 * width), BF16),
            jax.ShapeDtypeStruct((images, half, width), F32),
            jax.ShapeDtypeStruct((images, half, width), BF16),
            jax.ShapeDtypeStruct((1, width), F32),
            jax.ShapeDtypeStruct((1, width), F32),
        ],
        compiler_params=pltpu.CompilerParams(vmem_limit_bytes=56 * MIB),
        cost_estimate=pl.CostEstimate(flops=14 * tokens * width * width, transcendentals=0, bytes_accessed=35_000_000),
        name="tail",
    )(mine, n1, d_join, attended, d_branch, w["qkv_weight"], own, oth, d_middle, w["ln1_gain"])


def emit_kernel(
    fc2_ref, fc1_ref, u_ref, proj_ref, sums_ref, gain_ref, bias_ref, w_ref, own_ref, back_ref, lo_ref,
    out_ref, grad_ref, l1g, l1b, qkvg, qvb, projg, pjb, l2g, l2b, fc1g, f1b, fc2g, f2b, buf, own_buf, back_buf, lo_buf, sems,
):
    side = lax.axis_index("seq")
    owner = 2 * lax.axis_index("img") + side
    images, half, width = own_ref.shape
    unit = u_ref.shape[0]
    arrivals = [
        pltpu.make_async_copy(back_ref, back_buf, sems.at[0]), pltpu.make_async_copy(own_ref, own_buf, sems.at[1]),
        pltpu.make_async_copy(lo_ref, lo_buf, sems.at[2]),
    ]
    for copy in arrivals:
        copy.start()
    arrivals[0].wait()
    buf[...] = back_buf[...].astype(F32)
    other = pltpu.make_async_copy(buf, grad_ref.at[pl.ds((1 - side) * images, images)], sems.at[0])
    other.start()
    arrivals[1].wait()
    mine = pltpu.make_async_copy(own_buf, grad_ref.at[pl.ds(side * images, images)], sems.at[1])
    mine.start()
    arrivals[2].wait()
    keep = pltpu.make_async_copy(lo_buf, out_ref, sems.at[2])
    keep.start()
    fc2g[...] = fc2_ref[...]
    fc1g[...] = fc1_ref[...]
    projg[...] = proj_ref[...]
    lane = lax.broadcasted_iota(jnp.int32, (unit, width), 1)
    slot = lax.broadcasted_iota(jnp.int32, (unit, width), 0)
    here = lane == owner * unit + slot
    column = lambda ref: jnp.sum(jnp.where(here, ref[...].reshape(1, width), 0.0), axis=1, keepdims=True)
    gain, bias = column(gain_ref), column(bias_ref)
    gain_sum = bias_sum = 0.0
    for k, at in enumerate((2, 0, 3)):
        cut = slice(k * width, k * width + width)
        total, weight, sums = u_ref[:, cut], w_ref[:, cut].astype(F32), sums_ref[at : at + 1, :]
        qkvg[:, cut] = gain * total + bias * sums
        gain_sum += jnp.sum(weight * total, axis=1, keepdims=True)
        bias_sum += jnp.sum(weight * sums, axis=1, keepdims=True)
    diag = lax.broadcasted_iota(jnp.int32, (unit, 128), 1) == lax.broadcasted_iota(jnp.int32, (unit, 128), 0)
    for ref, value in ((l1g, gain_sum), (l1b, bias_sum)):
        ref[...] = jnp.sum(jnp.where(diag, value, 0.0), axis=0, keepdims=True)[0, :unit]
    for ref, at, count in ((pjb, 4, 1), (l2g, 5, 1), (l2b, 6, 1), (f2b, 11, 1), (f1b, 7, 4), (qvb, 2, 2)):
        size = unit * count
        place = owner * size
        which, start = place // width, place % width
        row = sums_ref[at : at + 1, :]
        for k in range(1, count):
            row = jnp.where(which == k, sums_ref[at + k : at + k + 1, :], row)
        sel = lax.broadcasted_iota(jnp.int32, (size, width), 1) == start + lax.broadcasted_iota(jnp.int32, (size, width), 0)
        tall = jnp.sum(jnp.where(sel, row, 0.0), axis=1, keepdims=True)
        eye = lax.broadcasted_iota(jnp.int32, (size, 128), 1) == lax.broadcasted_iota(jnp.int32, (size, 128), 0)
        ref[...] = jnp.sum(jnp.where(eye, tall, 0.0), axis=0, keepdims=True)[0, :size]
    keep.wait()
    mine.wait()
    other.wait()


def emit(fc2, fc1, u, proj, sums, gain, bias, qkv_weight, own, back, layer_out):
    images, half, width = own.shape
    unit = u.shape[0]
    hbm = pl.BlockSpec(memory_space=pl.ANY)
    whole = lambda v: pl.BlockSpec(v.shape, lambda i: (0,) * len(v.shape))
    shape = lambda *dims: jax.ShapeDtypeStruct(dims, F32)
    outs = [
        shape(unit), shape(unit), shape(unit, 3 * width), shape(2 * unit), shape(unit, width), shape(unit), shape(unit),
        shape(unit), shape(*fc1.shape), shape(fc1.shape[1] // GROUP), shape(*fc2.shape), shape(unit),
    ]
    return pl.pallas_call(
        emit_kernel,
        grid=(1,),
        in_specs=[whole(v) for v in (fc2, fc1, u, proj, sums, gain, bias)]
        + [pl.BlockSpec((unit, 3 * width), lambda i: (2 * lax.axis_index("img") + lax.axis_index("seq"), 0)), hbm, hbm, hbm],
        out_specs=[hbm, hbm] + [whole(v) for v in outs],
        scratch_shapes=[
            pltpu.VMEM(own.shape, F32), pltpu.VMEM(own.shape, F32), pltpu.VMEM(back.shape, BF16),
            pltpu.VMEM(layer_out.shape, BF16), pltpu.SemaphoreType.DMA((3,)),
        ],
        out_shape=[jax.ShapeDtypeStruct(layer_out.shape, BF16), shape(2 * images, half, width)] + outs,
        compiler_params=pltpu.CompilerParams(vmem_limit_bytes=63 * MIB),
        name="emit",
    )(fc2, fc1, u, proj, sums, gain, bias, qkv_weight, own, back, layer_out)


MESH = pl.DeviceIdType.MESH
PARTS = 7
SLOTS = 3
GROUP = 32


class Far:
    def __init__(self, ends, send_sem, recv_sem, peer):
        self.parts = (ends, send_sem, recv_sem, peer)
        self.build().start()

    def build(self):
        ends, send_sem, recv_sem, peer = self.parts
        src, dst = ends()
        return pltpu.make_async_remote_copy(
            src_ref=src, dst_ref=dst, send_sem=send_sem(), recv_sem=recv_sem(), device_id=peer, device_id_type=MESH
        )

    def wait(self):
        self.build().wait()


class Parcel:
    def __init__(self, keep, send, landing, levels, sems, order, place, names="wvyx"):
        self.keep, self.send, self.landing, self.levels, self.sems = keep, send, landing, levels, sems
        self.order, self.place, self.names = order, place, names

    def copy(self, src, dst, slot, peer):
        send_sem, recv_sem = self.sems
        return pltpu.make_async_remote_copy(
            src_ref=src, dst_ref=dst, send_sem=send_sem(slot), recv_sem=recv_sem(slot), device_id=peer, device_id_type=MESH
        )

    def bring(self, step):
        if step == 0:
            return self.copy(self.send(), self.landing(), 0, self.place["core"][1])
        name, used = self.order[step - 1], self.order[:step]
        spot = tuple(
            self.place[n][2] if n == name else self.place[n][0] if n in used else slice(None) for n in self.names
        )
        return self.copy(self.keep().at[spot], self.levels(step - 1), step, self.place[name][1])

    def start(self):
        self.bring(0).start()

    def gather(self, step):
        self.bring(step).wait()
        return self.add(step)

    def add(self, step):
        used = self.order[:step]
        left = [n for n in self.names if n not in used]
        arrived = self.levels(step - 1) if step else self.landing()

        def one(i):
            at = {}
            for n in reversed(left):
                at[n] = i % 2
                i = i // 2
            inner = tuple(at[n] for n in left)
            spot = tuple(at[n] if n in at else self.place[n][0] for n in self.names)
            if step == len(self.order):
                return self.keep()[spot].astype(F32) + arrived[inner].astype(F32)
            self.keep()[spot] = self.keep()[spot] + arrived[inner]

        if not left:
            return one(0)
        pl.loop(0, 2 ** len(left))(lambda i: one(i) and None)

    def launch(self, step):
        self.bring(step + 1).start()

    def move(self, step):
        self.gather(step)
        self.launch(step)


class HalfParcel(Parcel):
    def launch(self, step):
        if step < 3:
            return super().launch(step)

        @pl.when(self.goes)
        def _():
            self.bring(4).start()

    def finish(self, write):
        @pl.when(self.goes)
        def _():
            self.bring(4).wait_send()

        @pl.when(self.mine)
        def _():
            self.bring(4).wait_recv()
            write(self.add(4))


def level_shapes(names, order, rows, cols):
    return [
        (2,) * len([n for n in names if n not in order[: step + 1]]) + (rows, cols) for step in range(len(order))
    ]


ORDERS = ("yvxw", "yvxw", "wxvy", "xwvy", "yvwx", "yvwx", "vyxw")
FC2_A, FC2_B, FC1_A, FC1_B, VAL_PROJ, QUERY, KEY = range(7)
PLAN = {
    "b02": ((FC2_B, 0),),
    "b24": ((FC1_B, 0),),
    "c01": ((FC2_A, 1),),
    "c04": ((VAL_PROJ, 0),),
    "c12": ((FC2_B, 1),),
    "c15": ((FC2_A, 2),),
    "c20": ((FC1_A, 1),),
    "c22": ((FC1_B, 1),),
    "c25": ((FC2_A, 3), (FC2_B, 2), (VAL_PROJ, 1)),
    "key": ((QUERY, 0),),
    "input0": ((KEY, 0), (FC2_B, 3)),
    "input1": ((VAL_PROJ, 2), (QUERY, 1)),
    "input2": ((FC1_A, 2), (FC2_A, 4), (KEY, 1)),
    "end0": ((FC2_B, 4), (FC1_B, 2), (QUERY, 2), (KEY, 2)),
    "end1": (
        (FC1_A, 3), (VAL_PROJ, 3), (FC1_B, 3), (KEY, 3), (QUERY, 3), (FC1_A, 4), (VAL_PROJ, 4), (FC1_B, 4), (QUERY, 4),
        (KEY, 4),
    ),
}


def rest_kernel(
    grid_ref, split_ref, owner_ref, drop_ref, patches_hbm, cot_hbm, w1_hbm, w2_hbm, wp_hbm, wqkv_hbm,
    g1_ref, b1_ref, qv_ref, pb_ref, g2_ref, b2_ref, c1_ref, c2_ref,
    fc2_ref, fc1_ref, qkvg_ref, projg_ref, vec_ref, out_ref, grad_ref, back_ref, unit_hbm, qkv_hbm, probs_hbm, att_hbm,
    cot, rstd_one, rows_ref, dn2, mid, acc, left, right, wbuf, qkv, probs, djoin, datt, tile, ost, gsend, grecv, vec, vget,
    keep_a, send_a, land_a, keep_b, send_b, land_b, keep_c, send_c, land_c, *others,
):
    levels = [others[4 * k : 4 * k + 4] for k in range(PARTS)]
    (load_sem, probs_sem, qkv_sem, w_sem, open_sem, open_send, open_recv, send_sem, recv_sem, side_send, side_recv, vec_send, vec_recv, out_sem,
     free_sem) = others[4 * PARTS :]
    images, rows, width = dn2.shape
    half = rows // 2
    pairs = width // 128
    steps = w1_hbm.shape[1] // width
    line = lax.axis_index("img")
    x = lax.axis_index("seq")
    core = line % 2
    y = (line // 2) % 2
    z = line // 4
    sibling = (line + 1 - 2 * core, x)
    level = (line + 2 - 4 * y, x)
    across = (line, 1 - x)
    scal_ref = Facts((grid_ref, split_ref, owner_ref, drop_ref), images, x)
    zv, zw = z % 2, z // 2
    near_z = (line + 4 - 8 * zv, x)
    far_z = (line + 8 - 16 * zw, x)
    peers = [sibling, level, across, near_z, far_z]
    barrier = pltpu.get_barrier_semaphore()
    for peer in peers:
        pl.semaphore_signal(barrier, inc=1, device_id=peer, device_id_type=MESH)

    loads = []

    def fetch(src, dst):
        copy = pltpu.make_async_copy(src, dst, load_sem.at[len(loads)])
        copy.start()
        loads.append(copy)
        return copy

    def probs_copy(index, slot):
        return pltpu.make_async_copy(
            probs_hbm.at[index // pairs, pl.ds(2 * (index % pairs), 2)], probs.at[slot], probs_sem.at[slot]
        )

    def qkv_copy(i, slot):
        return pltpu.make_async_copy(qkv_hbm.at[i], qkv.at[slot], qkv_sem.at[slot])

    def w1_copy(t, slot):
        at = pl.multiple_of(t * width, 128)
        return pltpu.make_async_copy(w1_hbm.at[:, pl.ds(at, width)], wbuf.at[slot], w_sem.at[slot])

    def w2_copy(t, slot):
        at = pl.multiple_of(t * width, 128)
        return pltpu.make_async_copy(w2_hbm.at[pl.ds(at, width), :], wbuf.at[2 + slot], w_sem.at[2 + slot])

    def x_copy(i):
        return pltpu.make_async_copy(patches_hbm.at[x * images + i], right.at[i, pl.ds(0, half)], open_sem.at[i])

    def x_far(i):
        return pltpu.make_async_remote_copy(
            src_ref=patches_hbm.at[(1 - x) * images + i], dst_ref=right.at[i, pl.ds(half, half)],
            send_sem=open_send.at[i], recv_sem=open_recv.at[i], device_id=across, device_id_type=MESH,
        )

    def cot_far(i):
        return pltpu.make_async_remote_copy(
            src_ref=cot_hbm.at[(1 - x) * images + i], dst_ref=cot.at[i, pl.ds(half, half)],
            send_sem=open_send.at[images + i], recv_sem=open_recv.at[images + i], device_id=across, device_id_type=MESH,
        )

    def probs_out(index, slot):
        return pltpu.make_async_copy(
            probs.at[slot], probs_hbm.at[index // pairs, pl.ds(2 * (index % pairs), 2)], probs_sem.at[slot]
        )

    def saves(i):
        return [
            pltpu.make_async_copy(datt.at[i], unit_hbm.at[i], open_sem.at[images + 4 * i]),
            pltpu.make_async_copy(djoin.at[i], qkv_hbm.at[i], open_sem.at[images + 4 * i + 1]),
            pltpu.make_async_copy(ost.at[i], att_hbm.at[i, pl.ds(0, half)], open_sem.at[images + 4 * i + 2]),
            pltpu.make_async_copy(gsend.at[i], att_hbm.at[i, pl.ds(half, half)], open_sem.at[images + 4 * i + 3]),
        ]

    def wqkv_copy(k, slot):
        return pltpu.make_async_copy(wqkv_hbm.at[:, pl.ds(k * width, width)], wbuf.at[slot], w_sem.at[slot])

    def wp_copy(slot):
        return pltpu.make_async_copy(wp_hbm, wbuf.at[slot], w_sem.at[slot])

    def write_folds(total, ref, tile_at):
        for t in range(total.shape[1] // side_cols):
            for h in range(2):
                at = (tile_at + t) * width + h * side_cols
                ref[:, at : at + side_cols] = total[h * unit : h * unit + unit, t * side_cols : t * side_cols + side_cols]

    def write_fc2(total):
        fc2_ref[...] = total

    def write_out(k):
        if k in (FC2_A, FC2_B):
            return parcels[k].finish(write_fc2)
        total = parcels[k].gather(4)
        if k == VAL_PROJ:
            write_folds(total[:, :side_cols], qkvg_ref, 2)
            write_folds(total[:, side_cols:], projg_ref, 0)
        else:
            ref, tile_at = {FC1_A: (fc1_ref, 0), FC1_B: (fc1_ref, 2), QUERY: (qkvg_ref, 0), KEY: (qkvg_ref, 1)}[k]
            write_folds(total, ref, tile_at)

    def at_point(name):
        for k, step in PLAN.get(name, ()):
            if step == 0:
                step_one(k)
            elif step < 4:
                parcels[k].move(step)
            else:
                write_out(k)

    def plan_of(tag):
        return {
            (int(name[1]), int(name[2])): (lambda name=name: at_point(name))
            for name in PLAN if len(name) == 3 and name[0] == tag and name[1:].isdigit()
        }

    def pump(plan, i, pair):
        for (image, at), job in plan.items():
            if at == pair:

                @pl.when(i == image)
                def _():
                    job()

    first_plan = {
        (0, 3): lambda: x_far(2).start(),
        (1, 1): lambda: cot_far(0).start(),
        (2, 3): lambda: cot_far(2).start(),
    }
    weights_in = [wqkv_copy(0, 0), wqkv_copy(1, 2), wqkv_copy(2, 3), wp_copy(1)]
    x_copy(0).start()
    pl.semaphore_wait(barrier, len(peers))
    x_far(0).start()
    for copy in weights_in:
        copy.start()
    for i in range(1, images):
        x_copy(i).start()
    cot_in = fetch(cot_hbm.at[pl.ds(x * images, images)], cot.at[:, pl.ds(0, half)])
    line_of = lambda ref: ref[...].reshape(1, -1)
    for k in range(steps):
        rows_ref[k : k + 1, :] = line_of(c1_ref)[:, k * width : k * width + width]
    for k, ref in enumerate((c2_ref, g1_ref, b1_ref, g2_ref, b2_ref, pb_ref)):
        rows_ref[4 + k : 5 + k, :] = line_of(ref)
    rows_ref[10:11, :] = line_of(qv_ref)[:, :width]
    rows_ref[11:12, :] = line_of(qv_ref)[:, width:]
    vector = lambda k: rows_ref[k : k + 1, :]
    low_lane = lax.broadcasted_iota(jnp.int32, (rows, 128), 1) < HEAD_DIM
    sides = (low_lane, jnp.logical_not(low_lane))
    cuts = lambda pair: [slice(k * width + 128 * pair, k * width + 128 * pair + 128) for k in range(3)]
    vec[...] = jnp.zeros_like(vec)
    acc[...] = jnp.zeros_like(acc)
    dn2[...] = jnp.zeros_like(dn2)
    for copy in weights_in:
        copy.wait()

    @pl.loop(0, images)
    def _(i):
        x_copy(i).wait()
        x_far(i).wait()

        @pl.when(i == 0)
        def _():
            x_far(1).start()

        @pl.when(i == images - 1)
        def _():
            cot_far(1).start()

        unit_one, rstd = norm_parts(right[i].astype(F32))
        datt[i] = unit_one.astype(BF16)
        rstd_one[i] = rstd
        n1 = (unit_one * vector(5) + vector(6)).astype(BF16)
        djoin[i, :, :width] = (dot_nn(n1, wbuf[0]) + vector(10)).astype(BF16) * BF16(HEAD_DIM**-0.5)
        djoin[i, :, width : 2 * width] = dot_nn(n1, wbuf[2]).astype(BF16)
        djoin[i, :, 2 * width :] = (dot_nn(n1, wbuf[3]) + vector(11)).astype(BF16)

        @pl.when(i == images - 1)
        def _():
            w1_copy(0, 0).start()
            w2_copy(0, 0).start()

        fill = jnp.where(row_valid(scal_ref, i, rows, half, 0), 0.0, MASK_FILL)
        for pair in range(pairs):
            index = i * pairs + pair
            slot = index % SLOTS

            @pl.when(index >= SLOTS)
            def _():
                probs_out(index - SLOTS, slot).wait()

            q_cut, k_cut, v_cut = cuts(pair)
            q2, k2, v2 = djoin[i, :, q_cut], djoin[i, :, k_cut], djoin[i, :, v_cut]
            total = None
            for side in range(2):
                scores = dot_nt(k2, jnp.where(sides[side], q2, 0)) + fill
                top = jnp.max(scores, axis=0, keepdims=True)
                weight = jnp.exp(scores - top)
                low = (weight * (1.0 / jnp.sum(weight, axis=0, keepdims=True))).astype(BF16)
                probs[slot, side] = low
                part = dot_tn(low, jnp.where(sides[side], v2, 0))
                total = part if total is None else total + part
            attended = total.astype(BF16)
            ost[i, :, q_cut] = attended[:half]
            gsend[i, :, q_cut] = attended[half:]
            probs_out(index, slot).start()
            pump(first_plan, i, pair)
        gate = scal_ref[i, 4].astype(F32) * KEEP_SCALE
        attended = jnp.concatenate([ost[i], gsend[i]], axis=0)
        middle = right[i].astype(F32) + gate * (dot_nn(attended, wbuf[1]) + vector(9))
        mid[i] = middle
        unit_two, _ = norm_parts(middle)
        left[i] = (unit_two * vector(7) + vector(8)).astype(BF16)
        for copy in saves(i):
            copy.start()

    for slot in range(SLOTS):
        probs_out(images * pairs - SLOTS + slot, slot).wait()
    for i in range(images):
        for copy in saves(i):
            copy.wait()
    for slot in range(SLOTS):
        probs_copy(slot, slot).start()
    for slot in range(2):
        qkv_copy(slot, slot).start()
    cot_in.wait()

    place = {
        "core": (core, sibling), "y": (y, level, 1 - y), "x": (x, across, 1 - x),
        "v": (zv, near_z, 1 - zv), "w": (zw, far_z, 1 - zw),
    }
    homes = [
        (keep_a.at[0], send_a, land_a), (keep_a.at[1], send_a, land_a),
        (keep_b.at[0], send_b.at[0], land_b.at[0]), (keep_b.at[1], send_b.at[1], land_b.at[1]),
        (keep_b.at[2], send_b.at[0], land_b.at[0]),
        (keep_c.at[0], send_c.at[0], land_c.at[0]), (keep_c.at[1], send_c.at[1], land_c.at[1]),
    ]
    parcels = []
    for k in range(PARTS):
        keep, send, land = (lambda k=k, n=n: homes[k][n] for n in range(3))
        sems = (lambda slot, k=k: send_sem.at[k, slot]), (lambda slot, k=k: recv_sem.at[k, slot])
        build = HalfParcel if k < 2 else Parcel
        parcels.append(
            build(keep, send, land, lambda step, k=k: levels[k][step], sems, ORDERS[k], place, "vyx" if k < 2 else "wvyx")
        )
    for k in range(2):
        parcels[k].goes, parcels[k].mine = zw != k, zw == k
    free_slot = {FC2_A: 0, FC1_A: 1}
    needs = {FC2_B: 0, VAL_PROJ: 1}

    def release(k):
        pl.semaphore_signal(free_sem.at[free_slot[k]], inc=1, device_id=sibling, device_id_type=MESH)

    def start(k):
        if k in needs:
            pl.semaphore_wait(free_sem.at[needs[k]], 1)
        parcels[k].start()

    r, c = keep_b.shape[-2], keep_b.shape[-1]
    unit, side_cols = r // 2, c // 2

    def put_block_rows(k, zz):
        for ref, who in ((send_a, 1 - core), (keep_a.at[k], core)):
            for b in range(2):
                for e in range(2):
                    at = pl.multiple_of((2 * b + who) * 4 * r + e * 2 * r, 8)
                    ref[zz, b, e] = tile[pl.ds(at, 2 * r), :].astype(BF16)

    def put_folds(send, kept, t):
        spot = pl.ds(pl.multiple_of(t * side_cols, 128), side_cols)

        @pl.loop(0, 8)
        def _(k):
            for ref, who in ((send, 1 - core), (kept, core)):
                for e in range(2):
                    at = pl.multiple_of((4 * k + 2 * who + e) * unit, 8)
                    piece = tile[pl.ds(at, unit), :]
                    ref[k // 4, (k // 2) % 2, k % 2, e, :, spot] = jnp.concatenate(
                        [piece[:, :side_cols], piece[:, side_cols:]], axis=0
                    ).astype(BF16)

    def step_one(k):
        parcels[k].gather(0)
        if k in free_slot:
            release(k)
        parcels[k].launch(0)

    flat = lambda ref: ref[...].reshape(images * rows, ref.shape[-1])
    column = lambda k: djoin[:, :, k * width : k * width + width].reshape(images * rows, width)

    @pl.loop(0, steps)
    def _(t):
        slot = t % 2
        w1_copy(t, slot).wait()
        w2_copy(t, slot).wait()

        @pl.when(t + 1 < steps)
        def _():
            w1_copy(t + 1, 1 - slot).start()
            w2_copy(t + 1, 1 - slot).start()

        @pl.when(t + 1 == steps)
        def _():
            wqkv_copy(0, 0).start()
            wp_copy(2).start()

        @pl.when(t == 2)
        def _():
            start(FC2_A)
            start(FC1_A)

        for i in range(images):
            hidden, slope = gelu_both(dot_nn(left[i], wbuf[slot]) + rows_ref[pl.ds(t, 1), :])
            hidden = hidden.astype(BF16)
            djoin[i, :, :width] = hidden
            djoin[i, :, 2 * width :] = slope.astype(BF16)
            acc[i] += dot_nn(hidden, wbuf[2 + slot])

        @pl.when(t == 0)
        def _():
            for i in range(images):
                cot_far(i).wait()
                gate = scal_ref[i, 5].astype(F32) * KEEP_SCALE
                live = row_valid(scal_ref, i, rows, half, 0)
                d_mlp = (jnp.where(live, cot[i].astype(F32), 0.0) * gate).astype(BF16)
                right[i] = d_mlp
                vec[11:12, :] += jnp.sum(d_mlp.astype(F32), axis=0, keepdims=True)

        for i in range(images):
            d_pre = (djoin[i, :, 2 * width :].astype(F32) * dot_nt(right[i], wbuf[2 + slot])).astype(BF16)
            djoin[i, :, width : 2 * width] = d_pre
            vec[pl.ds(7 + t, 1), :] += jnp.sum(d_pre.astype(F32), axis=0, keepdims=True)
            dn2[i] += dot_nt(d_pre, wbuf[slot])

        tile[...] = dot_tn(column(0), flat(right))

        @pl.when(t == 2)
        def _():
            for k in (FC2_A, FC1_A):
                step_one(k)

        for k in range(2):

            @pl.when(t // 2 == k)
            def _():
                put_block_rows(k, t % 2)

        tile[...] = dot_tn(flat(left), column(1))
        for k in range(2):

            @pl.when(t // 2 == k)
            def _():
                put_folds(send_b.at[k], keep_b.at[k], t % 2)

    wqkv_copy(1, 1).start()
    wqkv_copy(2, 3).start()
    unit_in, att_in = fetch(unit_hbm, left), fetch(att_hbm, right)
    start(FC2_B)
    start(FC1_B)
    for i in range(images):
        gate = scal_ref[i, 5].astype(F32) * KEEP_SCALE
        final = mid[i] + gate * (acc[i] + rows_ref[4:5, :])
        out = jnp.where(row_valid(scal_ref, i, rows, half, 0), final, 0.0).astype(BF16)
        ost[i] = out[:half]
        gsend[i] = out[half:]
    out_own = pltpu.make_async_copy(ost, out_ref.at[pl.ds(x * images, images)], out_sem.at[0])
    out_own.start()
    out_far = Far(
        lambda: (gsend, out_ref.at[pl.ds(x * images, images)]), lambda: side_send.at[images], lambda: side_recv.at[images], across
    )

    wp_copy(2).wait()
    for i in range(images):
        live = row_valid(scal_ref, i, rows, half, 0)
        d_final = jnp.where(live, cot[i].astype(F32), 0.0)
        unit_two, rstd = norm_parts(mid[i])
        d_normed = dn2[i]
        vec[5:6, :] += jnp.sum(d_normed * unit_two, axis=0, keepdims=True)
        vec[6:7, :] += jnp.sum(d_normed, axis=0, keepdims=True)
        d_middle = d_final + norm_back(d_normed, rows_ref[7:8, :], unit_two, rstd)
        dn2[i] = d_middle
        gate = scal_ref[i, 4].astype(F32) * KEEP_SCALE
        d_branch = (d_middle * gate).astype(BF16)
        datt[i] = d_branch
        vec[4:5, :] += jnp.sum(d_branch.astype(F32), axis=0, keepdims=True)
    at_point("norm")
    unit_in.wait()
    att_in.wait()
    tile[...] = dot_tn(flat(right), flat(datt))
    put_folds(send_b.at[0], keep_b.at[2], 1)
    at_point("proj")
    for i in range(images):
        datt[i] = dot_nt(datt[i], wbuf[2]).astype(BF16)
    at_point("back")

    total_pairs = images * pairs

    def next_probs(index, slot):
        @pl.when(index + SLOTS < 2 * total_pairs)
        def _():
            probs_copy((index + SLOTS) % total_pairs, slot).start()

    @pl.loop(0, images)
    def _(i):
        for pair in range(pairs):
            index = i * pairs + pair
            slot = index % SLOTS
            probs_copy(index, slot).wait()
            q_cut, _, v_cut = cuts(pair)
            a2 = datt[i, :, q_cut]
            dv = dot_nn(probs[slot, 0], jnp.where(sides[0], a2, 0)) + dot_nn(probs[slot, 1], jnp.where(sides[1], a2, 0))
            djoin[i, :, v_cut] = dv.astype(BF16)
            next_probs(index, slot)
            pump(plan_of("b"), i, pair)
        vec[3:4, :] += jnp.sum(djoin[i, :, 2 * width :].astype(F32), axis=0, keepdims=True)

    tile[...] = dot_tn(flat(left), column(2))
    put_folds(send_b.at[0], keep_b.at[2], 0)
    start(VAL_PROJ)

    @pl.loop(0, images)
    def _(i):
        q_slot = i % 2
        qkv_copy(i, q_slot).wait()
        for pair in range(pairs):
            index = total_pairs + i * pairs + pair
            slot = index % SLOTS
            probs_copy(index - total_pairs, slot).wait()
            q_cut, k_cut, v_cut = cuts(pair)
            q2, k2, v2, a2 = qkv[q_slot, :, q_cut], qkv[q_slot, :, k_cut], qkv[q_slot, :, v_cut], datt[i, :, q_cut]
            dq = dk = None
            for side in range(2):
                high = probs[slot, side].astype(F32)
                d_probs = dot_nt(v2, jnp.where(sides[side], a2, 0))
                inner = jnp.sum(high * d_probs, axis=0, keepdims=True)
                d_scores = (high * (d_probs - inner)).astype(BF16)
                parts = dot_tn(d_scores, jnp.where(sides[side], k2, 0)), dot_nn(d_scores, jnp.where(sides[side], q2, 0))
                dq, dk = parts if dq is None else (dq + parts[0], dk + parts[1])
            djoin[i, :, q_cut] = (dq * HEAD_DIM**-0.5).astype(BF16)
            djoin[i, :, k_cut] = dk.astype(BF16)
            next_probs(index, slot)
            pump(plan_of("c"), i, pair)

        @pl.when(i + 2 < images)
        def _():
            qkv_copy(i + 2, q_slot).start()

        vec[2:3, :] += jnp.sum(djoin[i, :, :width].astype(F32), axis=0, keepdims=True)
        vec[0:1, :] += jnp.sum(djoin[i, :, width : 2 * width].astype(F32), axis=0, keepdims=True)

    for t, k in ((0, QUERY), (1, KEY)):
        tile[...] = dot_tn(flat(left), column(t))
        put_folds(send_c.at[t], keep_c.at[t], 0)
        start(k)
    at_point("key")
    wqkv_copy(0, 0).wait()
    wqkv_copy(1, 1).wait()
    wqkv_copy(2, 3).wait()
    out_far.wait()

    def input_grad(i):
        d_normed = dot_nt(djoin[i, :, :width], wbuf[0])
        d_normed += dot_nt(djoin[i, :, width : 2 * width], wbuf[1])
        d_normed += dot_nt(djoin[i, :, 2 * width :], wbuf[3])
        out = dn2[i] + norm_back(d_normed, rows_ref[5:6, :], left[i].astype(F32), rstd_one[i])
        acc[i, :half] = out[:half]
        gsend[i] = out[half:].astype(BF16)

    def exchange(k):
        return Far(lambda: (vec, vget.at[k]), lambda: vec_send.at[k], lambda: vec_recv.at[k], peers[k])

    def settle(k, trade):
        trade.wait()
        vec[...] += vget[k]

    swaps = []

    def swap_out(i):
        swaps.append(
            Far(lambda: (gsend.at[i], grecv.at[i]), lambda: side_send.at[i], lambda: side_recv.at[i], across)
        )

    for i in range(images):
        trade = exchange(i)
        input_grad(i)
        swap_out(i)
        settle(i, trade)
        if i + 1 < images:
            at_point("input%d" % i)
    grad_own = pltpu.make_async_copy(acc.at[:, pl.ds(0, half)], grad_ref, out_sem.at[1])
    grad_own.start()
    trade = exchange(3)
    at_point("input2")
    settle(3, trade)
    trade = exchange(4)
    at_point("end0")
    settle(4, trade)
    vec_ref[...] = vec[...]
    at_point("end1")
    for copy in swaps:
        copy.wait()
    grad_oth = pltpu.make_async_copy(grecv, back_ref, out_sem.at[2])
    grad_oth.start()
    out_own.wait()
    grad_own.wait()
    grad_oth.wait()


def rest(facts, patches, cotangent, vectors, w):
    all_images, half, width = patches.shape
    images = all_images // 2
    rows = 2 * half
    heads = width // HEAD_DIM
    hidden_width = w["fc1_weight"].shape[1]
    r, c = 2 * (width // GROUP), width
    fc2_rows = hidden_width // GROUP
    hbm = pl.BlockSpec(memory_space=pl.ANY)
    vmem = pl.BlockSpec(memory_space=pltpu.VMEM)
    smem = pl.BlockSpec(memory_space=pltpu.SMEM)
    dma = pltpu.SemaphoreType.DMA
    whole = lambda dtype: pltpu.VMEM((images, rows, width), dtype)
    half_block = lambda dtype: pltpu.VMEM((images, half, width), dtype)
    level_bufs = []
    for k, order in enumerate(ORDERS):
        names = "vyx" if k < 2 else "wvyx"
        block = (fc2_rows, width) if k < 2 else (r, c) if k < 5 else (r, c // 2)
        level_bufs += [pltpu.VMEM(shape, BF16) for shape in level_shapes(names, order, *block)]
    rows_of = lambda *lead: pltpu.VMEM(lead + (2, 2, 2, fc2_rows, width), BF16)
    folds_of = lambda count, cols: pltpu.VMEM((count, 2, 2, 2, 2, r, cols), BF16)
    return pl.pallas_call(
        rest_kernel,
        in_specs=[smem] * 4 + [hbm] * 6 + [vmem] * 8,
        out_specs=[vmem] * 5 + [hbm] * 7,
        out_shape=[
            jax.ShapeDtypeStruct((fc2_rows, width), F32),
            jax.ShapeDtypeStruct((r // 2, hidden_width), F32),
            jax.ShapeDtypeStruct((r // 2, 3 * width), F32),
            jax.ShapeDtypeStruct((r // 2, width), F32),
            jax.ShapeDtypeStruct((16, width), F32),
            jax.ShapeDtypeStruct((2 * images, half, width), BF16),
            jax.ShapeDtypeStruct((images, half, width), F32),
            jax.ShapeDtypeStruct((images, half, width), BF16),
            jax.ShapeDtypeStruct((images, rows, width), BF16),
            jax.ShapeDtypeStruct((images, rows, 3 * width), BF16),
            jax.ShapeDtypeStruct((images, heads, rows, rows), BF16),
            jax.ShapeDtypeStruct((images, rows, width), BF16),
        ],
        scratch_shapes=[
            whole(BF16), pltpu.VMEM((images, rows, 1), F32), pltpu.VMEM((16, width), F32), whole(F32), whole(F32), whole(F32), whole(BF16), whole(BF16),
            pltpu.VMEM((4, width, width), BF16),
            pltpu.VMEM((2, rows, 3 * width), BF16),
            pltpu.VMEM((SLOTS, 2, rows, rows), BF16),
            pltpu.VMEM((images, rows, 3 * width), BF16),
            whole(BF16),
            pltpu.VMEM((width, width), F32),
            half_block(BF16), half_block(BF16), half_block(BF16),
            pltpu.VMEM((16, width), F32),
            pltpu.VMEM((5, 16, width), F32),
            rows_of(2), rows_of(), rows_of(),
            folds_of(3, c), folds_of(2, c), folds_of(2, c),
            folds_of(2, c // 2), folds_of(2, c // 2), folds_of(2, c // 2),
            *level_bufs,
            dma((4,)), dma((SLOTS,)), dma((2,)), dma((4,)), dma((5 * images,)), dma((2 * images,)), dma((2 * images,)),
            dma((PARTS, 5)), dma((PARTS, 5)), dma((images + 1,)),
            dma((images + 1,)), dma((5,)), dma((5,)), dma((3,)), pltpu.SemaphoreType.REGULAR((2,)),
        ],
        compiler_params=pltpu.CompilerParams(collective_id=0, has_side_effects=True, vmem_limit_bytes=64 * MIB),
        name="rest",
    )(*facts, patches, cotangent, w["fc1_weight"], w["fc2_weight"], w["proj_weight"], w["qkv_weight"], *vectors)


def spread(value):
    return lax.psum_scatter(value, ("img", "seq"), scatter_dimension=0, tiled=True)


def unfold(send, keep, core, folds):
    rows, cols = send.shape[-2], send.shape[-1]
    send, keep = (v.reshape(GROUP // 4, 2, rows, cols) for v in (send, keep))
    both = jnp.stack([jnp.where(core == 0, keep, send), jnp.where(core == 0, send, keep)], axis=1).astype(F32)
    if folds == 1:
        return both.reshape(GROUP * rows, cols)
    tiles = 4
    both = both.reshape(GROUP, 2, rows // 2, tiles, cols // tiles)
    return both.transpose(0, 2, 3, 1, 4).reshape(GROUP * rows // 2, 2 * cols)


def swap(value, axis, bit, size):
    return lax.ppermute(value, axis, [(i, i ^ bit) for i in range(size)])


def shards(img_size, args):
    (patches, grid_shape, split_rows, owner_shard, drop_masks, ln1_gain, ln1_bias, qkv_weight, qv_bias, proj_weight,
     proj_bias, ln2_gain, ln2_bias, fc1_weight, fc1_bias, fc2_weight, fc2_bias, cotangent) = args
    all_images, _, half, width = patches.shape
    images = all_images // 2
    rows = 2 * half
    tokens = images * rows
    side = lax.axis_index("seq")
    line = lax.axis_index("img")
    owners = 2 * img_size
    row = lambda v: v.reshape(1, -1)
    w = dict(
        ln1_gain=row(ln1_gain), ln1_bias=row(ln1_bias), qkv_weight=qkv_weight, q_bias=row(qv_bias[:width]),
        v_bias=row(qv_bias[width:]), proj_weight=proj_weight, proj_bias=row(proj_bias), ln2_gain=row(ln2_gain),
        ln2_bias=row(ln2_bias), fc1_weight=fc1_weight, fc1_bias=row(fc1_bias), fc2_weight=fc2_weight, fc2_bias=row(fc2_bias),
    )

    def exchange(value):
        value = value.reshape(all_images, half, width)
        own = lax.dynamic_slice_in_dim(value, side * images, images, axis=0)
        away = lax.dynamic_slice_in_dim(value, (1 - side) * images, images, axis=0)
        return own, swap(away, "seq", 1, 2)

    def place(own, back):
        back = back.astype(own.dtype)
        first = jnp.where(side == 0, own, back)
        second = jnp.where(side == 0, back, own)
        return jnp.concatenate([first, second], axis=0).reshape(all_images, 1, half, width)

    def restore(own, oth):
        return place(own, swap(oth, "seq", 1, 2))

    across = grid_shape[:, 1]
    counts = jnp.stack([split_rows * across, (grid_shape[:, 0] - split_rows) * across], axis=0)
    count_own = jnp.where(side == 0, counts[0], counts[1])
    count_oth = jnp.where(side == 0, counts[1], counts[0])
    special = (owner_shard == side).astype(jnp.int32)
    table = jnp.stack([count_own, special, count_oth, 1 - special, drop_masks[:, 0], drop_masks[:, 1]], axis=1)
    scal = lax.dynamic_slice_in_dim(table, side * images, images, axis=0)

    flat = lambda v: v.reshape(tokens, v.shape[-1])
    unit1 = width // GROUP
    unit2 = fc2_weight.shape[0] // GROUP
    if owners == GROUP:
        merge = lambda v: v.reshape(all_images, half, width)
        facts = (grid_shape.T, split_rows, owner_shard, drop_masks.T)
        fc2_part, fc1_part, u_part, proj_part, sums, out_part, grad_own, grad_back, *_ = rest(
            facts, merge(patches), merge(cotangent),
            (ln1_gain, ln1_bias, qv_bias, proj_bias, ln2_gain, ln2_bias, fc1_bias, fc2_bias), w,
        )
        outs = emit(
            fc2_part, fc1_part, u_part, proj_part, sums, ln1_gain, ln1_bias, qkv_weight, grad_own, grad_back, out_part
        )
        layer_out, patches_grad = (v.reshape(all_images, 1, half, width) for v in outs[:2])
        return (layer_out, patches_grad, *outs[2:])
    else:
        x_own, x_oth = exchange(patches)
        c_own, c_oth = exchange(cotangent)
        n1, qkv, probs, attended, middle, n2 = front(scal, x_own, x_oth, w)
        mine = lax.rem(line, 2).reshape(1)
        hidden, slope, out_own, out_oth = mlp(scal, flat(n2), flat(middle), w, images, 512)
        layer_out = restore(out_own, out_oth)
        dn2, s2, k2, s1, k1, fc2_bias_grad, fc1_bias_grad = mlp_back(
            scal, mine, c_own, c_oth, flat(n2), hidden, slope, w, unit1, unit2
        )
        dn2 = dn2.reshape(images, rows, width)
        d_middle, d_branch, d_join, ln2_gain_grad, ln2_bias_grad, proj_bias_grad, q_grad, v_grad = attend_back(
            scal, c_own, c_oth, dn2, middle, qkv, probs, w
        )
        st, kt, grad_own, grad_oth, ln1_gain_grad, ln1_bias_grad = tail(
            mine, flat(n1), flat(d_join), flat(attended), flat(d_branch), x_own, x_oth, flat(d_middle), w, unit1
        )
        patches_grad = restore(grad_own, grad_oth)
        vectors = (
            ln1_gain_grad, ln1_bias_grad, jnp.concatenate([q_grad, v_grad], axis=1), proj_bias_grad, ln2_gain_grad,
            ln2_bias_grad, fc1_bias_grad, fc2_bias_grad,
        )
        fc2_grad = spread(unfold(s2, k2, line % 2, 1))
        fc1_grad = spread(unfold(s1, k1, line % 2, 2))
        tail_grad = spread(unfold(st, kt, line % 2, 2))
        qkv_grad, proj_grad = tail_grad[:, : 3 * width], tail_grad[:, 3 * width :]
        pieces = [spread(v.reshape(-1)) for v in vectors]
    l1g, l1b, qvb, pjb, l2g, l2b, f1b, f2b = pieces
    return (
        layer_out, patches_grad, l1g, l1b, qkv_grad, qvb, proj_grad, pjb, l2g, l2b, fc1_grad, f1b, fc2_grad, f2b,
    )


def solution(mesh):
    rep = [P()] * 12
    vec = P(("img", "seq"))
    mat = P(("img", "seq"), None)
    rows = P("img", "seq", None, None)

    def run(*args):
        return shards(mesh.shape["img"], args)

    return jax.shard_map(
        run,
        mesh=mesh,
        in_specs=(rows, P("img", None), P("img"), P("img"), P("img", None), *rep, rows),
        out_specs=(rows, rows, vec, vec, mat, vec, mat, vec, vec, vec, mat, vec, mat, vec),
        check_vma=False,
    )
```
